32 devices in a mesh: dp: 8 (over z, y), tp: 4 (over x, core).
Axes of the slice: x: 2, y: 2, z: 4, core: 2. Of those that a mesh axis runs over, the one named last changes fastest.
Arguments:
- tokens: bfloat16 [4096, 1024], P(('dp', 'tp')), may hold values from -6 to 6
- cotangent: bfloat16 [4096, 1024], P(('dp', 'tp')), may hold values from -6 to 6
- lengths: int32 [8], P('dp'), may hold values from 20 to 512, as said below
- qkv_weight: bfloat16 [2, 1024, 3, 1024], P(None, None, None, 'tp'), may hold values from -0.1875 to 0.1875
- qv_bias: bfloat16 [2, 2, 1024], P(None, None, 'tp'), may hold values from -1 to 1
- out_weight: bfloat16 [2, 1024, 1024], P(None, 'tp'), may hold values from -1.5 to 1.5
- out_bias: bfloat16 [2, 1024], replicated, may hold values from -1 to 1
- up_weight: bfloat16 [2, 1024, 4096], P(None, None, 'tp'), may hold values from -0.1875 to 0.1875
- up_bias: bfloat16 [2, 4096], P(None, 'tp'), may hold values from -1 to 1
- down_weight: bfloat16 [2, 4096, 1024], P(None, 'tp'), may hold values from -0.09375 to 0.09375
- down_bias: bfloat16 [2, 1024], replicated, may hold values from -1 to 1
- norm_params: float32 [2, 4, 1024], replicated, may hold values from -1 to 1.3, as said below
- act_ranges: float32 [2, 4], replicated, may hold values from 0.45 to 5, as said below
Outputs:
- output: bfloat16 [4096, 1024], P(('dp', 'tp'))
- input_grad: float32 [4096, 1024], P(('dp', 'tp'))
- qkv_weight_grad: float32 [2, 1024, 3, 1024], P(None, None, None, 'tp')
- qv_bias_grad: float32 [2, 2, 1024], P(None, None, 'tp')
- out_weight_grad: float32 [2, 1024, 1024], P(None, 'tp')
- out_bias_grad: float32 [2, 1024], replicated
- up_weight_grad: float32 [2, 1024, 4096], P(None, None, 'tp')
- up_bias_grad: float32 [2, 4096], P(None, 'tp')
- down_weight_grad: float32 [2, 4096, 1024], P(None, 'tp')
- down_bias_grad: float32 [2, 1024], replicated
- norm_grad: float32 [2, 4, 1024], replicated
- act_peaks: float32 [2, 4], replicated
The draws below stay inside these ranges and needn't reach their ends.
Inputs may be any that keep to these rules, and one draw needn't show every extreme that they name: `lengths`: every sequence has at least 20 tokens; the first slot holds a full sequence of 512. `norm_params`: gains lie between 0.7 and 1.3, shifts of order 0.2. `act_ranges`: positive ranges.
All inputs are finite; a program needn't handle non-finite values.
Results may differ from the reference program's by a relative error of at most 0.02.
Values may be sent and summed in bfloat16 or wider, within the bound.
No kernel may reach another device: no remote copies, remote signals or barrier semaphores. Data moves between devices by JAX's collectives and lax.ppermute only.
A program may use at most 192 MiB of HBM per device.

```python
import math
import jax
import jax.numpy as jnp
from jax import lax

D = 1024
HEADS = 16
HD = 64
FF = 4096
LAYERS = 2
SEQ_LEN = 512
SEQS = 8
TOKENS = 4096


def draw_lengths(key, part):
    least = max(2, SEQ_LEN // 25)
    drawn = jax.random.randint(key, (SEQS,), least, SEQ_LEN + 1)
    return jnp.where(jnp.arange(SEQS) == 0, SEQ_LEN, drawn).astype(jnp.int32)


def draw_norm_params(key, part):
    spread = jax.random.uniform(jax.random.fold_in(key, 1), (LAYERS, 4, D), minval=-1.0, maxval=1.0)
    normal = jax.random.normal(jax.random.fold_in(key, 2), (LAYERS, 4, D))
    is_gain = (jnp.arange(4) % 2 == 0)[None, :, None]
    return jnp.where(is_gain, 1.0 + 0.3 * spread, 0.2 * jnp.clip(normal, -5.0, 5.0)).astype(jnp.float32)


def draw_act_ranges(key, part):
    base = jnp.array([4.0, 0.6, 4.0, 3.0], jnp.float32)
    factor = jax.random.uniform(key, (LAYERS, 4), minval=0.75, maxval=1.25)
    return (base[None, :] * factor).astype(jnp.float32)


def levels(rng, extent, cuts, smallest, top_value):
    def one(dim, shards_of):
        draws = jax.random.uniform(jax.random.fold_in(jax.random.fold_in(rng, 6), dim), (shards_of,), jnp.float32, smallest / len(cuts), top_value / len(cuts))
        return jnp.repeat(jnp.exp(draws), extent[dim] // shards_of).reshape((-1,) + (1,) * (len(extent) - dim - 1))

    factor_of = one(*cuts[0])
    for cut in cuts[1:]:
        factor_of = factor_of * one(*cut)
    return factor_of


def scatter_about(key, dims, scale, most, pieces=(), kind=jnp.bfloat16):
    level = levels(key, dims, pieces, -0.22, 0.18) if pieces else 1.0
    values = jax.random.normal(key, dims, jnp.float32) * scale * level
    return jnp.minimum(jnp.maximum(values, -most), most).astype(kind)


def setup_inputs(seed: int = 0) -> dict:
    streams_of = jax.random.split(jax.random.key(seed), 14)
    return {
        "tokens": scatter_about(streams_of[0], (TOKENS, D), 1.0, 6.0, ((0, 32),)),
        "cotangent": scatter_about(streams_of[1], (TOKENS, D), 1.0, 6.0, ((0, 32),)),
        "lengths": draw_lengths(jax.random.fold_in(streams_of[13], 71), 0),
        "qkv_weight": scatter_about(streams_of[3], (LAYERS, D, 3, D), D ** -0.5, 0.1875, ((3, 4),)),
        "qv_bias": scatter_about(streams_of[4], (LAYERS, 2, D), 0.2, 1.0, ((2, 4),)),
        "out_weight": scatter_about(streams_of[5], (LAYERS, D, D), (max(D // 64, 4)) ** -0.5, 1.5, ((1, 4),)),
        "out_bias": scatter_about(streams_of[6], (LAYERS, D), 0.2, 1.0),
        "up_weight": scatter_about(streams_of[7], (LAYERS, D, FF), D ** -0.5, 0.1875, ((2, 4),)),
        "up_bias": scatter_about(streams_of[8], (LAYERS, FF), 0.2, 1.0, ((1, 4),)),
        "down_weight": scatter_about(streams_of[9], (LAYERS, FF, D), FF ** -0.5, 0.09375, ((1, 4),)),
        "down_bias": scatter_about(streams_of[10], (LAYERS, D), 0.2, 1.0),
        "norm_params": draw_norm_params(jax.random.fold_in(streams_of[13], 71), 0),
        "act_ranges": draw_act_ranges(jax.random.fold_in(streams_of[13], 71), 0),
    }


PRECISE = lax.Precision.HIGHEST
NORM_EPSILON = 1e-06

@jax.custom_vjp
def low(v):
    return lax.optimization_barrier(v.astype(jnp.bfloat16)).astype(jnp.float32)

@jax.custom_vjp
def low_back(v):
    return v

def low_keep(v):
    return (low(v), None)

def low_pass(kept, grad):
    return (grad,)

def back_keep(v):
    return (v, None)

def back_low(kept, grad):
    return (low(grad),)
low.defvjp(low_keep, low_pass)
low_back.defvjp(back_keep, back_low)

def squash(value, limit):
    return limit * jnp.tanh(value / limit)

def layer_norm(values, gain, shift):
    centre = lax.optimization_barrier(jnp.mean(values, axis=-1, keepdims=True))
    centred = values - centre
    spread = lax.optimization_barrier(jnp.mean(centred * centred, axis=-1, keepdims=True))
    return centred * lax.rsqrt(spread + NORM_EPSILON) * gain + shift

def attend(queries, key_rows, value_rows, key_bias):
    scores = jnp.einsum('sqhd,skhd->shqk', queries, key_rows, precision=PRECISE) * HD ** (-0.5) + key_bias[:, None, None, :]
    scores = low_back(scores)
    weights = low(jax.nn.softmax(scores, axis=-1))
    return jnp.einsum('shqk,skhd->sqhd', weights, value_rows, precision=PRECISE)

def encoder(params, weight_tops, act_ranges, hidden_rows, key_bias, valid):
    qkv_weight, qv_bias, out_weight, out_bias, up_weight, up_bias, down_weight, down_bias, norm_params = params
    row_count = hidden_rows.shape[0]
    slot_count = row_count // SEQ_LEN
    mask = valid[:, None]
    peak_list = []
    for level in range(LAYERS):
        limits = act_ranges[level]
        tops = weight_tops[level]
        inputs = hidden_rows
        x_low = low(squash(inputs, limits[0]))
        w_qkv = low(squash(qkv_weight[level], tops[0])).reshape(D, 3 * D)
        zero_bias = jnp.zeros((D,), jnp.float32)
        bias_all = jnp.stack([qv_bias[level, 0], zero_bias, qv_bias[level, 1]]).reshape(3 * D)
        projected = low(low_back(jnp.dot(x_low, w_qkv, precision=PRECISE) + bias_all))
        shaped = projected.reshape(slot_count, SEQ_LEN, 3, HEADS, HD)
        context = jax.checkpoint(attend)(shaped[:, :, 0], shaped[:, :, 1], shaped[:, :, 2], key_bias)
        context = low_back(context.reshape(row_count, D))
        ctx_low = low(squash(context, limits[1]))
        w_out = low(squash(out_weight[level], tops[1]))
        attn_out = low_back(jnp.dot(ctx_low, w_out, precision=PRECISE) + out_bias[level])
        mid_sum = inputs + attn_out
        hidden = layer_norm(mid_sum, norm_params[level, 0], norm_params[level, 1])
        hid_low = low(squash(hidden, limits[2]))
        w_up = low(squash(up_weight[level], tops[2]))
        up_value = low_back(jnp.dot(hid_low, w_up, precision=PRECISE) + up_bias[level])
        active = jax.nn.gelu(up_value, approximate=False)
        act_low = low(squash(active, limits[3]))
        w_down = low(squash(down_weight[level], tops[3]))
        down_value = low_back(jnp.dot(act_low, w_down, precision=PRECISE) + down_bias[level])
        peak_list.append(jnp.stack([jnp.max(jnp.abs(inputs) * mask), jnp.max(jnp.abs(context) * mask), jnp.max(jnp.abs(hidden) * mask), jnp.max(jnp.abs(active) * mask)]))
        hidden_rows = layer_norm(hidden + down_value, norm_params[level, 2], norm_params[level, 3])
    return (hidden_rows, jnp.stack(peak_list))

def reference(tokens, cotangent, lengths, qkv_weight, qv_bias, out_weight, out_bias, up_weight, up_bias, down_weight, down_bias, norm_params, act_ranges):
    params = tuple((item.astype(jnp.float32) for item in (qkv_weight, qv_bias, out_weight, out_bias, up_weight, up_bias, down_weight, down_bias, norm_params)))
    ranges_f = act_ranges.astype(jnp.float32)
    weight_tops = jnp.stack([jnp.stack([jnp.max(jnp.abs(params[0][level])), jnp.max(jnp.abs(params[2][level])), jnp.max(jnp.abs(params[4][level])), jnp.max(jnp.abs(params[6][level]))]) for level in range(LAYERS)])
    group = math.gcd(SEQS, max(1, 4096 // SEQ_LEN))
    blocks = SEQS // group
    rows_in = tokens.astype(jnp.float32).reshape(blocks, group * SEQ_LEN, D)
    cot_in = cotangent.astype(jnp.float32).reshape(blocks, group * SEQ_LEN, D)
    lens_in = lengths.reshape(blocks, group)

    def per_block(carry, item):
        totals, peak_now = carry
        block_rows, block_cot, block_lens = item
        inside = jnp.arange(SEQ_LEN, dtype=jnp.int32)[None, :] < block_lens[:, None]
        valid = inside.reshape(-1).astype(jnp.float32)
        key_bias = jnp.where(inside, jnp.float32(0.0), jnp.float32(-1000000000.0)).astype(jnp.float32)

        def forward(param_set, rows_now):
            return encoder(param_set, weight_tops, ranges_f, rows_now, key_bias, valid)
        result, pull, peaks = jax.vjp(forward, params, block_rows, has_aux=True)
        grads, grad_rows = pull(block_cot * valid[:, None])
        totals = jax.tree.map(jnp.add, totals, grads)
        return ((totals, jnp.maximum(peak_now, peaks)), (result, grad_rows))
    init = (jax.tree.map(jnp.zeros_like, params), jnp.zeros((LAYERS, 4), jnp.float32))
    (totals, peak_all), (results, grads_rows) = lax.scan(per_block, init, (rows_in, cot_in, lens_in))
    return (results.reshape(TOKENS, D).astype(jnp.bfloat16), grads_rows.reshape(TOKENS, D), totals[0], totals[1], totals[2], totals[3], totals[4], totals[5], totals[6], totals[7], totals[8], peak_all)
```

```python
import jax
import jax.numpy as jnp
from jax import lax
from jax.sharding import PartitionSpec as P

HD = 64
SEQ_LEN = 512
NORM_EPSILON = 1e-06
F32 = jnp.float32
BF16 = jnp.bfloat16


def bits_of(count):
    return [1 << place for place in range(count.bit_length() - 1)]


def swap(value, axis, bit):
    count = lax.axis_size(axis)
    return lax.ppermute(value, axis, [(item, item ^ bit) for item in range(count)])


def block_order(count):
    order = [0]
    for bit in reversed(bits_of(count)):
        order = order + [item ^ bit for item in order]
    return order


def gather_rows(rows):
    block = rows
    for bit in reversed(bits_of(lax.axis_size("tp"))):
        block = jnp.concatenate([block, swap(block, "tp", bit)], axis=0)
    return block


def scatter_rows(partial):
    for bit in bits_of(lax.axis_size("tp")):
        half = partial.shape[0] // 2
        arrived = swap(partial[half:].astype(BF16), "tp", bit)
        partial = partial[:half] + arrived.astype(F32)
    return partial


def squash(value, limit):
    return limit * jnp.tanh(value / limit)


def squash_slope(value, limit):
    level_value = jnp.tanh(value / limit)
    return 1.0 - level_value * level_value


def norm_parts(values):
    centre = jnp.mean(values, axis=-1, keepdims=True)
    centred = values - centre
    spread = jnp.mean(centred * centred, axis=-1, keepdims=True)
    scale = lax.rsqrt(spread + NORM_EPSILON)
    return centred * scale, scale


def norm_back(gradient, unit, scale, gain):
    scaled = gradient * gain
    first = jnp.mean(scaled, axis=-1, keepdims=True)
    second = jnp.mean(scaled * unit, axis=-1, keepdims=True)
    d_values = scale * (scaled - first - unit * second)
    return d_values, jnp.sum(gradient * unit, axis=0), jnp.sum(gradient, axis=0)


def mm(first, second):
    return jnp.dot(first, second, preferred_element_type=F32)


def mm_t(first, second):
    return lax.dot_general(first, second, (((1,), (1,)), ((), ())), preferred_element_type=F32)


def t_mm(first, second):
    return lax.dot_general(first, second, (((0,), (0,)), ((), ())), preferred_element_type=F32)


def reduce_weight(left, right, raw, top, order):
    place = lax.axis_index("dp")
    rows = left.shape[1]
    start = 0
    bit = order[0]
    mine = (place // bit) % 2
    half = rows // 2
    send = t_mm(lax.dynamic_slice_in_dim(left, (1 - mine) * half, half, 1), right).astype(BF16)
    arrived = swap(send, "dp", bit)
    total = t_mm(lax.dynamic_slice_in_dim(left, mine * half, half, 1), right)
    total = total + arrived.astype(F32)
    start = mine * half
    for bit in order[1:]:
        mine = (place // bit) % 2
        half = half // 2
        send = lax.dynamic_slice_in_dim(total, (1 - mine) * half, half, 0).astype(BF16)
        arrived = swap(send, "dp", bit)
        total = lax.dynamic_slice_in_dim(total, mine * half, half, 0) + arrived.astype(F32)
        start = start + mine * half
    raw_piece = lax.dynamic_slice_in_dim(raw, start, half, 0).astype(F32)
    piece = (total * squash_slope(raw_piece, top)).astype(BF16)
    for bit in reversed(order):
        mine = (place // bit) % 2
        arrived = swap(piece, "dp", bit)
        low_half = jnp.where(mine == 0, piece, arrived)
        high_half = jnp.where(mine == 0, arrived, piece)
        piece = jnp.concatenate([low_half, high_half], axis=0)
    return piece.astype(F32)


def on_device(
    tokens,
    cotangent,
    lengths,
    qkv_weight,
    qv_bias,
    out_weight,
    out_bias,
    up_weight,
    up_bias,
    down_weight,
    down_bias,
    norm_params,
    act_ranges,
):
    row_count, width = tokens.shape
    tp_count = lax.axis_size("tp")
    dp_count = lax.axis_size("dp")
    rank = lax.axis_index("tp")
    all_rows = row_count * tp_count
    assert lengths.shape[0] == 1 and all_rows == SEQ_LEN
    layer_count = qkv_weight.shape[0]
    local_width = qkv_weight.shape[3]
    local_units = up_weight.shape[2]
    heads_here = local_width // HD
    score_scale = HD ** (-0.5)
    order = jnp.array(block_order(tp_count), jnp.int32)
    places = ((rank ^ order)[:, None] * row_count + jnp.arange(row_count)[None, :]).reshape(all_rows)
    inside = places < lengths[0]
    valid_all = inside.astype(F32)[:, None]
    valid_rows = valid_all[:row_count]
    key_bias = jnp.where(inside, 0.0, -1000000000.0).astype(F32)
    qkv_blocks = jnp.transpose(qkv_weight, (0, 2, 1, 3))
    local_tops = jnp.stack(
        [
            jnp.stack(
                [
                    jnp.max(jnp.abs(qkv_blocks[level])),
                    jnp.max(jnp.abs(out_weight[level])),
                    jnp.max(jnp.abs(up_weight[level])),
                    jnp.max(jnp.abs(down_weight[level])),
                ]
            )
            for level in range(layer_count)
        ]
    ).astype(F32)
    weight_tops = local_tops
    for bit in bits_of(tp_count):
        weight_tops = jnp.maximum(weight_tops, swap(weight_tops, "tp", bit))

    def scores_of(queries, key_rows):
        raw = jnp.einsum("qhd,khd->hqk", queries, key_rows, preferred_element_type=F32)
        return raw * score_scale + key_bias[None, None, :]

    stored = []
    peak_list = []
    current = tokens.astype(F32)
    for level in range(layer_count):
        limits = act_ranges[level]
        tops = weight_tops[level]
        w_qkv = squash(qkv_blocks[level].astype(F32), tops[0]).astype(BF16)
        w_out = squash(out_weight[level].astype(F32), tops[1]).astype(BF16)
        w_up = squash(up_weight[level].astype(F32), tops[2]).astype(BF16)
        w_down = squash(down_weight[level].astype(F32), tops[3]).astype(BF16)
        x_low_all = gather_rows(squash(current, limits[0]).astype(BF16))
        heads = (all_rows, heads_here, HD)
        queries = (mm(x_low_all, w_qkv[0]) + qv_bias[level, 0].astype(F32)).astype(BF16).reshape(heads)
        key_rows = mm(x_low_all, w_qkv[1]).astype(BF16).reshape(heads)
        value_rows = (mm(x_low_all, w_qkv[2]) + qv_bias[level, 1].astype(F32)).astype(BF16).reshape(heads)
        scores = scores_of(queries, key_rows)
        peak_score = jnp.max(scores, axis=-1, keepdims=True)
        log_total = peak_score + jnp.log(jnp.sum(jnp.exp(scores - peak_score), axis=-1, keepdims=True))
        attn_probs = jnp.exp(scores - log_total).astype(BF16)
        context = jnp.einsum("hqk,khd->qhd", attn_probs, value_rows, preferred_element_type=F32)
        context = context.reshape(all_rows, local_width)
        ctx_low = squash(context, limits[1]).astype(BF16)
        attn_rows = scatter_rows(mm(ctx_low, w_out))
        mid_unit, mid_scale = norm_parts(current + attn_rows + out_bias[level].astype(F32))
        hidden = mid_unit * norm_params[level, 0] + norm_params[level, 1]
        hid_low_all = gather_rows(squash(hidden, limits[2]).astype(BF16))
        up_value = mm(hid_low_all, w_up) + up_bias[level].astype(F32)
        normal_cdf = 0.5 + 0.5 * lax.erf(up_value * (0.5**0.5))
        active = up_value * normal_cdf
        act_level = jnp.tanh(active / limits[3])
        act_low = (limits[3] * act_level).astype(BF16)
        gelu_slope = normal_cdf + up_value * jnp.exp(-0.5 * up_value * up_value) * 0.3989422804014327
        up_slope = (1.0 - act_level * act_level) * gelu_slope
        down_rows = scatter_rows(mm(act_low, w_down))
        out_unit, out_scale = norm_parts(hidden + down_rows + down_bias[level].astype(F32))
        peak_list.append(
            jnp.stack(
                [
                    jnp.max(jnp.abs(current) * valid_rows),
                    jnp.max(jnp.abs(context) * valid_all),
                    jnp.max(jnp.abs(hidden) * valid_rows),
                    jnp.max(jnp.abs(active) * valid_all),
                ]
            )
        )
        stored.append(
            (
                current, mid_unit, mid_scale, hidden, out_unit, out_scale, x_low_all, queries, key_rows, value_rows,
                log_total, context, ctx_low, hid_low_all, up_slope, act_low, w_qkv, w_out, w_up, w_down,
            )
        )
        current = out_unit * norm_params[level, 2] + norm_params[level, 3]
    output = current.astype(BF16)
    gradient = cotangent.astype(F32) * valid_rows

    dp_bits = bits_of(dp_count)
    big_list = [None] * layer_count
    rep_list = [None] * layer_count
    shard_list = [None] * layer_count
    for level in reversed(range(layer_count)):
        (
            inputs, mid_unit, mid_scale, hidden, out_unit, out_scale, x_low_all, queries, key_rows, value_rows,
            log_total, context, ctx_low, hid_low_all, up_slope, act_low, w_qkv, w_out, w_up, w_down,
        ) = stored[level]
        limits = act_ranges[level]
        tops = weight_tops[level]
        d_final, d_gain_out, d_shift_out = norm_back(gradient, out_unit, out_scale, norm_params[level, 2])
        down_grad = d_final.astype(BF16)
        d_down_bias = jnp.sum(down_grad.astype(F32), axis=0)
        down_grad_all = gather_rows(down_grad)
        up_grad = (mm_t(down_grad_all, w_down) * up_slope).astype(BF16)
        g_down = reduce_weight(act_low, down_grad_all, down_weight[level], tops[3], dp_bits)
        d_up_bias = jnp.sum(up_grad.astype(F32), axis=0)
        d_hid_rows = scatter_rows(mm_t(up_grad, w_up))
        g_up = reduce_weight(hid_low_all, up_grad, up_weight[level], tops[2], dp_bits)
        d_hidden = d_final + d_hid_rows * squash_slope(hidden, limits[2])
        d_mid, d_gain_mid, d_shift_mid = norm_back(d_hidden, mid_unit, mid_scale, norm_params[level, 0])
        out_grad = d_mid.astype(BF16)
        d_out_bias = jnp.sum(out_grad.astype(F32), axis=0)
        out_grad_all = gather_rows(out_grad)
        ctx_grad = (mm_t(out_grad_all, w_out) * squash_slope(context, limits[1])).astype(BF16)
        g_out = reduce_weight(ctx_low, out_grad_all, out_weight[level], tops[1], dp_bits)
        ctx_grad = ctx_grad.reshape(heads)
        soft_probs = jnp.exp(scores_of(queries, key_rows) - log_total)
        soft_low = soft_probs.astype(BF16)
        d_values = jnp.einsum("hqk,qhd->khd", soft_low, ctx_grad, preferred_element_type=F32)
        d_probs = jnp.einsum("qhd,khd->hqk", ctx_grad, value_rows, preferred_element_type=F32)
        d_scores = (
            soft_probs * (d_probs - jnp.sum(soft_probs * d_probs, axis=-1, keepdims=True))
        ).astype(BF16)
        d_queries = jnp.einsum("hqk,khd->qhd", d_scores, key_rows, preferred_element_type=F32) * score_scale
        d_keys = jnp.einsum("hqk,qhd->khd", d_scores, queries, preferred_element_type=F32) * score_scale
        parts = [
            item.astype(BF16).reshape(all_rows, local_width) for item in (d_queries, d_keys, d_values)
        ]
        d_x_rows = scatter_rows(
            mm_t(parts[0], w_qkv[0]) + mm_t(parts[1], w_qkv[1]) + mm_t(parts[2], w_qkv[2])
        )
        g_qkv = reduce_weight(
            x_low_all,
            jnp.concatenate(parts, axis=1),
            jnp.transpose(qkv_blocks[level], (1, 0, 2)).reshape(width, 3 * local_width),
            tops[0],
            dp_bits,
        ).reshape(width, 3, local_width)
        d_qv_bias = jnp.stack([jnp.sum(parts[0].astype(F32), axis=0), jnp.sum(parts[2].astype(F32), axis=0)])
        gradient = d_mid + d_x_rows * squash_slope(inputs, limits[0])
        big_list[level] = (g_qkv, g_out, g_up, g_down)
        rep_list[level] = jnp.stack([d_out_bias, d_down_bias, d_gain_mid, d_shift_mid, d_gain_out, d_shift_out])
        shard_list[level] = (d_qv_bias, d_up_bias)

    rep = jnp.stack(rep_list)
    peaks = jnp.stack(peak_list)
    for bit in bits_of(tp_count):
        rep = rep + swap(rep, "tp", bit)
        peaks = jnp.maximum(peaks, swap(peaks, "tp", bit))
    qv_sum = jnp.stack([item[0] for item in shard_list])
    up_sum = jnp.stack([item[1] for item in shard_list])
    sizes = [rep.size, qv_sum.size, up_sum.size]
    pack = jnp.concatenate([rep.reshape(-1), qv_sum.reshape(-1), up_sum.reshape(-1)])
    for bit in dp_bits:
        pack = pack + swap(pack, "dp", bit)
        peaks = jnp.maximum(peaks, swap(peaks, "dp", bit))
    rep = pack[: sizes[0]].reshape(rep.shape)
    qv_sum = pack[sizes[0] : sizes[0] + sizes[1]].reshape(qv_sum.shape)
    up_sum = pack[sizes[0] + sizes[1] :].reshape(up_sum.shape)
    grads = [jnp.stack([entry[item] for entry in big_list]) for item in range(4)]
    return (
        output,
        gradient,
        grads[0],
        qv_sum,
        grads[1],
        rep[:, 0],
        grads[2],
        up_sum,
        grads[3],
        rep[:, 1],
        rep[:, 2:],
        peaks,
    )


def solution(mesh):
    return jax.shard_map(
        on_device,
        mesh=mesh,
        in_specs=(
            P(("dp", "tp"), None),
            P(("dp", "tp"), None),
            P("dp"),
            P(None, None, None, "tp"),
            P(None, None, "tp"),
            P(None, "tp", None),
            P(),
            P(None, None, "tp"),
            P(None, "tp"),
            P(None, "tp", None),
            P(),
            P(),
            P(),
        ),
        out_specs=(
            P(("dp", "tp"), None),
            P(("dp", "tp"), None),
            P(None, None, None, "tp"),
            P(None, None, "tp"),
            P(None, "tp", None),
            P(),
            P(None, None, "tp"),
            P(None, "tp"),
            P(None, "tp", None),
            P(),
            P(),
            P(),
        ),
        check_vma=False,
    )
```

```python
import functools

import jax
import jax.numpy as jnp
from jax import lax
from jax.experimental import pallas as pl
from jax.experimental.pallas import tpu as pltpu
from jax.sharding import PartitionSpec as P

HD = 64
SEQ_LEN = 512
NORM_EPSILON = 1e-06
F32 = jnp.float32
BF16 = jnp.bfloat16


def bits_of(count):
    return [1 << place for place in range(count.bit_length() - 1)]


def swap(value, axis, bit):
    count = lax.axis_size(axis)
    return lax.ppermute(value, axis, [(item, item ^ bit) for item in range(count)])


def block_order(count):
    order = [0]
    for bit in reversed(bits_of(count)):
        order = order + [item ^ bit for item in order]
    return order


def gather_rows(rows):
    block = rows
    for bit in reversed(bits_of(lax.axis_size("tp"))):
        block = jnp.concatenate([block, swap(block, "tp", bit)], axis=0)
    return block


def scatter_rows(partial):
    for bit in bits_of(lax.axis_size("tp")):
        half = partial.shape[0] // 2
        arrived = swap(partial[half:].astype(BF16), "tp", bit)
        partial = partial[:half] + arrived.astype(F32)
    return partial


def squash(value, limit):
    return limit * jnp.tanh(value / limit)


def squash_slope(value, limit):
    level_value = jnp.tanh(value / limit)
    return 1.0 - level_value * level_value


def norm_parts(values):
    centre = jnp.mean(values, axis=-1, keepdims=True)
    centred = values - centre
    spread = jnp.mean(centred * centred, axis=-1, keepdims=True)
    scale = lax.rsqrt(spread + NORM_EPSILON)
    return centred * scale, scale


def norm_back(gradient, unit, scale, gain):
    scaled = gradient * gain
    first = jnp.mean(scaled, axis=-1, keepdims=True)
    second = jnp.mean(scaled * unit, axis=-1, keepdims=True)
    d_values = scale * (scaled - first - unit * second)
    return d_values, jnp.sum(gradient * unit, axis=0), jnp.sum(gradient, axis=0)


def mm(first, second):
    return jnp.dot(first, second, preferred_element_type=F32)


def mm_t(first, second):
    return lax.dot_general(first, second, (((1,), (1,)), ((), ())), preferred_element_type=F32)


def t_mm(first, second):
    return lax.dot_general(first, second, (((0,), (0,)), ((), ())), preferred_element_type=F32)


def reduce_weight(left, right, raw, top, order):
    place = lax.axis_index("dp")
    rows = left.shape[1]
    start = 0
    bit = order[0]
    mine = (place // bit) % 2
    half = rows // 2
    send = t_mm(lax.dynamic_slice_in_dim(left, (1 - mine) * half, half, 1), right).astype(BF16)
    arrived = swap(send, "dp", bit)
    total = t_mm(lax.dynamic_slice_in_dim(left, mine * half, half, 1), right)
    total = total + arrived.astype(F32)
    start = mine * half
    for bit in order[1:]:
        mine = (place // bit) % 2
        half = half // 2
        send = lax.dynamic_slice_in_dim(total, (1 - mine) * half, half, 0).astype(BF16)
        arrived = swap(send, "dp", bit)
        total = lax.dynamic_slice_in_dim(total, mine * half, half, 0) + arrived.astype(F32)
        start = start + mine * half
    raw_piece = lax.dynamic_slice_in_dim(raw, start, half, 0).astype(F32)
    piece = (total * squash_slope(raw_piece, top)).astype(BF16)
    for bit in reversed(order):
        mine = (place // bit) % 2
        arrived = swap(piece, "dp", bit)
        low_half = jnp.where(mine == 0, piece, arrived)
        high_half = jnp.where(mine == 0, arrived, piece)
        piece = jnp.concatenate([low_half, high_half], axis=0)
    return piece.astype(F32)


def on_device(
    tokens,
    cotangent,
    lengths,
    qkv_weight,
    qv_bias,
    out_weight,
    out_bias,
    up_weight,
    up_bias,
    down_weight,
    down_bias,
    norm_params,
    act_ranges,
):
    row_count, width = tokens.shape
    tp_count = lax.axis_size("tp")
    dp_count = lax.axis_size("dp")
    rank = lax.axis_index("tp")
    all_rows = row_count * tp_count
    assert lengths.shape[0] == 1 and all_rows == SEQ_LEN
    layer_count = qkv_weight.shape[0]
    local_width = qkv_weight.shape[3]
    local_units = up_weight.shape[2]
    heads_here = local_width // HD
    score_scale = HD ** (-0.5)
    order = jnp.array(block_order(tp_count), jnp.int32)
    places = ((rank ^ order)[:, None] * row_count + jnp.arange(row_count)[None, :]).reshape(all_rows)
    inside = places < lengths[0]
    valid_all = inside.astype(F32)[:, None]
    valid_rows = valid_all[:row_count]
    key_bias = jnp.where(inside, 0.0, -1000000000.0).astype(F32)
    qkv_blocks = jnp.transpose(qkv_weight, (0, 2, 1, 3))
    local_tops = jnp.stack(
        [
            jnp.stack(
                [
                    jnp.max(jnp.abs(qkv_blocks[level])),
                    jnp.max(jnp.abs(out_weight[level])),
                    jnp.max(jnp.abs(up_weight[level])),
                    jnp.max(jnp.abs(down_weight[level])),
                ]
            )
            for level in range(layer_count)
        ]
    ).astype(F32)
    weight_tops = local_tops
    for bit in bits_of(tp_count):
        weight_tops = jnp.maximum(weight_tops, swap(weight_tops, "tp", bit))

    def scores_of(queries, key_rows):
        raw = jnp.einsum("qhd,khd->hqk", queries, key_rows, preferred_element_type=F32)
        return raw * score_scale + key_bias[None, None, :]

    stored = []
    peak_list = []
    current = tokens.astype(F32)
    for level in range(layer_count):
        limits = act_ranges[level]
        tops = weight_tops[level]
        w_qkv = squash(qkv_blocks[level].astype(F32), tops[0]).astype(BF16)
        w_out = squash(out_weight[level].astype(F32), tops[1]).astype(BF16)
        w_up = squash(up_weight[level].astype(F32), tops[2]).astype(BF16)
        w_down = squash(down_weight[level].astype(F32), tops[3]).astype(BF16)
        x_low_all = gather_rows(squash(current, limits[0]).astype(BF16))
        heads = (all_rows, heads_here, HD)
        queries = (mm(x_low_all, w_qkv[0]) + qv_bias[level, 0].astype(F32)).astype(BF16).reshape(heads)
        key_rows = mm(x_low_all, w_qkv[1]).astype(BF16).reshape(heads)
        value_rows = (mm(x_low_all, w_qkv[2]) + qv_bias[level, 1].astype(F32)).astype(BF16).reshape(heads)
        scores = scores_of(queries, key_rows)
        peak_score = jnp.max(scores, axis=-1, keepdims=True)
        log_total = peak_score + jnp.log(jnp.sum(jnp.exp(scores - peak_score), axis=-1, keepdims=True))
        attn_probs = jnp.exp(scores - log_total).astype(BF16)
        context = jnp.einsum("hqk,khd->qhd", attn_probs, value_rows, preferred_element_type=F32)
        context = context.reshape(all_rows, local_width)
        ctx_low = squash(context, limits[1]).astype(BF16)
        attn_rows = scatter_rows(mm(ctx_low, w_out))
        mid_unit, mid_scale = norm_parts(current + attn_rows + out_bias[level].astype(F32))
        hidden = mid_unit * norm_params[level, 0] + norm_params[level, 1]
        hid_low_all = gather_rows(squash(hidden, limits[2]).astype(BF16))
        up_value = mm(hid_low_all, w_up) + up_bias[level].astype(F32)
        normal_cdf = 0.5 + 0.5 * lax.erf(up_value * (0.5**0.5))
        active = up_value * normal_cdf
        act_level = jnp.tanh(active / limits[3])
        act_low = (limits[3] * act_level).astype(BF16)
        gelu_slope = normal_cdf + up_value * jnp.exp(-0.5 * up_value * up_value) * 0.3989422804014327
        up_slope = (1.0 - act_level * act_level) * gelu_slope
        down_rows = scatter_rows(mm(act_low, w_down))
        out_unit, out_scale = norm_parts(hidden + down_rows + down_bias[level].astype(F32))
        peak_list.append(
            jnp.stack(
                [
                    jnp.max(jnp.abs(current) * valid_rows),
                    jnp.max(jnp.abs(context) * valid_all),
                    jnp.max(jnp.abs(hidden) * valid_rows),
                    jnp.max(jnp.abs(active) * valid_all),
                ]
            )
        )
        stored.append(
            (
                current, mid_unit, mid_scale, hidden, out_unit, out_scale, x_low_all, queries, key_rows, value_rows,
                log_total, context, ctx_low, hid_low_all, up_slope, act_low, w_qkv, w_out, w_up, w_down,
            )
        )
        current = out_unit * norm_params[level, 2] + norm_params[level, 3]
    output = current.astype(BF16)
    gradient = cotangent.astype(F32) * valid_rows

    dp_bits = bits_of(dp_count)
    big_list = [None] * layer_count
    rep_list = [None] * layer_count
    shard_list = [None] * layer_count
    for level in reversed(range(layer_count)):
        (
            inputs, mid_unit, mid_scale, hidden, out_unit, out_scale, x_low_all, queries, key_rows, value_rows,
            log_total, context, ctx_low, hid_low_all, up_slope, act_low, w_qkv, w_out, w_up, w_down,
        ) = stored[level]
        limits = act_ranges[level]
        tops = weight_tops[level]
        d_final, d_gain_out, d_shift_out = norm_back(gradient, out_unit, out_scale, norm_params[level, 2])
        down_grad = d_final.astype(BF16)
        d_down_bias = jnp.sum(down_grad.astype(F32), axis=0)
        down_grad_all = gather_rows(down_grad)
        up_grad = (mm_t(down_grad_all, w_down) * up_slope).astype(BF16)
        g_down = reduce_weight(act_low, down_grad_all, down_weight[level], tops[3], dp_bits)
        d_up_bias = jnp.sum(up_grad.astype(F32), axis=0)
        d_hid_rows = scatter_rows(mm_t(up_grad, w_up))
        g_up = reduce_weight(hid_low_all, up_grad, up_weight[level], tops[2], dp_bits)
        d_hidden = d_final + d_hid_rows * squash_slope(hidden, limits[2])
        d_mid, d_gain_mid, d_shift_mid = norm_back(d_hidden, mid_unit, mid_scale, norm_params[level, 0])
        out_grad = d_mid.astype(BF16)
        d_out_bias = jnp.sum(out_grad.astype(F32), axis=0)
        out_grad_all = gather_rows(out_grad)
        ctx_grad = (mm_t(out_grad_all, w_out) * squash_slope(context, limits[1])).astype(BF16)
        g_out = reduce_weight(ctx_low, out_grad_all, out_weight[level], tops[1], dp_bits)
        ctx_grad = ctx_grad.reshape(heads)
        soft_probs = jnp.exp(scores_of(queries, key_rows) - log_total)
        soft_low = soft_probs.astype(BF16)
        d_values = jnp.einsum("hqk,qhd->khd", soft_low, ctx_grad, preferred_element_type=F32)
        d_probs = jnp.einsum("qhd,khd->hqk", ctx_grad, value_rows, preferred_element_type=F32)
        d_scores = (
            soft_probs * (d_probs - jnp.sum(soft_probs * d_probs, axis=-1, keepdims=True))
        ).astype(BF16)
        d_queries = jnp.einsum("hqk,khd->qhd", d_scores, key_rows, preferred_element_type=F32) * score_scale
        d_keys = jnp.einsum("hqk,qhd->khd", d_scores, queries, preferred_element_type=F32) * score_scale
        parts = [
            item.astype(BF16).reshape(all_rows, local_width) for item in (d_queries, d_keys, d_values)
        ]
        d_x_rows = scatter_rows(
            mm_t(parts[0], w_qkv[0]) + mm_t(parts[1], w_qkv[1]) + mm_t(parts[2], w_qkv[2])
        )
        g_qkv = reduce_weight(
            x_low_all,
            jnp.concatenate(parts, axis=1),
            jnp.transpose(qkv_blocks[level], (1, 0, 2)).reshape(width, 3 * local_width),
            tops[0],
            dp_bits,
        ).reshape(width, 3, local_width)
        d_qv_bias = jnp.stack([jnp.sum(parts[0].astype(F32), axis=0), jnp.sum(parts[2].astype(F32), axis=0)])
        gradient = d_mid + d_x_rows * squash_slope(inputs, limits[0])
        big_list[level] = (g_qkv, g_out, g_up, g_down)
        rep_list[level] = jnp.stack([d_out_bias, d_down_bias, d_gain_mid, d_shift_mid, d_gain_out, d_shift_out])
        shard_list[level] = (d_qv_bias, d_up_bias)

    rep = jnp.stack(rep_list)
    peaks = jnp.stack(peak_list)
    for bit in bits_of(tp_count):
        rep = rep + swap(rep, "tp", bit)
        peaks = jnp.maximum(peaks, swap(peaks, "tp", bit))
    qv_sum = jnp.stack([item[0] for item in shard_list])
    up_sum = jnp.stack([item[1] for item in shard_list])
    sizes = [rep.size, qv_sum.size, up_sum.size]
    pack = jnp.concatenate([rep.reshape(-1), qv_sum.reshape(-1), up_sum.reshape(-1)])
    for bit in dp_bits:
        pack = pack + swap(pack, "dp", bit)
        peaks = jnp.maximum(peaks, swap(peaks, "dp", bit))
    rep = pack[: sizes[0]].reshape(rep.shape)
    qv_sum = pack[sizes[0] : sizes[0] + sizes[1]].reshape(qv_sum.shape)
    up_sum = pack[sizes[0] + sizes[1] :].reshape(up_sum.shape)
    grads = [jnp.stack([entry[item] for entry in big_list]) for item in range(4)]
    return (
        output,
        gradient,
        grads[0],
        qv_sum,
        grads[1],
        rep[:, 0],
        grads[2],
        up_sum,
        grads[3],
        rep[:, 1],
        rep[:, 2:],
        peaks,
    )


ERF_TOP = (
    -2.72614225801306e-10, 2.77068142495902e-08, -2.10102402082508e-06, -5.69250639462346e-05,
    -7.34990630326855e-04, -2.95459980854025e-03, -1.60960333262415e-02,
)
ERF_LOW = (
    -1.45660718464996e-05, -2.13374055278905e-04, -1.68282697438203e-03, -7.37332916720468e-03,
    -1.42647390514189e-02,
)


def erf_ratio(value):
    value = jnp.clip(value, -4.0, 4.0)
    square = value * value
    top = ERF_TOP[0]
    for factor in ERF_TOP[1:]:
        top = top * square + factor
    low = ERF_LOW[0]
    for factor in ERF_LOW[1:]:
        low = low * square + factor
    return value * top / low


def whole(shape):
    return pl.BlockSpec(shape, lambda *_: (0,) * len(shape))


SMEM = pl.BlockSpec(memory_space=pltpu.SMEM)


def cost(*_):
    return pl.CostEstimate(flops=1, bytes_accessed=1, transcendentals=0)


def params(mib=56):
    return pltpu.CompilerParams(vmem_limit_bytes=mib << 20)


def shaped(shape, dtype):
    return jax.ShapeDtypeStruct(shape, dtype)


class Line:
    mark = None
    due = []
    free = False


def launch(
    kernel, *, out_shape, in_specs=(), out_specs=(), grid=None, grid_spec=None, scratch_shapes=(),
    input_output_aliases=None, compiler_params=None, cost_estimate=None, far_ins=(), far_outs=(),
):
    single = not isinstance(out_shape, (list, tuple))
    outs = [out_shape] if single else list(out_shape)
    if grid_spec is None:
        scalars, scratch = 0, list(scratch_shapes)
        ins_list, outs_list = list(in_specs), [out_specs] if single else list(out_specs)
    else:
        scalars, grid, scratch = grid_spec.num_scalar_prefetch, grid_spec.grid, list(grid_spec.scratch_shapes)
        ins_list, outs_list = list(grid_spec.in_specs), list(grid_spec.out_specs)

    def called(*args):
        marks = ([] if Line.mark is None else [Line.mark]) + Line.due
        Line.due = []
        args = [
            pltpu.with_memory_space_constraint(item, pltpu.HBM) if place - scalars in far_ins else item
            for place, item in enumerate(args)
        ]
        first = scalars + len(ins_list)

        def body(*refs):
            refs = list(refs)
            del refs[first : first + len(marks)]
            del refs[first + len(outs)]
            kernel(*refs)

        anywhere = pl.BlockSpec(memory_space=pl.ANY)
        spec = pltpu.PrefetchScalarGridSpec(
            num_scalar_prefetch=scalars,
            grid=grid,
            in_specs=ins_list + [anywhere] * len(marks),
            out_specs=outs_list + [anywhere],
            scratch_shapes=scratch,
        )
        results = pl.pallas_call(
            body,
            out_shape=[
                pltpu.HBM(item.shape, item.dtype) if place in far_outs else item for place, item in enumerate(outs)
            ]
            + [shaped((8, 128), F32)],
            grid_spec=spec,
            input_output_aliases=input_output_aliases or {},
            compiler_params=compiler_params,
            cost_estimate=cost_estimate,
        )(*args, *marks)
        if not Line.free:
            Line.mark = results[-1]
        return results[0] if single else list(results[:-1])

    return called


def tops_kernel(*refs):
    weights, out_ref, scratch = refs[:4], refs[4], refs[5:]
    layer, step = pl.program_id(0), pl.program_id(1)
    for item in range(4):
        block = jnp.abs(weights[item][...])
        lanes = block.shape[-1]
        part = jnp.max(block.reshape(-1, 16, lanes), axis=0)

        @pl.when(step == 0)
        def _():
            scratch[item][...] = part

        @pl.when(step > 0)
        def _():
            scratch[item][...] = jnp.maximum(scratch[item][...], part)

    @pl.when(step == pl.num_programs(1) - 1)
    def _():
        for item in range(4):
            top = jnp.max(scratch[item][...].astype(F32), axis=0, keepdims=True)
            top = jnp.max(top, axis=1, keepdims=True)
            out_ref[0, item : item + 1, :] = jnp.broadcast_to(top, (1, 128))


def weight_tops_of(weights):
    layers = weights[0].shape[0]
    steps = 4
    in_specs, scratch = [], []
    for weight in weights:
        rows = weight.shape[-2] // steps
        if weight.ndim == 4:
            in_specs.append(pl.BlockSpec((1, weight.shape[1], rows, weight.shape[3]), lambda l, s: (l, 0, s, 0)))
        else:
            in_specs.append(pl.BlockSpec((1, rows, weight.shape[2]), lambda l, s: (l, s, 0)))
        scratch.append(pltpu.VMEM((16, weight.shape[-1]), BF16))
    return launch(
        tops_kernel,
        out_shape=shaped((layers, 4, 128), F32),
        grid=(layers, steps),
        in_specs=in_specs,
        out_specs=pl.BlockSpec((1, 4, 128), lambda l, s: (l, 0, 0)),
        scratch_shapes=scratch,
        compiler_params=params(16),
        cost_estimate=cost(0, sum(weight.size * 2 for weight in weights)),
        far_ins=(0, 1, 2, 3),
    )(*weights)


def top_of(tops_refs, level, item):
    top = tops_refs[0][level, item : item + 1, 0:1]
    for ref in tops_refs[1:]:
        top = jnp.maximum(top, ref[level, item : item + 1, 0:1])
    return top


def squash_kernel(level, items, t0, t1, t2, t3, *refs):
    for place, item in enumerate(items):
        top = top_of((t0, t1, t2, t3), level, item)
        inverse = 1.0 / top
        value = refs[place][0].astype(F32)
        refs[len(items) + place][...] = (top * jnp.tanh(value * inverse)).astype(BF16)


def squash_weights(level, items, tops, weights):
    steps = 4
    in_specs, out_specs, outs = [whole(tops[0].shape)] * 4, [], []
    for weight in weights:
        rows = weight.shape[-2] // steps
        if weight.ndim == 4:
            in_specs.append(
                pl.BlockSpec((1, weight.shape[1], rows, weight.shape[3]), lambda s: (level, 0, s, 0))
            )
            out_specs.append(pl.BlockSpec((weight.shape[1], rows, weight.shape[3]), lambda s: (0, s, 0)))
        else:
            in_specs.append(pl.BlockSpec((1, rows, weight.shape[2]), lambda s: (level, s, 0)))
            out_specs.append(pl.BlockSpec((rows, weight.shape[2]), lambda s: (s, 0)))
        outs.append(shaped(weight.shape[1:], BF16))
    moved = sum(weight.size * 2 for weight in weights)
    return launch(
        functools.partial(squash_kernel, level, items),
        out_shape=outs,
        grid=(steps,),
        in_specs=in_specs,
        out_specs=out_specs,
        compiler_params=params(16),
        cost_estimate=cost(0, moved, moved // 4),
        far_ins=range(4, 8), far_outs=range(4),
    )(*tops, *weights)


def slope_kernel(level, place_ref, t0, t1, t2, t3, qkv_ref, out_ref, up_ref, down_ref, *targets):
    def slope(value, item):
        level_value = jnp.tanh(value.astype(F32) * (1.0 / top_of((t0, t1, t2, t3), level, item)))
        return 1.0 - level_value * level_value

    targets[0][...] = slope(down_ref[0], 3)
    targets[1][...] = slope(up_ref[0], 2)
    local = qkv_ref.shape[3]
    for part in range(3):
        targets[2][:, part * local : (part + 1) * local] = slope(qkv_ref[0, part], 0)
    piece = slope(out_ref[0], 1)
    span = piece.shape[0]
    rows = targets[2].shape[0]
    side = piece.shape[1] * span // rows
    for item in range(rows // span):
        targets[2][item * span : (item + 1) * span, 3 * local :] = piece[:, item * side : (item + 1) * side]


def slope_pieces(level, place, tops, weights):
    specs = []
    for weight in weights:
        rows = weight.shape[-2] // 8
        if weight.ndim == 4:
            specs.append(pl.BlockSpec((1, weight.shape[1], rows, weight.shape[3]), lambda s, p: (level, 0, p[0], 0)))
        else:
            specs.append(pl.BlockSpec((1, rows, weight.shape[2]), lambda s, p: (level, p[0], 0)))
    width = weights[2].shape[1]
    rows = width // 8
    outs = [shaped((rows, width), F32)] * 3
    return launch(
        functools.partial(slope_kernel, level),
        out_shape=outs,
        grid_spec=pltpu.PrefetchScalarGridSpec(
            num_scalar_prefetch=1,
            grid=(1,),
            in_specs=[whole(tops[0].shape)] * 4 + specs,
            out_specs=[whole(item.shape) for item in outs],
        ),
        compiler_params=params(12),
        cost_estimate=cost(0, 3 << 20, 1 << 19),
        far_ins=range(4, 8), far_outs=range(3),
    )(place, *tops, *weights)


def valid_of(info_ref, rows, blocks):
    row = lax.broadcasted_iota(jnp.int32, (rows, 1), 0)
    columns = [(row + info_ref[block] < info_ref[4]).astype(F32) for block in blocks]
    return columns[0] if len(columns) == 1 else jnp.concatenate(columns, axis=0)


def key_bias_of(info_ref, rows):
    lane = lax.broadcasted_iota(jnp.int32, (1, rows), 1)
    return jnp.concatenate(
        [jnp.where(lane + info_ref[block] < info_ref[4], 0.0, -1000000000.0) for block in range(4)], axis=1
    )


def attn_forward_kernel(level, info_ref, limits_ref, x0, x1, x2, x3, w_ref, bias_ref, out_w_ref,
                        qkv_ref, ctx_ref, low_ref, peak_ref, send_ref, keep_ref, x_ref):
    rows = x0.shape[0]
    for place, piece in enumerate((x0, x1, x2, x3)):
        x_ref[place * rows : (place + 1) * rows, :] = piece[...]
    x = x_ref[...]
    for part in range(3):
        total = mm(x, w_ref[part])
        if part != 1:
            total = total + bias_ref[level, part // 2 : part // 2 + 1, :].astype(F32)
        qkv_ref[part] = total.astype(BF16)
    limit = limits_ref[level, 1]
    key_bias = key_bias_of(info_ref, rows)
    inverse = 1.0 / limit
    for head in range(qkv_ref.shape[2] // HD):
        here = slice(head * HD, (head + 1) * HD)
        scores = mm_t(qkv_ref[0, :, here], qkv_ref[1, :, here]) * (HD**-0.5) + key_bias
        scores = jnp.exp(scores - jnp.max(scores, axis=-1, keepdims=True))
        probs = (scores * (1.0 / jnp.sum(scores, axis=-1, keepdims=True))).astype(BF16)
        ctx_ref[:, here] = mm(probs, qkv_ref[2, :, here])
    context = ctx_ref[...]
    peak_ref[...] = jnp.max(jnp.abs(context) * valid_of(info_ref, rows, (0, 1, 2, 3)), axis=0, keepdims=True)
    low = (limit * jnp.tanh(context * inverse)).astype(BF16)
    low_ref[...] = low
    half = low.shape[0] // 2
    send_ref[...] = mm(low[half:], out_w_ref[...]).astype(BF16)
    keep_ref[...] = mm(low[:half], out_w_ref[...])


def attn_forward(level, info, limits, pieces, w_qkv, bias, w_out):
    rows, width = pieces[0].shape
    total = 4 * rows
    local = w_out.shape[0]
    ins = (info, limits, *pieces, w_qkv, bias, w_out)
    outs = [
        shaped((3, total, local), BF16),
        shaped((total, local), F32),
        shaped((total, local), BF16),
        shaped((1, local), F32),
        shaped((total // 2, width), BF16),
        shaped((total // 2, width), F32),
    ]
    return launch(
        functools.partial(attn_forward_kernel, level),
        out_shape=outs,
        in_specs=[SMEM, SMEM] + [whole(item.shape) for item in ins[2:]],
        out_specs=[whole(item.shape) for item in outs],
        scratch_shapes=[pltpu.VMEM((total, width), BF16)],
        grid=(1,),
        compiler_params=params(28),
        cost_estimate=cost(5e9, 8 << 20, 1 << 20),
        far_ins=(6, 8), far_outs=(0, 1, 2),
    )(*ins)


def ffn_forward_kernel(level, info_ref, limits_ref, x0, x1, x2, x3, up_w_ref, bias_ref, down_w_ref,
                       low_ref, slope_ref, peak_ref, send_ref, keep_ref):
    step = pl.program_id(0)
    limit = limits_ref[level, 3]
    inverse = 1.0 / limit

    def work(first, second, blocks, out_ref):
        both = jnp.concatenate([first[...], second[...]], axis=0)
        up = mm(both, up_w_ref[...]) + bias_ref[level : level + 1, :].astype(F32)
        cdf = 0.5 + 0.5 * erf_ratio(up * (0.5**0.5))
        active = up * cdf
        tanh = jnp.tanh(active * inverse)
        low = (limit * tanh).astype(BF16)
        low_ref[...] = low
        slope_ref[...] = (1.0 - tanh * tanh) * (
            cdf + up * jnp.exp(-0.5 * up * up) * 0.3989422804014327
        )
        peak = jnp.max(jnp.abs(active) * valid_of(info_ref, x0.shape[0], blocks), axis=0, keepdims=True)
        peak_ref[...] = jnp.where(step == 0, peak, jnp.maximum(peak_ref[...], peak))
        out_ref[...] = mm(low, down_w_ref[...]).astype(out_ref.dtype)

    pl.when(step == 0)(functools.partial(work, x0, x1, (0, 1), keep_ref))
    pl.when(step == 1)(functools.partial(work, x2, x3, (2, 3), send_ref))


def ffn_forward(level, info, limits, pieces, w_up, bias, w_down):
    rows, width = pieces[0].shape
    units = w_up.shape[1]
    total = 4 * rows
    outs = [
        shaped((total, units), BF16),
        shaped((total, units), F32),
        shaped((1, units), F32),
        shaped((total // 2, width), BF16),
        shaped((total // 2, width), F32),
    ]
    return launch(
        functools.partial(ffn_forward_kernel, level),
        out_shape=outs,
        grid=(2,),
        in_specs=[SMEM, SMEM]
        + [whole((rows, width))] * 4
        + [whole(w_up.shape), whole(bias.shape), whole(w_down.shape)],
        out_specs=[
            pl.BlockSpec((2 * rows, units), lambda s: (s, 0)),
            pl.BlockSpec((2 * rows, units), lambda s: (s, 0)),
            whole((1, units)),
            whole((2 * rows, width)),
            whole((2 * rows, width)),
        ],
        compiler_params=params(32),
        cost_estimate=cost(8e9, 12 << 20, 2 << 20),
        far_ins=(6, 8), far_outs=(0, 1),
    )(info, limits, *pieces, w_up, bias, w_down)


def enter_kernel(info_ref, limits_ref, tokens_ref, low_ref, peak_ref):
    value = tokens_ref[...].astype(F32)
    limit = limits_ref[0, 0]
    low_ref[...] = (limit * jnp.tanh(value * (1.0 / limit))).astype(BF16)
    peak_ref[...] = jnp.max(jnp.abs(value) * valid_of(info_ref, value.shape[0], (0,)), axis=0, keepdims=True)


def enter(info, limits, tokens):
    outs = [shaped(tokens.shape, BF16), shaped((1, tokens.shape[1]), F32)]
    return launch(
        enter_kernel,
        out_shape=outs,
        grid=(1,),
        in_specs=[SMEM, SMEM, whole(tokens.shape)],
        out_specs=[whole(item.shape) for item in outs],
        compiler_params=params(8),
        cost_estimate=cost(),
    )(info, limits, tokens)


def join_kernel(level, item, last, info_ref, limits_ref, base_ref, keep_ref, core_ref, far_ref, bias_ref, norm_ref,
                *outs):
    arrived = keep_ref[...] + core_ref[...].astype(F32) + far_ref[...].astype(F32)
    unit, scale = norm_parts(base_ref[...].astype(F32) + arrived + bias_ref[level : level + 1, :].astype(F32))
    value = unit * norm_ref[level, item : item + 1, :] + norm_ref[level, item + 1 : item + 2, :]
    outs[0][...] = unit
    outs[1][...] = scale
    if last:
        outs[2][...] = value.astype(BF16)
    else:
        outs[2][...] = value
        limit = limits_ref[level, 2] if item == 0 else limits_ref[level + 1, 0]
        outs[3][...] = (limit * jnp.tanh(value * (1.0 / limit))).astype(BF16)
        peak = jnp.abs(value) * valid_of(info_ref, value.shape[0], (0,))
        outs[4][...] = jnp.max(peak, axis=0, keepdims=True)


def join_rows(level, item, last, info, limits, base, keep, core, far, bias, norm):
    rows, width = base.shape
    outs = [shaped((rows, width), F32), shaped((rows, 1), F32)]
    if last:
        outs += [shaped((rows, width), BF16)]
    else:
        outs += [shaped((rows, width), F32), shaped((rows, width), BF16), shaped((1, width), F32)]
    block = whole((rows, width))
    return launch(
        functools.partial(join_kernel, level, item, last),
        out_shape=outs,
        grid=(1,),
        in_specs=[SMEM, SMEM, block, block, block, block, whole(bias.shape), whole(norm.shape)],
        out_specs=[whole(item.shape) for item in outs],
        compiler_params=params(12),
        cost_estimate=cost(),
        far_outs=(0, 1),
    )(info, limits, base, keep, core, far, bias, norm)


def norm_back_store(gradient, unit_ref, scale_ref, gain, d_ref, low_ref, sums_ref):
    unit = unit_ref[...]
    scaled = gradient * gain
    first = jnp.mean(scaled, axis=-1, keepdims=True)
    second = jnp.mean(scaled * unit, axis=-1, keepdims=True)
    d_values = scale_ref[...] * (scaled - first - unit * second)
    low = d_values.astype(BF16)
    d_ref[...] = d_values
    low_ref[...] = low
    sums_ref[0:1, :] = jnp.sum(low.astype(F32), axis=0, keepdims=True)
    sums_ref[1:2, :] = jnp.sum(gradient * unit, axis=0, keepdims=True)
    sums_ref[2:3, :] = jnp.sum(gradient, axis=0, keepdims=True)


def top_back_kernel(level, info_ref, cot_ref, unit_ref, scale_ref, norm_ref, d_ref, low_ref, sums_ref):
    gradient = cot_ref[...].astype(F32) * valid_of(info_ref, cot_ref.shape[0], (0,))
    norm_back_store(gradient, unit_ref, scale_ref, norm_ref[level, 2:3, :], d_ref, low_ref, sums_ref)


def mid_back_kernel(level, item, limits_ref, base_ref, keep_ref, core_ref, far_ref, unit_ref, scale_ref, norm_ref,
                    d_ref, low_ref, sums_ref):
    arrived = keep_ref[...] + core_ref[...].astype(F32) + far_ref[...].astype(F32)
    gain = norm_ref[level, item : item + 1, :]
    value = unit_ref[...] * gain + norm_ref[level, item + 1 : item + 2, :]
    limit = limits_ref[level, 2] if item == 0 else limits_ref[level + 1, 0]
    tanh = jnp.tanh(value * (1.0 / limit))
    gradient = base_ref[...] + arrived * (1.0 - tanh * tanh)
    norm_back_store(gradient, unit_ref, scale_ref, gain, d_ref, low_ref, sums_ref)


def end_back_kernel(limits_ref, base_ref, keep_ref, core_ref, far_ref, x_ref, out_ref):
    arrived = keep_ref[...] + core_ref[...].astype(F32) + far_ref[...].astype(F32)
    tanh = jnp.tanh(x_ref[...].astype(F32) * (1.0 / limits_ref[0, 0]))
    out_ref[...] = base_ref[...] + arrived * (1.0 - tanh * tanh)


def top_back(level, info, cotangent, unit, scale, norm):
    rows, width = unit.shape
    outs = [shaped((rows, width), F32), shaped((rows, width), BF16), shaped((3, width), F32)]
    ins = (cotangent, unit, scale, norm)
    return launch(
        functools.partial(top_back_kernel, level),
        out_shape=outs,
        grid=(1,),
        in_specs=[SMEM] + [whole(item.shape) for item in ins],
        out_specs=[whole(item.shape) for item in outs],
        compiler_params=params(12),
        cost_estimate=cost(),
        far_ins=(1, 2, 3),
    )(info, *ins)


def mid_back(level, item, limits, base, keep, core, far, unit, scale, norm):
    rows, width = unit.shape
    outs = [shaped((rows, width), F32), shaped((rows, width), BF16), shaped((3, width), F32)]
    block = whole((rows, width))
    return launch(
        functools.partial(mid_back_kernel, level, item),
        out_shape=outs,
        grid=(1,),
        in_specs=[SMEM, block, block, block, block, block, whole(scale.shape), whole(norm.shape)],
        out_specs=[whole(item.shape) for item in outs],
        compiler_params=params(12),
        cost_estimate=cost(),
        far_ins=(5, 6), far_outs=(0,),
    )(limits, base, keep, core, far, unit, scale, norm)


def end_back(limits, base, keep, core, far, x):
    block = whole(base.shape)
    return launch(
        end_back_kernel,
        out_shape=shaped(base.shape, F32),
        grid=(1,),
        in_specs=[SMEM] + [block] * 5,
        out_specs=block,
        compiler_params=params(12),
        cost_estimate=cost(),
    )(limits, base, keep, core, far, x)


def ffn_backward_kernel(g0, g1, g2, g3, down_w_ref, slope_ref, up_w_ref, grad_ref, sum_ref, send_ref, keep_ref):
    step = pl.program_id(0)

    def work(first, second, out_ref):
        both = jnp.concatenate([first[...], second[...]], axis=0)
        grad = (mm_t(both, down_w_ref[...]) * slope_ref[...]).astype(BF16)
        grad_ref[...] = grad
        part = jnp.sum(grad.astype(F32), axis=0, keepdims=True)
        sum_ref[...] = jnp.where(step == 0, part, sum_ref[...] + part)
        out_ref[...] = mm_t(grad, up_w_ref[...]).astype(out_ref.dtype)

    pl.when(step == 0)(functools.partial(work, g0, g1, keep_ref))
    pl.when(step == 1)(functools.partial(work, g2, g3, send_ref))


def ffn_backward(pieces, w_down, slope, w_up):
    rows, width = pieces[0].shape
    units = w_up.shape[1]
    total = 4 * rows
    outs = [
        shaped((total, units), BF16),
        shaped((1, units), F32),
        shaped((total // 2, width), BF16),
        shaped((total // 2, width), F32),
    ]
    return launch(
        ffn_backward_kernel,
        out_shape=outs,
        grid=(2,),
        in_specs=[whole((rows, width))] * 4
        + [whole(w_down.shape), pl.BlockSpec((2 * rows, units), lambda s: (s, 0)), whole(w_up.shape)],
        out_specs=[
            pl.BlockSpec((2 * rows, units), lambda s: (s, 0)),
            whole((1, units)),
            whole((2 * rows, width)),
            whole((2 * rows, width)),
        ],
        compiler_params=params(32),
        cost_estimate=cost(3e9, 12 << 20),
        far_ins=(4, 5, 6),
    )(*pieces, w_down, slope, w_up)


def attn_backward_kernel(level, info_ref, limits_ref, g0, g1, g2, g3, out_w_ref, ctx_ref, qkv_ref, w_ref,
                         grad_ref, sum_ref, send_ref, keep_ref, g_ref, cg_ref):
    rows = g0.shape[0]
    for place, piece in enumerate((g0, g1, g2, g3)):
        g_ref[place * rows : (place + 1) * rows, :] = piece[...]
    tanh = jnp.tanh(ctx_ref[...] * (1.0 / limits_ref[level, 1]))
    cg_ref[...] = (mm_t(g_ref[...], out_w_ref[...]) * (1.0 - tanh * tanh)).astype(BF16)
    key_bias = key_bias_of(info_ref, rows)
    local = cg_ref.shape[1]
    for head in range(local // HD):
        here = slice(head * HD, (head + 1) * HD)
        queries, keys, values = qkv_ref[0, :, here], qkv_ref[1, :, here], qkv_ref[2, :, here]
        grad = cg_ref[:, here]
        scores = mm_t(queries, keys) * (HD**-0.5) + key_bias
        scores = jnp.exp(scores - jnp.max(scores, axis=-1, keepdims=True))
        probs = scores * (1.0 / jnp.sum(scores, axis=-1, keepdims=True))
        d_values = t_mm(probs.astype(BF16), grad)
        d_probs = mm_t(grad, values)
        inner = jnp.sum(probs * d_probs, axis=-1, keepdims=True)
        d_scores = (probs * (d_probs - inner)).astype(BF16)
        d_queries = mm(d_scores, keys) * (HD**-0.5)
        d_keys = t_mm(d_scores, queries) * (HD**-0.5)
        for part, item in enumerate((d_queries, d_keys, d_values)):
            start = part * local + head * HD
            grad_ref[:, start : start + HD] = item.astype(BF16)
    sum_ref[0:1, :] = jnp.sum(grad_ref[:, :local].astype(F32), axis=0, keepdims=True)
    sum_ref[1:2, :] = jnp.sum(grad_ref[:, 2 * local :].astype(F32), axis=0, keepdims=True)
    half = g_ref.shape[0] // 2

    def back(first, last):
        total = mm_t(grad_ref[first:last, :local], w_ref[0])
        total += mm_t(grad_ref[first:last, local : 2 * local], w_ref[1])
        return total + mm_t(grad_ref[first:last, 2 * local :], w_ref[2])

    send_ref[...] = back(half, 2 * half).astype(BF16)
    keep_ref[...] = back(0, half)


def attn_backward(level, info, limits, pieces, w_out, context, qkv, w_qkv):
    rows, width = pieces[0].shape
    total = 4 * rows
    local = w_out.shape[0]
    ins = (info, limits, *pieces, w_out, context, qkv, w_qkv)
    outs = [
        shaped((total, 3 * local), BF16),
        shaped((2, local), F32),
        shaped((total // 2, width), BF16),
        shaped((total // 2, width), F32),
    ]
    return launch(
        functools.partial(attn_backward_kernel, level),
        out_shape=outs,
        grid=(1,),
        in_specs=[SMEM, SMEM] + [whole(item.shape) for item in ins[2:]],
        out_specs=[whole(item.shape) for item in outs],
        scratch_shapes=[pltpu.VMEM((total, width), BF16), pltpu.VMEM((total, local), BF16)],
        compiler_params=params(32),
        cost_estimate=cost(6e9, 8 << 20, 1 << 20),
        far_ins=(6, 7, 8, 9),
    )(*ins)


LINK_ORDERS = ((1, 2, 4), (2, 1, 4))
FFN_ORDERS = (0, 1)
ATTN_WHOLE = ((0,), ((0, 1024),))
ATTN_CUT = ((0, 1), ((0, 512), (512, 1024)))


def block_masks(bits):
    return [
        (bits[0] if item & 4 else 0) ^ (bits[1] if item & 2 else 0) ^ (bits[2] if item & 1 else 0)
        for item in range(8)
    ]


def halves(target_pair, item):
    send_ref, keep_ref = target_pair
    return keep_ref if item < 4 else send_ref


def ffn_grad_kernel(table_ref, low_ref, g0, g1, g2, g3, h0, h1, h2, h3, grad_ref, *refs):
    targets, total_ref = refs[:4], refs[4]
    block = total_ref.shape[0] // 8
    for part, order in enumerate(FFN_ORDERS):
        if part == 0:
            total_ref[...] = t_mm(low_ref[...], jnp.concatenate([g0[...], g1[...], g2[...], g3[...]], axis=0))
        else:
            total_ref[...] = t_mm(jnp.concatenate([h0[...], h1[...], h2[...], h3[...]], axis=0), grad_ref[...])
        for item in range(8):
            first = pl.multiple_of(table_ref[order, item] * block, block)
            target = halves(targets[2 * part : 2 * part + 2], item)
            target[item % 4] = total_ref[pl.ds(first, block), :].astype(target.dtype)


def ffn_grad(table, act_low, g_pieces, h_pieces, up_grad):
    ins = [act_low, *g_pieces, *h_pieces, up_grad]
    width = up_grad.shape[1]
    outs = [shaped((4, width // 8, width), dtype) for _ in FFN_ORDERS for dtype in (BF16, F32)]
    return launch(
        ffn_grad_kernel,
        out_shape=outs,
        grid_spec=pltpu.PrefetchScalarGridSpec(
            num_scalar_prefetch=1,
            grid=(1,),
            in_specs=[whole(item.shape) for item in ins],
            out_specs=[whole(item.shape) for item in outs],
            scratch_shapes=[pltpu.VMEM((width, width), F32)],
        ),
        compiler_params=params(34),
        cost_estimate=cost(),
        far_ins=(0, 5, 6, 7, 8), far_outs=range(4),
    )(table, *ins)


def attn_grad_kernel(plan, table_ref, x0, x1, x2, x3, grad_ref, low_ref, g0, g1, g2, g3, *refs):
    targets, total_ref, out_ref = refs[:-2], refs[-2], refs[-1]
    total_ref[...] = t_mm(jnp.concatenate([x0[...], x1[...], x2[...], x3[...]], axis=0), grad_ref[...])
    out_ref[...] = t_mm(low_ref[...], jnp.concatenate([g0[...], g1[...], g2[...], g3[...]], axis=0))
    block = total_ref.shape[0] // 8
    local3 = total_ref.shape[1]
    span = out_ref.shape[0] // 8
    side = out_ref.shape[1] * span // block
    for part, (order, (start, stop)) in enumerate(zip(*plan)):
        for item in range(8):
            target = halves(targets[2 * part : 2 * part + 2], item)
            if start < local3:
                end = min(stop, local3)
                first = pl.multiple_of(table_ref[order, item] * block, block)
                value = total_ref[pl.ds(first, block), start:end]
                target[item % 4, :, : end - start] = value.astype(target.dtype)
            if stop > local3:
                first = pl.multiple_of(table_ref[order, item] * span, span)
                taken = out_ref[pl.ds(first, span), :]
                for place in range(block // span):
                    target[item % 4, place * span : (place + 1) * span, local3 - start :] = taken[
                        :, place * side : (place + 1) * side
                    ].astype(target.dtype)


def attn_grad(plan, table, x_pieces, qkv_grad, ctx_low, g_pieces):
    ins = [*x_pieces, qkv_grad, ctx_low, *g_pieces]
    width = x_pieces[0].shape[1]
    outs = [shaped((4, width // 8, last - first), dtype) for first, last in plan[1] for dtype in (BF16, F32)]
    return launch(
        functools.partial(attn_grad_kernel, plan),
        out_shape=outs,
        grid_spec=pltpu.PrefetchScalarGridSpec(
            num_scalar_prefetch=1,
            grid=(1,),
            in_specs=[whole(item.shape) for item in ins],
            out_specs=[whole(item.shape) for item in outs],
            scratch_shapes=[
                pltpu.VMEM((width, qkv_grad.shape[1]), F32),
                pltpu.VMEM((ctx_low.shape[1], width), F32),
            ],
        ),
        compiler_params=params(30),
        cost_estimate=cost(),
        far_ins=(0, 1, 2, 3, 5), far_outs=range(6),
    )(table, *ins)


def fold_kernel(count, parts, scaled, *refs):
    outs = refs[-parts:]
    for part in range(parts):
        mine = refs[part * count : (part + 1) * count]
        total = mine[0][...]
        for other in mine[1:]:
            total = total + other[...].astype(F32)
        if scaled:
            total = total * refs[parts * count + part][...]
        outs[part][...] = total.astype(BF16)


def fold(size, parts, scales=None):
    ins, in_specs, outs, out_specs = [], [], [], []
    count = len(parts[0])
    blocks = max(size, 1)
    for arrays in parts:
        rest = arrays[0].shape[1:]
        for array in arrays:
            ins.append(array)
            place = 1 if size else 0
            in_specs.append(pl.BlockSpec((blocks, *rest), lambda s, place=place: (place, 0, 0)))
        outs.append(shaped((blocks, *rest), BF16))
        out_specs.append(whole((blocks, *rest)))
    if scales is not None:
        for scale, columns in scales:
            width = columns[1] - columns[0]
            ins.append(scale)
            in_specs.append(pl.BlockSpec((scale.shape[0], width), lambda s, at=columns[0] // width: (0, at)))
    return launch(
        functools.partial(fold_kernel, count, len(parts), scales is not None),
        out_shape=outs,
        grid=(1,),
        in_specs=in_specs,
        out_specs=out_specs,
        compiler_params=params(16),
        cost_estimate=cost(),
        far_ins=range(len(ins)), far_outs=range(len(outs)),
    )(*ins)


def pair_kernel(parts, *refs):
    for part in range(parts):
        first, second, target = refs[2 * part], refs[2 * part + 1], refs[2 * parts + part]
        half = first.shape[0]
        target[:half] = first[...]
        target[half:] = second[...]


def pair(firsts, seconds):
    ins = [item for both in zip(firsts, seconds) for item in both]
    outs = [shaped((2 * item.shape[0], *item.shape[1:]), BF16) for item in firsts]
    return launch(
        functools.partial(pair_kernel, len(firsts)),
        out_shape=outs,
        grid=(1,),
        in_specs=[whole(item.shape) for item in ins],
        out_specs=[whole(item.shape) for item in outs],
        compiler_params=params(12),
        cost_estimate=cost(),
        far_ins=range(len(ins)), far_outs=range(len(outs)),
    )(*ins)


def place_kernel(plan, table_ref, *refs):
    outs = refs[-2:]
    step = pl.program_id(0)

    def store(part, source, item):
        start, stop = plan[1][part]
        if len(outs[0].shape) == 3:
            outs[part][0] = source[item].astype(F32)
            return
        qkv_ref, out_ref = outs
        local = qkv_ref.shape[3]
        for column in range(start, min(stop, 3 * local), 128):
            target = slice(column % local, column % local + 128)
            qkv_ref[0, column // local, :, target] = source[item, :, column - start : column - start + 128].astype(F32)
        if stop > 3 * local:
            span = out_ref.shape[1]
            side = stop - 3 * local
            for place in range(source.shape[1] // span):
                out_ref[0, :, place * side : (place + 1) * side] = source[
                    item, place * span : (place + 1) * span, 3 * local - start :
                ].astype(F32)

    for part, order in enumerate(plan[0]):
        item = table_ref[order, step]
        pl.when(item < 4)(functools.partial(store, part, refs[2 * part], item))
        pl.when(item >= 4)(functools.partial(store, part, refs[2 * part + 1], item - 4))


def place_blocks(plan, table, level, nears, fars, shapes, earlier):
    specs = []
    for shape in shapes:
        if len(shape) == 4:
            specs.append(pl.BlockSpec((1, shape[1], shape[2] // 8, shape[3]), lambda s, t: (level, 0, s, 0)))
        else:
            specs.append(pl.BlockSpec((1, shape[1] // 8, shape[2]), lambda s, t: (level, s, 0)))
    ins = [item for both in zip(nears, fars) for item in both]
    earlier = list(earlier or [])
    return launch(
        functools.partial(place_kernel, plan),
        out_shape=[shaped(shape, F32) for shape in shapes],
        grid_spec=pltpu.PrefetchScalarGridSpec(
            num_scalar_prefetch=1,
            grid=(8,),
            in_specs=[whole(item.shape) for item in ins] + [pl.BlockSpec(memory_space=pl.ANY)] * len(earlier),
            out_specs=specs,
        ),
        input_output_aliases={1 + len(ins) + place: place for place in range(len(earlier))},
        compiler_params=params(24),
        cost_estimate=cost(),
        far_ins=range(len(ins)), far_outs=range(len(shapes)),
    )(table, *ins, *earlier)


def near_sum_kernel(keep_ref, near_ref, out_ref):
    out_ref[...] = (keep_ref[...] + near_ref[...].astype(F32)).astype(BF16)


def near_sum(keep, near):
    rows, width = keep.shape[0] // 2, keep.shape[1]
    second = pl.BlockSpec((rows, width), lambda s: (1, 0))
    return launch(
        near_sum_kernel,
        out_shape=shaped((rows, width), BF16),
        grid=(1,),
        in_specs=[second, second],
        out_specs=whole((rows, width)),
        compiler_params=params(8),
        cost_estimate=cost(),
    )(keep, near)


def pack_kernel(layers, *refs):
    out_ref = refs[-1]
    row = 0
    for layer in range(layers):
        mid, out = refs[2 * layer], refs[2 * layer + 1]
        for source in (mid[0:1, :], out[0:1, :], mid[1:3, :], out[1:3, :]):
            out_ref[row : row + source.shape[0], :] = source
            row += source.shape[0]
    out_ref[row : row + 1, :] = refs[-2][...]


def pack(sums, peaks):
    ins = [item for both in sums for item in both] + [peaks]
    out = shaped((6 * len(sums) + 1, peaks.shape[1]), F32)
    return launch(
        functools.partial(pack_kernel, len(sums)),
        out_shape=out,
        grid=(1,),
        in_specs=[whole(item.shape) for item in ins],
        out_specs=whole(out.shape),
        compiler_params=params(8),
        cost_estimate=cost(),
    )(*ins)


def merge_kernel(peak_row, more, mine_ref, other_ref, *refs):
    out_ref = refs[-1]
    mine, other = mine_ref[...], other_ref[...]
    row = lax.broadcasted_iota(jnp.int32, mine.shape, 0)
    merged = jnp.where(row == peak_row, jnp.maximum(mine, other), mine + other)
    if not more:
        out_ref[...] = merged
        return
    count = mine.shape[0]
    out_ref[:count, :] = merged
    for item in range(more):
        up_ref, qv_ref = refs[2 * item], refs[2 * item + 1]
        out_ref[count + item : count + item + 1, :] = up_ref[...]
        local = qv_ref.shape[1]
        for part in range(2):
            start = (2 * item + part) * local
            out_ref[count + more : count + more + 1, start : start + local] = qv_ref[part : part + 1, :]


def merge(peak_row, mine, other, shards=()):
    ins = [mine, other] + [item for both in shards for item in both]
    rows = mine.shape[0] + (len(shards) + 1 if shards else 0)
    return launch(
        functools.partial(merge_kernel, peak_row, len(shards)),
        out_shape=shaped((rows, mine.shape[1]), F32),
        grid=(1,),
        in_specs=[whole(item.shape) for item in ins],
        out_specs=whole((rows, mine.shape[1])),
        compiler_params=params(8),
        cost_estimate=cost(),
    )(*ins)


def peaks_kernel(*refs):
    out_ref = refs[-1]
    for item, ref in enumerate(refs[:-1]):
        top = jnp.max(ref[...], axis=1, keepdims=True)
        out_ref[0:1, item * 128 : (item + 1) * 128] = jnp.broadcast_to(top, (1, 128))


def peaks_row(rows):
    return launch(
        peaks_kernel,
        out_shape=shaped((1, 128 * len(rows)), F32),
        grid=(1,),
        in_specs=[whole(item.shape) for item in rows],
        out_specs=whole((1, 128 * len(rows))),
        compiler_params=params(8),
        cost_estimate=cost(0, 1 << 16),
    )(*rows)


STEPS = {
    "M41": "F1",
    "M20": "F1",
    "tail0": "F1 F1 F1 F1 T1 T1 T1 T1 T1 T1 F0 F0 F0 F0 F0 F0 T0 T0 T0 T0 T0 T0 S0 S0 S0 S0 S0",
}


def fast_on_device(
    tokens,
    cotangent,
    lengths,
    qkv_weight,
    qv_bias,
    out_weight,
    out_bias,
    up_weight,
    up_bias,
    down_weight,
    down_bias,
    norm_params,
    act_ranges,
):
    row_count, width = tokens.shape
    tp_count = lax.axis_size("tp")
    rank = lax.axis_index("tp")
    place = lax.axis_index("dp")
    layers = qkv_weight.shape[0]
    local = qkv_weight.shape[3]
    order = jnp.array(block_order(tp_count), jnp.int32)
    info = jnp.concatenate([(rank ^ order) * row_count, lengths])
    qkv_blocks = jnp.transpose(qkv_weight, (0, 2, 1, 3))
    weights = (qkv_blocks, out_weight, up_weight, down_weight)
    core_bit, far_bit = bits_of(tp_count)
    place_list = place[None].astype(jnp.int32)
    Line.mark = None
    Line.due = []
    Line.free = False

    def run(step, *values):
        return step(*values)

    def spread(rows):
        return rows, swap(rows, "tp", far_bit), swap(rows, "tp", core_bit)

    def finish(begun):
        rows, far, near = begun
        far, _ = lax.optimization_barrier((far, Line.mark))
        return (rows, far, near, swap(far, "tp", core_bit))

    def gather_sum(send, keep):
        near = swap(send, "tp", core_bit)
        return near, swap(near_sum(keep, near), "tp", far_bit)

    x_low, x_peak = run(enter, info, act_ranges, tokens)
    x_begun = spread(x_low)
    tops = run(weight_tops_of, weights)
    tops = (tops, swap(tops, "tp", core_bit), swap(tops, "tp", far_bit), swap(tops, "tp", core_bit | far_bit))
    low_weights = [dict() for _ in range(layers)]

    def squash_some(level, items, names):
        outs = run(lambda *t: squash_weights(level, items, t, [weights[item] for item in items]), *tops)
        for name, out in zip(names, outs):
            low_weights[level][name] = out

    squash_some(0, (0,), ("qkv",))
    slopes = [None] * layers
    kept = []
    peak_rows = []
    current = tokens
    for level in range(layers):
        low = low_weights[level]
        last = level == layers - 1
        if level == 0:
            squash_some(0, (1,), ("out",))
        x_pieces = finish(x_begun)
        qkv, context, ctx_low, ctx_peak, send, keep = run(
            lambda pieces, w_qkv, w_out: attn_forward(level, info, act_ranges, pieces, w_qkv, qv_bias, w_out),
            x_pieces, low["qkv"], low["out"],
        )
        near, far = gather_sum(send, keep)
        if level == 0:
            squash_some(0, (2, 3), ("up", "down"))
        else:
            slopes[1] = run(lambda *t: slope_pieces(1, place_list, t, weights), *tops)
            slopes[0] = run(lambda *t: slope_pieces(0, place_list, t, weights), *tops)
        mid_unit, mid_scale, hidden, hid_low, hid_peak = run(
            lambda *t: join_rows(level, 0, False, info, act_ranges, *t, out_bias, norm_params),
            current, keep, near, far,
        )
        h_begun = spread(hid_low)
        if level == 0:
            squash_some(1, (0, 1), ("qkv", "out"))
        h_pieces = finish(h_begun)
        act_low, slope, act_peak, send, keep = run(
            lambda pieces, w_up, w_down: ffn_forward(level, info, act_ranges, pieces, w_up, up_bias, w_down),
            h_pieces, low["up"], low["down"],
        )
        near, far = gather_sum(send, keep)
        if level == 0:
            squash_some(1, (2, 3), ("up", "down"))
        else:
            peak_rows.append([x_peak, ctx_peak, hid_peak, act_peak])
            peaks = run(lambda *t: peaks_row(t), *peak_rows[0], *peak_rows[1])
        result = run(
            lambda *t: join_rows(level, 2, last, info, act_ranges, *t, down_bias, norm_params),
            hidden, keep, near, far,
        )
        peak_rows.append([x_peak, ctx_peak, hid_peak, act_peak])
        kept.append(
            dict(
                x=x_pieces, qkv=qkv, context=context, ctx_low=ctx_low, mid_unit=mid_unit, mid_scale=mid_scale,
                h=h_pieces, act_low=act_low, slope=slope, out_unit=result[0], out_scale=result[1], **{
                    "w_" + name: value for name, value in low.items()
                },
            )
        )
        if last:
            output = result[2]
        else:
            current, x_low, x_peak = result[2:]
            x_begun = spread(x_low)

    masks = [block_masks(bits) for bits in LINK_ORDERS]
    table = place ^ jnp.array(masks, jnp.int32)
    inverse = jnp.array([[row.index(item) for item in range(8)] for row in masks], jnp.int32)
    inverse = jnp.take(inverse, place ^ jnp.arange(8), axis=1)
    finished = {"ffn": None, "attn": None}
    shapes = {"ffn": [down_weight.shape, up_weight.shape], "attn": [qkv_blocks.shape, out_weight.shape]}

    full = (0, width)
    plans = {
        "ffn1": (FFN_ORDERS, (full, full)), "ffn0": (FFN_ORDERS, (full, full)), "attn1": ATTN_WHOLE, "attn0": ATTN_CUT,
    }

    def stream(level, name, outs):
        plan = plans[name + str(level)]

        key = {"ffn": "F", "attn": "T"}[name] + str(level)

        def swap_parts(parts, step):
            flying[key] = [swap(item, "dp", LINK_ORDERS[order][step]) for item, order in zip(parts, plan[0])]
            return flying[key]

        moved = [list(outs[1::2]), swap_parts(outs[0::2], 0)]
        yield
        moved.append(swap_parts(fold(2, list(zip(*moved))), 1))
        yield
        moved.append(swap_parts(fold(1, list(zip(*moved))), 2))
        yield
        scales = slopes[level][:2] if name == "ffn" else [slopes[level][2]] * len(plan[0])
        pieces = fold(0, list(zip(*moved)), list(zip(scales, plan[1])))
        for step in (2, 1):
            others = swap_parts(pieces, step)
            yield
            pieces = pair(pieces, others)
        others = swap_parts(pieces, 0)
        yield
        finished[name] = place_blocks(plan, inverse, level, pieces, others, shapes[name], finished[name])
        yield

    streams, flying = {}, {}

    def begin(level, name, outs):
        streams[{"ffn": "F", "attn": "T"}[name] + str(level)] = stream(level, name, outs)
        next(streams[{"ffn": "F", "attn": "T"}[name] + str(level)])

    def go(point, level):
        for item in STEPS.get(point + str(level), "").split():
            if item[-1] == "?":
                Line.due = Line.due + flying[item[:-1]]
            else:
                next(streams[item])

    def back_norm(level, base, keep, near, far):
        return run(
            lambda *t: mid_back(level, 0, act_ranges, *t, norm_params),
            base, keep, near, far, kept[level]["mid_unit"], kept[level]["mid_scale"],
        )

    rep_list = [None] * layers
    shard_list = [None] * layers
    top = layers - 1
    d_final, down_grad, sums_out = run(
        lambda *t: top_back(top, info, cotangent, *t, norm_params),
        kept[top]["out_unit"], kept[top]["out_scale"],
    )
    g_begun = spread(down_grad)
    for level in reversed(range(layers)):
        saved = kept[level]
        go("M4", level + 1)
        g_pieces = finish(g_begun)
        up_grad, up_sum, send, keep = run(
            ffn_backward, g_pieces, saved["w_down"], saved["slope"], saved["w_up"]
        )
        near, far = gather_sum(send, keep)
        begin(
            level, "ffn", run(lambda *t: ffn_grad(table, *t), saved["act_low"], g_pieces, saved["h"], up_grad)
        )
        go("WF", level)
        d_mid, out_grad, sums_mid = back_norm(level, d_final, keep, near, far)
        o_begun = spread(out_grad)
        go("M2", level)
        o_pieces = finish(o_begun)
        qkv_grad, qv_sum, send, keep = run(
            lambda *t: attn_backward(level, info, act_ranges, *t),
            o_pieces, saved["w_out"], saved["context"], saved["qkv"], saved["w_qkv"],
        )
        near, far = gather_sum(send, keep)
        begin(
            level, "attn",
            run(lambda *t: attn_grad(plans["attn" + str(level)], table, *t), saved["x"], qkv_grad, saved["ctx_low"], o_pieces),
        )
        go("WT", level)
        rep_list[level] = (sums_mid, sums_out)
        shard_list[level] = (up_sum, qv_sum)
        if level > 0:
            below = kept[level - 1]
            d_final, down_grad, sums_out = run(
                lambda *t: mid_back(level - 1, 2, act_ranges, *t, norm_params),
                d_mid, keep, near, far, below["out_unit"], below["out_scale"],
            )
            g_begun = spread(down_grad)
        else:
            input_grad = run(lambda *t: end_back(act_ranges, *t, tokens), d_mid, keep, near, far)

    def small():
        peak_row = 6 * layers
        total = pack(rep_list, peaks)
        moved = swap(total, "tp", far_bit)
        flying["S0"] = [moved]
        yield
        total = merge(peak_row, total, moved)
        moved = swap(total, "tp", core_bit)
        flying["S0"] = [moved]
        yield
        total = merge(peak_row, total, moved, shard_list)
        for bit in (1, 2, 4):
            moved = swap(total, "dp", bit)
            flying["S0"] = [moved]
            yield
            total = merge(peak_row, total, moved)
        finished["small"] = total
        yield

    streams["S0"] = small()
    next(streams["S0"])
    Line.free = True
    go("tail", 0)
    rep = finished["small"]
    sums = rep[: 6 * layers].reshape(layers, 6, width)
    peaks = rep[6 * layers].reshape(layers, 4, 128)[:, :, 0]
    up_sum = rep[6 * layers + 1 : 6 * layers + 1 + layers]
    qv_sum = rep[6 * layers + 1 + layers].reshape(layers, 2, local)
    return (
        output,
        input_grad,
        jnp.transpose(finished["attn"][0], (0, 2, 1, 3)),
        qv_sum,
        finished["attn"][1],
        sums[:, 0],
        finished["ffn"][1],
        up_sum,
        finished["ffn"][0],
        sums[:, 1],
        sums[:, 2:],
        peaks,
    )


def any_on_device(*args):
    tokens, lengths, qkv_weight, out_weight, up_weight = args[0], args[2], args[3], args[5], args[7]
    fits = (
        lax.axis_size("tp") == 4
        and lax.axis_size("dp") == 8
        and lengths.shape[0] == 1
        and tokens.shape[0] * 4 == SEQ_LEN
        and tokens.shape[1] == 1024
        and qkv_weight.shape[3] == 256
        and up_weight.shape[2] == 1024
    )
    return (fast_on_device if fits else on_device)(*args)


def solution(mesh):
    return jax.shard_map(
        any_on_device,
        mesh=mesh,
        in_specs=(
            P(("dp", "tp"), None),
            P(("dp", "tp"), None),
            P("dp"),
            P(None, None, None, "tp"),
            P(None, None, "tp"),
            P(None, "tp", None),
            P(),
            P(None, None, "tp"),
            P(None, "tp"),
            P(None, "tp", None),
            P(),
            P(),
            P(),
        ),
        out_specs=(
            P(("dp", "tp"), None),
            P(("dp", "tp"), None),
            P(None, None, None, "tp"),
            P(None, None, "tp"),
            P(None, "tp", None),
            P(),
            P(None, None, "tp"),
            P(None, "tp"),
            P(None, "tp", None),
            P(),
            P(),
            P(),
        ),
        check_vma=False,
    )
```

```python
import functools

import jax
import jax.numpy as jnp
from jax import lax
from jax.experimental import pallas as pl
from jax.experimental.pallas import tpu as pltpu
from jax.sharding import PartitionSpec as P

HD = 64
SEQ_LEN = 512
NORM_EPSILON = 1e-06
F32 = jnp.float32
BF16 = jnp.bfloat16


def bits_of(count):
    return [1 << place for place in range(count.bit_length() - 1)]


def swap(value, axis, bit):
    count = lax.axis_size(axis)
    return lax.ppermute(value, axis, [(item, item ^ bit) for item in range(count)])


def block_order(count):
    order = [0]
    for bit in reversed(bits_of(count)):
        order = order + [item ^ bit for item in order]
    return order


def gather_rows(rows):
    block = rows
    for bit in reversed(bits_of(lax.axis_size("tp"))):
        block = jnp.concatenate([block, swap(block, "tp", bit)], axis=0)
    return block


def scatter_rows(partial):
    for bit in bits_of(lax.axis_size("tp")):
        half = partial.shape[0] // 2
        arrived = swap(partial[half:].astype(BF16), "tp", bit)
        partial = partial[:half] + arrived.astype(F32)
    return partial


def squash(value, limit):
    return limit * jnp.tanh(value / limit)


def squash_slope(value, limit):
    level_value = jnp.tanh(value / limit)
    return 1.0 - level_value * level_value


def norm_parts(values):
    centre = jnp.mean(values, axis=-1, keepdims=True)
    centred = values - centre
    spread = jnp.mean(centred * centred, axis=-1, keepdims=True)
    scale = lax.rsqrt(spread + NORM_EPSILON)
    return centred * scale, scale


def norm_back(gradient, unit, scale, gain):
    scaled = gradient * gain
    first = jnp.mean(scaled, axis=-1, keepdims=True)
    second = jnp.mean(scaled * unit, axis=-1, keepdims=True)
    d_values = scale * (scaled - first - unit * second)
    return d_values, jnp.sum(gradient * unit, axis=0), jnp.sum(gradient, axis=0)


def mm(first, second):
    return jnp.dot(first, second, preferred_element_type=F32)


def mm_t(first, second):
    return lax.dot_general(first, second, (((1,), (1,)), ((), ())), preferred_element_type=F32)


def t_mm(first, second):
    return lax.dot_general(first, second, (((0,), (0,)), ((), ())), preferred_element_type=F32)


def reduce_weight(left, right, raw, top, order):
    place = lax.axis_index("dp")
    rows = left.shape[1]
    start = 0
    bit = order[0]
    mine = (place // bit) % 2
    half = rows // 2
    send = t_mm(lax.dynamic_slice_in_dim(left, (1 - mine) * half, half, 1), right).astype(BF16)
    arrived = swap(send, "dp", bit)
    total = t_mm(lax.dynamic_slice_in_dim(left, mine * half, half, 1), right)
    total = total + arrived.astype(F32)
    start = mine * half
    for bit in order[1:]:
        mine = (place // bit) % 2
        half = half // 2
        send = lax.dynamic_slice_in_dim(total, (1 - mine) * half, half, 0).astype(BF16)
        arrived = swap(send, "dp", bit)
        total = lax.dynamic_slice_in_dim(total, mine * half, half, 0) + arrived.astype(F32)
        start = start + mine * half
    raw_piece = lax.dynamic_slice_in_dim(raw, start, half, 0).astype(F32)
    piece = (total * squash_slope(raw_piece, top)).astype(BF16)
    for bit in reversed(order):
        mine = (place // bit) % 2
        arrived = swap(piece, "dp", bit)
        low_half = jnp.where(mine == 0, piece, arrived)
        high_half = jnp.where(mine == 0, arrived, piece)
        piece = jnp.concatenate([low_half, high_half], axis=0)
    return piece.astype(F32)


def on_device(
    tokens,
    cotangent,
    lengths,
    qkv_weight,
    qv_bias,
    out_weight,
    out_bias,
    up_weight,
    up_bias,
    down_weight,
    down_bias,
    norm_params,
    act_ranges,
):
    row_count, width = tokens.shape
    tp_count = lax.axis_size("tp")
    dp_count = lax.axis_size("dp")
    rank = lax.axis_index("tp")
    all_rows = row_count * tp_count
    assert lengths.shape[0] == 1 and all_rows == SEQ_LEN
    layer_count = qkv_weight.shape[0]
    local_width = qkv_weight.shape[3]
    local_units = up_weight.shape[2]
    heads_here = local_width // HD
    score_scale = HD ** (-0.5)
    order = jnp.array(block_order(tp_count), jnp.int32)
    places = ((rank ^ order)[:, None] * row_count + jnp.arange(row_count)[None, :]).reshape(all_rows)
    inside = places < lengths[0]
    valid_all = inside.astype(F32)[:, None]
    valid_rows = valid_all[:row_count]
    key_bias = jnp.where(inside, 0.0, -1000000000.0).astype(F32)
    qkv_blocks = jnp.transpose(qkv_weight, (0, 2, 1, 3))
    local_tops = jnp.stack(
        [
            jnp.stack(
                [
                    jnp.max(jnp.abs(qkv_blocks[level])),
                    jnp.max(jnp.abs(out_weight[level])),
                    jnp.max(jnp.abs(up_weight[level])),
                    jnp.max(jnp.abs(down_weight[level])),
                ]
            )
            for level in range(layer_count)
        ]
    ).astype(F32)
    weight_tops = local_tops
    for bit in bits_of(tp_count):
        weight_tops = jnp.maximum(weight_tops, swap(weight_tops, "tp", bit))

    def scores_of(queries, key_rows):
        raw = jnp.einsum("qhd,khd->hqk", queries, key_rows, preferred_element_type=F32)
        return raw * score_scale + key_bias[None, None, :]

    stored = []
    peak_list = []
    current = tokens.astype(F32)
    for level in range(layer_count):
        limits = act_ranges[level]
        tops = weight_tops[level]
        w_qkv = squash(qkv_blocks[level].astype(F32), tops[0]).astype(BF16)
        w_out = squash(out_weight[level].astype(F32), tops[1]).astype(BF16)
        w_up = squash(up_weight[level].astype(F32), tops[2]).astype(BF16)
        w_down = squash(down_weight[level].astype(F32), tops[3]).astype(BF16)
        x_low_all = gather_rows(squash(current, limits[0]).astype(BF16))
        heads = (all_rows, heads_here, HD)
        queries = (mm(x_low_all, w_qkv[0]) + qv_bias[level, 0].astype(F32)).astype(BF16).reshape(heads)
        key_rows = mm(x_low_all, w_qkv[1]).astype(BF16).reshape(heads)
        value_rows = (mm(x_low_all, w_qkv[2]) + qv_bias[level, 1].astype(F32)).astype(BF16).reshape(heads)
        scores = scores_of(queries, key_rows)
        peak_score = jnp.max(scores, axis=-1, keepdims=True)
        log_total = peak_score + jnp.log(jnp.sum(jnp.exp(scores - peak_score), axis=-1, keepdims=True))
        attn_probs = jnp.exp(scores - log_total).astype(BF16)
        context = jnp.einsum("hqk,khd->qhd", attn_probs, value_rows, preferred_element_type=F32)
        context = context.reshape(all_rows, local_width)
        ctx_low = squash(context, limits[1]).astype(BF16)
        attn_rows = scatter_rows(mm(ctx_low, w_out))
        mid_unit, mid_scale = norm_parts(current + attn_rows + out_bias[level].astype(F32))
        hidden = mid_unit * norm_params[level, 0] + norm_params[level, 1]
        hid_low_all = gather_rows(squash(hidden, limits[2]).astype(BF16))
        up_value = mm(hid_low_all, w_up) + up_bias[level].astype(F32)
        normal_cdf = 0.5 + 0.5 * lax.erf(up_value * (0.5**0.5))
        active = up_value * normal_cdf
        act_level = jnp.tanh(active / limits[3])
        act_low = (limits[3] * act_level).astype(BF16)
        gelu_slope = normal_cdf + up_value * jnp.exp(-0.5 * up_value * up_value) * 0.3989422804014327
        up_slope = (1.0 - act_level * act_level) * gelu_slope
        down_rows = scatter_rows(mm(act_low, w_down))
        out_unit, out_scale = norm_parts(hidden + down_rows + down_bias[level].astype(F32))
        peak_list.append(
            jnp.stack(
                [
                    jnp.max(jnp.abs(current) * valid_rows),
                    jnp.max(jnp.abs(context) * valid_all),
                    jnp.max(jnp.abs(hidden) * valid_rows),
                    jnp.max(jnp.abs(active) * valid_all),
                ]
            )
        )
        stored.append(
            (
                current, mid_unit, mid_scale, hidden, out_unit, out_scale, x_low_all, queries, key_rows, value_rows,
                log_total, context, ctx_low, hid_low_all, up_slope, act_low, w_qkv, w_out, w_up, w_down,
            )
        )
        current = out_unit * norm_params[level, 2] + norm_params[level, 3]
    output = current.astype(BF16)
    gradient = cotangent.astype(F32) * valid_rows

    dp_bits = bits_of(dp_count)
    big_list = [None] * layer_count
    rep_list = [None] * layer_count
    shard_list = [None] * layer_count
    for level in reversed(range(layer_count)):
        (
            inputs, mid_unit, mid_scale, hidden, out_unit, out_scale, x_low_all, queries, key_rows, value_rows,
            log_total, context, ctx_low, hid_low_all, up_slope, act_low, w_qkv, w_out, w_up, w_down,
        ) = stored[level]
        limits = act_ranges[level]
        tops = weight_tops[level]
        d_final, d_gain_out, d_shift_out = norm_back(gradient, out_unit, out_scale, norm_params[level, 2])
        down_grad = d_final.astype(BF16)
        d_down_bias = jnp.sum(down_grad.astype(F32), axis=0)
        down_grad_all = gather_rows(down_grad)
        up_grad = (mm_t(down_grad_all, w_down) * up_slope).astype(BF16)
        g_down = reduce_weight(act_low, down_grad_all, down_weight[level], tops[3], dp_bits)
        d_up_bias = jnp.sum(up_grad.astype(F32), axis=0)
        d_hid_rows = scatter_rows(mm_t(up_grad, w_up))
        g_up = reduce_weight(hid_low_all, up_grad, up_weight[level], tops[2], dp_bits)
        d_hidden = d_final + d_hid_rows * squash_slope(hidden, limits[2])
        d_mid, d_gain_mid, d_shift_mid = norm_back(d_hidden, mid_unit, mid_scale, norm_params[level, 0])
        out_grad = d_mid.astype(BF16)
        d_out_bias = jnp.sum(out_grad.astype(F32), axis=0)
        out_grad_all = gather_rows(out_grad)
        ctx_grad = (mm_t(out_grad_all, w_out) * squash_slope(context, limits[1])).astype(BF16)
        g_out = reduce_weight(ctx_low, out_grad_all, out_weight[level], tops[1], dp_bits)
        ctx_grad = ctx_grad.reshape(heads)
        soft_probs = jnp.exp(scores_of(queries, key_rows) - log_total)
        soft_low = soft_probs.astype(BF16)
        d_values = jnp.einsum("hqk,qhd->khd", soft_low, ctx_grad, preferred_element_type=F32)
        d_probs = jnp.einsum("qhd,khd->hqk", ctx_grad, value_rows, preferred_element_type=F32)
        d_scores = (
            soft_probs * (d_probs - jnp.sum(soft_probs * d_probs, axis=-1, keepdims=True))
        ).astype(BF16)
        d_queries = jnp.einsum("hqk,khd->qhd", d_scores, key_rows, preferred_element_type=F32) * score_scale
        d_keys = jnp.einsum("hqk,qhd->khd", d_scores, queries, preferred_element_type=F32) * score_scale
        parts = [
            item.astype(BF16).reshape(all_rows, local_width) for item in (d_queries, d_keys, d_values)
        ]
        d_x_rows = scatter_rows(
            mm_t(parts[0], w_qkv[0]) + mm_t(parts[1], w_qkv[1]) + mm_t(parts[2], w_qkv[2])
        )
        g_qkv = reduce_weight(
            x_low_all,
            jnp.concatenate(parts, axis=1),
            jnp.transpose(qkv_blocks[level], (1, 0, 2)).reshape(width, 3 * local_width),
            tops[0],
            dp_bits,
        ).reshape(width, 3, local_width)
        d_qv_bias = jnp.stack([jnp.sum(parts[0].astype(F32), axis=0), jnp.sum(parts[2].astype(F32), axis=0)])
        gradient = d_mid + d_x_rows * squash_slope(inputs, limits[0])
        big_list[level] = (g_qkv, g_out, g_up, g_down)
        rep_list[level] = jnp.stack([d_out_bias, d_down_bias, d_gain_mid, d_shift_mid, d_gain_out, d_shift_out])
        shard_list[level] = (d_qv_bias, d_up_bias)

    rep = jnp.stack(rep_list)
    peaks = jnp.stack(peak_list)
    for bit in bits_of(tp_count):
        rep = rep + swap(rep, "tp", bit)
        peaks = jnp.maximum(peaks, swap(peaks, "tp", bit))
    qv_sum = jnp.stack([item[0] for item in shard_list])
    up_sum = jnp.stack([item[1] for item in shard_list])
    sizes = [rep.size, qv_sum.size, up_sum.size]
    pack = jnp.concatenate([rep.reshape(-1), qv_sum.reshape(-1), up_sum.reshape(-1)])
    for bit in dp_bits:
        pack = pack + swap(pack, "dp", bit)
        peaks = jnp.maximum(peaks, swap(peaks, "dp", bit))
    rep = pack[: sizes[0]].reshape(rep.shape)
    qv_sum = pack[sizes[0] : sizes[0] + sizes[1]].reshape(qv_sum.shape)
    up_sum = pack[sizes[0] + sizes[1] :].reshape(up_sum.shape)
    grads = [jnp.stack([entry[item] for entry in big_list]) for item in range(4)]
    return (
        output,
        gradient,
        grads[0],
        qv_sum,
        grads[1],
        rep[:, 0],
        grads[2],
        up_sum,
        grads[3],
        rep[:, 1],
        rep[:, 2:],
        peaks,
    )


ERF_TOP = (
    -2.72614225801306e-10, 2.77068142495902e-08, -2.10102402082508e-06, -5.69250639462346e-05,
    -7.34990630326855e-04, -2.95459980854025e-03, -1.60960333262415e-02,
)
ERF_LOW = (
    -1.45660718464996e-05, -2.13374055278905e-04, -1.68282697438203e-03, -7.37332916720468e-03,
    -1.42647390514189e-02,
)


def erf_ratio(value):
    value = jnp.clip(value, -4.0, 4.0)
    square = value * value
    top = ERF_TOP[0]
    for factor in ERF_TOP[1:]:
        top = top * square + factor
    low = ERF_LOW[0]
    for factor in ERF_LOW[1:]:
        low = low * square + factor
    return value * top / low


def whole(shape):
    return pl.BlockSpec(shape, lambda *_: (0,) * len(shape))


SMEM = pl.BlockSpec(memory_space=pltpu.SMEM)


def cost(*_):
    return pl.CostEstimate(flops=1, bytes_accessed=1, transcendentals=0)


def params(mib=56):
    return pltpu.CompilerParams(vmem_limit_bytes=mib << 20)


def shaped(shape, dtype):
    return jax.ShapeDtypeStruct(shape, dtype)


class Line:
    mark = None
    free = False


def launch(
    kernel, *, out_shape, in_specs=(), out_specs=(), grid=None, grid_spec=None, scratch_shapes=(),
    input_output_aliases=None, compiler_params=None, cost_estimate=None, far_ins=(), far_outs=(),
):
    single = not isinstance(out_shape, (list, tuple))
    outs = [out_shape] if single else list(out_shape)
    if grid_spec is None:
        scalars, scratch = 0, list(scratch_shapes)
        ins_list, outs_list = list(in_specs), [out_specs] if single else list(out_specs)
    else:
        scalars, grid, scratch = grid_spec.num_scalar_prefetch, grid_spec.grid, list(grid_spec.scratch_shapes)
        ins_list, outs_list = list(grid_spec.in_specs), list(grid_spec.out_specs)

    def called(*args):
        marks = [] if Line.mark is None else [Line.mark]
        args = [
            pltpu.with_memory_space_constraint(item, pltpu.HBM) if place - scalars in far_ins else item
            for place, item in enumerate(args)
        ]
        first = scalars + len(ins_list)

        def body(*refs):
            refs = list(refs)
            del refs[first : first + len(marks)]
            del refs[first + len(outs)]
            kernel(*refs)

        anywhere = pl.BlockSpec(memory_space=pl.ANY)
        spec = pltpu.PrefetchScalarGridSpec(
            num_scalar_prefetch=scalars,
            grid=grid,
            in_specs=ins_list + [anywhere] * len(marks),
            out_specs=outs_list + [anywhere],
            scratch_shapes=scratch,
        )
        results = pl.pallas_call(
            body,
            out_shape=[
                pltpu.HBM(item.shape, item.dtype) if place in far_outs else item for place, item in enumerate(outs)
            ]
            + [shaped((8, 128), F32)],
            grid_spec=spec,
            input_output_aliases=input_output_aliases or {},
            compiler_params=compiler_params,
            cost_estimate=cost_estimate,
        )(*args, *marks)
        if not Line.free:
            Line.mark = results[-1]
        return results[0] if single else list(results[:-1])

    return called


def tops_kernel(count, *refs):
    weights, out_ref, scratch = refs[:count], refs[count], refs[count + 1 :]
    step = pl.program_id(0)
    for item in range(count):
        block = jnp.abs(weights[item][...])
        part = jnp.max(block.reshape(-1, 16, block.shape[-1]), axis=0)

        @pl.when(step == 0)
        def _():
            scratch[item][...] = part

        @pl.when(step > 0)
        def _():
            scratch[item][...] = jnp.maximum(scratch[item][...], part)

    @pl.when(step == pl.num_programs(0) - 1)
    def _():
        for item in range(count):
            top = jnp.max(scratch[item][...].astype(F32), axis=0, keepdims=True)
            top = jnp.max(top, axis=1, keepdims=True)
            out_ref[item : item + 1, :] = jnp.broadcast_to(top, (1, 128))


def row_specs(level, weights, steps, layered):
    specs = []
    for weight in weights:
        rows = weight.shape[-2] // steps
        if weight.ndim == 4 and layered:
            specs.append(pl.BlockSpec((1, weight.shape[1], rows, weight.shape[3]), lambda s: (level, 0, s, 0)))
        elif weight.ndim == 4:
            specs.append(pl.BlockSpec((weight.shape[1], rows, weight.shape[3]), lambda s: (0, s, 0)))
        elif layered:
            specs.append(pl.BlockSpec((1, rows, weight.shape[2]), lambda s: (level, s, 0)))
        else:
            specs.append(pl.BlockSpec((rows, weight.shape[2]), lambda s: (s, 0)))
    return specs


def weight_tops_of(level, weights):
    steps = 2
    return launch(
        functools.partial(tops_kernel, len(weights)),
        out_shape=shaped((len(weights), 128), F32),
        grid=(steps,),
        in_specs=row_specs(level, weights, steps, True),
        out_specs=whole((len(weights), 128)),
        scratch_shapes=[pltpu.VMEM((16, weight.shape[-1]), BF16) for weight in weights],
        compiler_params=params(24),
        cost_estimate=cost(),
        far_ins=range(len(weights)),
    )(*weights)


def top_of(tops, item):
    top = tops[0][item : item + 1, 0:1]
    for ref in tops[1:]:
        top = jnp.maximum(top, ref[item : item + 1, 0:1])
    return top


def squash_kernel(count, first, t0, t1, t2, t3, *refs):
    for item in range(count):
        top = top_of((t0, t1, t2, t3), first + item)
        value = refs[item][0].astype(F32)
        refs[count + item][...] = (top * jnp.tanh(value * (1.0 / top))).astype(BF16)


def squash_weights(level, tops, first, weights):
    steps = 2
    return launch(
        functools.partial(squash_kernel, len(weights), first),
        out_shape=[shaped(weight.shape[1:], BF16) for weight in weights],
        grid=(steps,),
        in_specs=[whole(tops[0].shape)] * 4 + row_specs(level, weights, steps, True),
        out_specs=row_specs(level, weights, steps, False),
        compiler_params=params(24),
        cost_estimate=cost(),
        far_ins=range(4, 8),
    )(*tops, *weights)


def slope_kernel(sets, rows_of, place_ref, *refs):
    tops, (qkv_ref, out_ref, up_ref, down_ref), targets = refs[: 4 * sets], refs[4 * sets : 4 * sets + 4], refs[-3:]

    def slope(value, item):
        group, row = rows_of[item]
        tanh = jnp.tanh(value.astype(F32) * (1.0 / top_of(tops[4 * group : 4 * group + 4], row)))
        return 1.0 - tanh * tanh

    targets[0][...] = slope(down_ref[0], 3)
    targets[1][...] = slope(up_ref[0], 2)
    local = qkv_ref.shape[3]
    for part in range(3):
        targets[2][:, part * local : (part + 1) * local] = slope(qkv_ref[0, part], 0)
    piece = slope(out_ref[0], 1)
    span = piece.shape[0]
    rows = targets[2].shape[0]
    side = piece.shape[1] * span // rows
    for item in range(rows // span):
        targets[2][item * span : (item + 1) * span, 3 * local :] = piece[:, item * side : (item + 1) * side]


def slope_pieces(level, place, tops, rows_of, weights):
    specs = []
    for weight in weights:
        rows = weight.shape[-2] // 8
        if weight.ndim == 4:
            specs.append(pl.BlockSpec((1, weight.shape[1], rows, weight.shape[3]), lambda s, p: (level, 0, p[0], 0)))
        else:
            specs.append(pl.BlockSpec((1, rows, weight.shape[2]), lambda s, p: (level, p[0], 0)))
    width = weights[2].shape[1]
    rows = width // 8
    outs = [shaped((rows, width), F32)] * 3
    return launch(
        functools.partial(slope_kernel, len(tops), rows_of),
        out_shape=outs,
        grid_spec=pltpu.PrefetchScalarGridSpec(
            num_scalar_prefetch=1,
            grid=(1,),
            in_specs=[whole(item.shape) for group in tops for item in group] + specs,
            out_specs=[whole(item.shape) for item in outs],
        ),
        compiler_params=params(12),
        cost_estimate=cost(0, 3 << 20, 1 << 19),
        far_ins=range(4 * len(tops), 4 * len(tops) + 4), far_outs=range(3),
    )(place, *[item for group in tops for item in group], *weights)


def valid_of(info_ref, rows, blocks):
    row = lax.broadcasted_iota(jnp.int32, (rows, 1), 0)
    columns = [(row + info_ref[block] < info_ref[4]).astype(F32) for block in blocks]
    return columns[0] if len(columns) == 1 else jnp.concatenate(columns, axis=0)


def key_bias_of(info_ref, rows):
    lane = lax.broadcasted_iota(jnp.int32, (1, rows), 1)
    return jnp.concatenate(
        [jnp.where(lane + info_ref[block] < info_ref[4], 0.0, -1000000000.0) for block in range(4)], axis=1
    )


def attn_forward_kernel(level, info_ref, limits_ref, x0, x1, x2, x3, w_ref, bias_ref, out_w_ref,
                        qkv_ref, ctx_ref, low_ref, peak_ref, send_ref, keep_ref, x_ref):
    rows = x0.shape[0]
    for place, piece in enumerate((x0, x1, x2, x3)):
        x_ref[place * rows : (place + 1) * rows, :] = piece[...]
    x = x_ref[...]
    for part in range(3):
        total = mm(x, w_ref[part])
        if part != 1:
            total = total + bias_ref[level, part // 2 : part // 2 + 1, :].astype(F32)
        qkv_ref[part] = total.astype(BF16)
    limit = limits_ref[level, 1]
    key_bias = key_bias_of(info_ref, rows)
    inverse = 1.0 / limit

    def heads(two, carry):
        lanes = pl.ds(pl.multiple_of(two * 2 * HD, 2 * HD), 2 * HD)
        queries, keys, values = qkv_ref[0, :, lanes], qkv_ref[1, :, lanes], qkv_ref[2, :, lanes]
        both = []
        for here in (slice(0, HD), slice(HD, 2 * HD)):
            scores = mm_t(queries[:, here], keys[:, here]) * (HD**-0.5) + key_bias
            scores = jnp.exp(scores - jnp.max(scores, axis=-1, keepdims=True))
            probs = (scores * (1.0 / jnp.sum(scores, axis=-1, keepdims=True))).astype(BF16)
            both.append(mm(probs, values[:, here]))
        ctx_ref[:, lanes] = jnp.concatenate(both, axis=1)
        return carry

    lax.fori_loop(0, qkv_ref.shape[2] // (2 * HD), heads, 0, unroll=True)
    context = ctx_ref[...]
    peak_ref[...] = jnp.max(jnp.abs(context) * valid_of(info_ref, rows, (0, 1, 2, 3)), axis=0, keepdims=True)
    low = (limit * jnp.tanh(context * inverse)).astype(BF16)
    low_ref[...] = low
    half = low.shape[0] // 2
    send_ref[...] = mm(low[half:], out_w_ref[...]).astype(BF16)
    keep_ref[...] = mm(low[:half], out_w_ref[...])


def attn_forward(level, info, limits, pieces, w_qkv, bias, w_out):
    rows, width = pieces[0].shape
    total = 4 * rows
    local = w_out.shape[0]
    ins = (info, limits, *pieces, w_qkv, bias, w_out)
    outs = [
        shaped((3, total, local), BF16),
        shaped((total, local), F32),
        shaped((total, local), BF16),
        shaped((1, local), F32),
        shaped((total // 2, width), BF16),
        shaped((total // 2, width), F32),
    ]
    return launch(
        functools.partial(attn_forward_kernel, level),
        out_shape=outs,
        in_specs=[SMEM, SMEM] + [whole(item.shape) for item in ins[2:]],
        out_specs=[whole(item.shape) for item in outs],
        scratch_shapes=[pltpu.VMEM((total, width), BF16)],
        grid=(1,),
        compiler_params=params(28),
        cost_estimate=cost(5e9, 8 << 20, 1 << 20),
        far_outs=(0, 1, 2),
    )(*ins)


def two_pieces(step, pieces, both_ref):
    rows = pieces[0].shape[0]
    for half in range(2):

        @pl.when(step == half)
        def _():
            both_ref[:rows] = pieces[2 * half][...]
            both_ref[rows:] = pieces[2 * half + 1][...]


def ffn_forward_kernel(level, info_ref, limits_ref, x0, x1, x2, x3, up_w_ref, bias_ref, down_w_ref,
                       low_ref, slope_ref, peak_ref, send_ref, keep_ref, both_ref, up_ref):
    step = pl.program_id(0)
    limit = limits_ref[level, 3]
    inverse = 1.0 / limit
    two_pieces(step, (x0, x1, x2, x3), both_ref)
    up_ref[...] = mm(both_ref[...], up_w_ref[...]) + bias_ref[level : level + 1, :].astype(F32)
    chunk = 64
    rows = x0.shape[0]

    def part(item, peak):
        here = pl.ds(pl.multiple_of(item * chunk, chunk), chunk)
        up = up_ref[here, :]
        cdf = 0.5 + 0.5 * erf_ratio(up * (0.5**0.5))
        active = up * cdf
        tanh = jnp.tanh(active * inverse)
        low_ref[here, :] = (limit * tanh).astype(BF16)
        slope_ref[here, :] = (1.0 - tanh * tanh) * (cdf + up * jnp.exp(-0.5 * up * up) * 0.3989422804014327)
        place = lax.broadcasted_iota(jnp.int32, (chunk, 1), 0) + item * chunk % rows
        inside = place + info_ref[2 * step + item * chunk // rows] < info_ref[4]
        size = jnp.where(inside, jnp.abs(active), 0.0)
        return jnp.maximum(peak, jnp.max(size.reshape(-1, 8, size.shape[1]), axis=0))

    peak = lax.fori_loop(0, 2 * rows // chunk, part, jnp.zeros((8, up_ref.shape[1]), F32))
    peak = jnp.max(peak, axis=0, keepdims=True)
    peak_ref[...] = jnp.where(step == 0, peak, jnp.maximum(peak_ref[...], peak))
    total = mm(low_ref[...], down_w_ref[...])

    @pl.when(step == 0)
    def _():
        keep_ref[...] = total

    @pl.when(step == 1)
    def _():
        send_ref[...] = total.astype(BF16)


def ffn_forward(level, info, limits, pieces, w_up, bias, w_down):
    rows, width = pieces[0].shape
    units = w_up.shape[1]
    total = 4 * rows
    outs = [
        shaped((total, units), BF16),
        shaped((total, units), F32),
        shaped((1, units), F32),
        shaped((total // 2, width), BF16),
        shaped((total // 2, width), F32),
    ]
    return launch(
        functools.partial(ffn_forward_kernel, level),
        out_shape=outs,
        grid=(2,),
        in_specs=[SMEM, SMEM]
        + [whole((rows, width))] * 4
        + [whole(w_up.shape), whole(bias.shape), whole(w_down.shape)],
        out_specs=[
            pl.BlockSpec((2 * rows, units), lambda s: (s, 0)),
            pl.BlockSpec((2 * rows, units), lambda s: (s, 0)),
            whole((1, units)),
            whole((2 * rows, width)),
            whole((2 * rows, width)),
        ],
        scratch_shapes=[pltpu.VMEM((2 * rows, width), BF16), pltpu.VMEM((2 * rows, units), F32)],
        compiler_params=params(32),
        cost_estimate=cost(8e9, 12 << 20, 2 << 20),
        far_outs=(0, 1),
    )(info, limits, *pieces, w_up, bias, w_down)


def enter_kernel(info_ref, limits_ref, tokens_ref, low_ref, peak_ref):
    value = tokens_ref[...].astype(F32)
    limit = limits_ref[0, 0]
    low_ref[...] = (limit * jnp.tanh(value * (1.0 / limit))).astype(BF16)
    peak_ref[...] = jnp.max(jnp.abs(value) * valid_of(info_ref, value.shape[0], (0,)), axis=0, keepdims=True)


def enter(info, limits, tokens):
    outs = [shaped(tokens.shape, BF16), shaped((1, tokens.shape[1]), F32)]
    return launch(
        enter_kernel,
        out_shape=outs,
        grid=(1,),
        in_specs=[SMEM, SMEM, whole(tokens.shape)],
        out_specs=[whole(item.shape) for item in outs],
        compiler_params=params(8),
        cost_estimate=cost(),
    )(info, limits, tokens)


def join_kernel(level, item, last, info_ref, limits_ref, base_ref, keep_ref, core_ref, far_ref, bias_ref, norm_ref,
                *outs):
    arrived = keep_ref[...] + core_ref[...].astype(F32) + far_ref[...].astype(F32)
    unit, scale = norm_parts(base_ref[...].astype(F32) + arrived + bias_ref[level : level + 1, :].astype(F32))
    value = unit * norm_ref[level, item : item + 1, :] + norm_ref[level, item + 1 : item + 2, :]
    outs[0][...] = unit
    outs[1][...] = scale
    if last:
        outs[2][...] = value.astype(BF16)
    else:
        outs[2][...] = value
        limit = limits_ref[level, 2] if item == 0 else limits_ref[level + 1, 0]
        outs[3][...] = (limit * jnp.tanh(value * (1.0 / limit))).astype(BF16)
        peak = jnp.abs(value) * valid_of(info_ref, value.shape[0], (0,))
        outs[4][...] = jnp.max(peak, axis=0, keepdims=True)


def join_rows(level, item, last, info, limits, base, keep, core, far, bias, norm):
    rows, width = base.shape
    outs = [shaped((rows, width), F32), shaped((rows, 1), F32)]
    if last:
        outs += [shaped((rows, width), BF16)]
    else:
        outs += [shaped((rows, width), F32), shaped((rows, width), BF16), shaped((1, width), F32)]
    block = whole((rows, width))
    return launch(
        functools.partial(join_kernel, level, item, last),
        out_shape=outs,
        grid=(1,),
        in_specs=[SMEM, SMEM, block, block, block, block, whole(bias.shape), whole(norm.shape)],
        out_specs=[whole(item.shape) for item in outs],
        compiler_params=params(12),
        cost_estimate=cost(),
        far_outs=(),
    )(info, limits, base, keep, core, far, bias, norm)


def norm_back_store(gradient, unit_ref, scale_ref, gain, d_ref, low_ref, sums_ref):
    unit = unit_ref[...]
    scaled = gradient * gain
    first = jnp.mean(scaled, axis=-1, keepdims=True)
    second = jnp.mean(scaled * unit, axis=-1, keepdims=True)
    d_values = scale_ref[...] * (scaled - first - unit * second)
    low = d_values.astype(BF16)
    d_ref[...] = d_values
    low_ref[...] = low
    sums_ref[0:1, :] = jnp.sum(low.astype(F32), axis=0, keepdims=True)
    sums_ref[1:2, :] = jnp.sum(gradient * unit, axis=0, keepdims=True)
    sums_ref[2:3, :] = jnp.sum(gradient, axis=0, keepdims=True)


def top_back_kernel(level, info_ref, cot_ref, unit_ref, scale_ref, norm_ref, d_ref, low_ref, sums_ref):
    gradient = cot_ref[...].astype(F32) * valid_of(info_ref, cot_ref.shape[0], (0,))
    norm_back_store(gradient, unit_ref, scale_ref, norm_ref[level, 2:3, :], d_ref, low_ref, sums_ref)


def mid_back_kernel(level, item, limits_ref, base_ref, keep_ref, core_ref, far_ref, unit_ref, scale_ref, norm_ref,
                    d_ref, low_ref, sums_ref):
    arrived = keep_ref[...] + core_ref[...].astype(F32) + far_ref[...].astype(F32)
    gain = norm_ref[level, item : item + 1, :]
    value = unit_ref[...] * gain + norm_ref[level, item + 1 : item + 2, :]
    limit = limits_ref[level, 2] if item == 0 else limits_ref[level + 1, 0]
    tanh = jnp.tanh(value * (1.0 / limit))
    gradient = base_ref[...] + arrived * (1.0 - tanh * tanh)
    norm_back_store(gradient, unit_ref, scale_ref, gain, d_ref, low_ref, sums_ref)


def end_back_kernel(limits_ref, base_ref, keep_ref, core_ref, far_ref, x_ref, out_ref):
    arrived = keep_ref[...] + core_ref[...].astype(F32) + far_ref[...].astype(F32)
    tanh = jnp.tanh(x_ref[...].astype(F32) * (1.0 / limits_ref[0, 0]))
    out_ref[...] = base_ref[...] + arrived * (1.0 - tanh * tanh)


def top_back(level, info, cotangent, unit, scale, norm):
    rows, width = unit.shape
    outs = [shaped((rows, width), F32), shaped((rows, width), BF16), shaped((3, width), F32)]
    ins = (cotangent, unit, scale, norm)
    return launch(
        functools.partial(top_back_kernel, level),
        out_shape=outs,
        grid=(1,),
        in_specs=[SMEM] + [whole(item.shape) for item in ins],
        out_specs=[whole(item.shape) for item in outs],
        compiler_params=params(12),
        cost_estimate=cost(),
        far_ins=(1, 2, 3),
    )(info, *ins)


def mid_back(level, item, limits, base, keep, core, far, unit, scale, norm):
    rows, width = unit.shape
    outs = [shaped((rows, width), F32), shaped((rows, width), BF16), shaped((3, width), F32)]
    block = whole((rows, width))
    return launch(
        functools.partial(mid_back_kernel, level, item),
        out_shape=outs,
        grid=(1,),
        in_specs=[SMEM, block, block, block, block, block, whole(scale.shape), whole(norm.shape)],
        out_specs=[whole(item.shape) for item in outs],
        compiler_params=params(12),
        cost_estimate=cost(),
        far_ins=(), far_outs=(),
    )(limits, base, keep, core, far, unit, scale, norm)


def end_back(limits, base, keep, core, far, x):
    block = whole(base.shape)
    return launch(
        end_back_kernel,
        out_shape=shaped(base.shape, F32),
        grid=(1,),
        in_specs=[SMEM] + [block] * 5,
        out_specs=block,
        compiler_params=params(12),
        cost_estimate=cost(),
    )(limits, base, keep, core, far, x)


def ffn_backward_kernel(g0, g1, g2, g3, down_w_ref, slope_ref, up_w_ref, grad_ref, sum_ref, send_ref, keep_ref,
                        both_ref):
    step = pl.program_id(0)
    two_pieces(step, (g0, g1, g2, g3), both_ref)
    grad = (mm_t(both_ref[...], down_w_ref[...]) * slope_ref[...]).astype(BF16)
    grad_ref[...] = grad
    part = jnp.sum(grad.astype(F32), axis=0, keepdims=True)
    sum_ref[...] = jnp.where(step == 0, part, sum_ref[...] + part)
    total = mm_t(grad, up_w_ref[...])

    @pl.when(step == 0)
    def _():
        keep_ref[...] = total

    @pl.when(step == 1)
    def _():
        send_ref[...] = total.astype(BF16)


def ffn_backward(pieces, w_down, slope, w_up):
    rows, width = pieces[0].shape
    units = w_up.shape[1]
    total = 4 * rows
    outs = [
        shaped((total, units), BF16),
        shaped((1, units), F32),
        shaped((total // 2, width), BF16),
        shaped((total // 2, width), F32),
    ]
    return launch(
        ffn_backward_kernel,
        out_shape=outs,
        grid=(2,),
        in_specs=[whole((rows, width))] * 4
        + [whole(w_down.shape), pl.BlockSpec((2 * rows, units), lambda s: (s, 0)), whole(w_up.shape)],
        out_specs=[
            pl.BlockSpec((2 * rows, units), lambda s: (s, 0)),
            whole((1, units)),
            whole((2 * rows, width)),
            whole((2 * rows, width)),
        ],
        scratch_shapes=[pltpu.VMEM((2 * rows, width), BF16)],
        compiler_params=params(32),
        cost_estimate=cost(3e9, 12 << 20),
        far_ins=(4, 5, 6),
    )(*pieces, w_down, slope, w_up)


def attn_backward_kernel(level, info_ref, limits_ref, g0, g1, g2, g3, out_w_ref, ctx_ref, qkv_ref, w_ref,
                         grad_ref, sum_ref, send_ref, keep_ref, g_ref, cg_ref):
    rows = g0.shape[0]
    for place, piece in enumerate((g0, g1, g2, g3)):
        g_ref[place * rows : (place + 1) * rows, :] = piece[...]
    tanh = jnp.tanh(ctx_ref[...] * (1.0 / limits_ref[level, 1]))
    cg_ref[...] = (mm_t(g_ref[...], out_w_ref[...]) * (1.0 - tanh * tanh)).astype(BF16)
    key_bias = key_bias_of(info_ref, rows)
    local = cg_ref.shape[1]

    def heads(two, carry):
        start = pl.multiple_of(two * 2 * HD, 2 * HD)
        lanes = pl.ds(start, 2 * HD)
        pairs = qkv_ref[0, :, lanes], qkv_ref[1, :, lanes], qkv_ref[2, :, lanes], cg_ref[:, lanes]
        parts = [[], [], []]
        for here in (slice(0, HD), slice(HD, 2 * HD)):
            queries, keys, values, grad = [item[:, here] for item in pairs]
            scores = mm_t(queries, keys) * (HD**-0.5) + key_bias
            scores = jnp.exp(scores - jnp.max(scores, axis=-1, keepdims=True))
            probs = scores * (1.0 / jnp.sum(scores, axis=-1, keepdims=True))
            d_values = t_mm(probs.astype(BF16), grad)
            d_probs = mm_t(grad, values)
            inner = jnp.sum(probs * d_probs, axis=-1, keepdims=True)
            d_scores = (probs * (d_probs - inner)).astype(BF16)
            parts[0].append(mm(d_scores, keys) * (HD**-0.5))
            parts[1].append(t_mm(d_scores, queries) * (HD**-0.5))
            parts[2].append(d_values)
        for part in range(3):
            target = pl.ds(pl.multiple_of(part * local + start, 2 * HD), 2 * HD)
            grad_ref[:, target] = jnp.concatenate(parts[part], axis=1).astype(BF16)
        return carry

    lax.fori_loop(0, local // (2 * HD), heads, 0)
    sum_ref[0:1, :] = jnp.sum(grad_ref[:, :local].astype(F32), axis=0, keepdims=True)
    sum_ref[1:2, :] = jnp.sum(grad_ref[:, 2 * local :].astype(F32), axis=0, keepdims=True)
    half = g_ref.shape[0] // 2

    def back(first, last):
        total = mm_t(grad_ref[first:last, :local], w_ref[0])
        total += mm_t(grad_ref[first:last, local : 2 * local], w_ref[1])
        return total + mm_t(grad_ref[first:last, 2 * local :], w_ref[2])

    send_ref[...] = back(half, 2 * half).astype(BF16)
    keep_ref[...] = back(0, half)


def attn_backward(level, info, limits, pieces, w_out, context, qkv, w_qkv):
    rows, width = pieces[0].shape
    total = 4 * rows
    local = w_out.shape[0]
    ins = (info, limits, *pieces, w_out, context, qkv, w_qkv)
    outs = [
        shaped((total, 3 * local), BF16),
        shaped((2, local), F32),
        shaped((total // 2, width), BF16),
        shaped((total // 2, width), F32),
    ]
    return launch(
        functools.partial(attn_backward_kernel, level),
        out_shape=outs,
        grid=(1,),
        in_specs=[SMEM, SMEM] + [whole(item.shape) for item in ins[2:]],
        out_specs=[whole(item.shape) for item in outs],
        scratch_shapes=[pltpu.VMEM((total, width), BF16), pltpu.VMEM((total, local), BF16)],
        compiler_params=params(32),
        cost_estimate=cost(6e9, 8 << 20, 1 << 20),
        far_ins=(6, 7, 8, 9),
    )(*ins)


LINK_ORDERS = ((1, 2, 4), (2, 1, 4))
FFN_ORDERS = (0, 1)
ATTN_WHOLE = ((0,), ((0, 1024),))
ATTN_CUT = ((0, 1), ((0, 512), (512, 1024)))


def block_masks(bits):
    return [
        (bits[0] if item & 4 else 0) ^ (bits[1] if item & 2 else 0) ^ (bits[2] if item & 1 else 0)
        for item in range(8)
    ]


def halves(target_pair, item):
    send_ref, keep_ref = target_pair
    return keep_ref if item < 4 else send_ref


def ffn_grad_kernel(table_ref, low_ref, g0, g1, g2, g3, h0, h1, h2, h3, grad_ref, *refs):
    targets, total_ref = refs[:4], refs[4]
    block = total_ref.shape[0] // 8
    for part, order in enumerate(FFN_ORDERS):
        if part == 0:
            total_ref[...] = t_mm(low_ref[...], jnp.concatenate([g0[...], g1[...], g2[...], g3[...]], axis=0))
        else:
            total_ref[...] = t_mm(jnp.concatenate([h0[...], h1[...], h2[...], h3[...]], axis=0), grad_ref[...])
        for item in range(8):
            first = pl.multiple_of(table_ref[order, item] * block, block)
            target = halves(targets[2 * part : 2 * part + 2], item)
            target[item % 4] = total_ref[pl.ds(first, block), :].astype(target.dtype)


def ffn_grad(table, act_low, g_pieces, h_pieces, up_grad):
    ins = [act_low, *g_pieces, *h_pieces, up_grad]
    width = up_grad.shape[1]
    outs = [shaped((4, width // 8, width), dtype) for _ in FFN_ORDERS for dtype in (BF16, F32)]
    return launch(
        ffn_grad_kernel,
        out_shape=outs,
        grid_spec=pltpu.PrefetchScalarGridSpec(
            num_scalar_prefetch=1,
            grid=(1,),
            in_specs=[whole(item.shape) for item in ins],
            out_specs=[whole(item.shape) for item in outs],
            scratch_shapes=[pltpu.VMEM((width, width), F32)],
        ),
        compiler_params=params(34),
        cost_estimate=cost(),
        far_ins=(0, 5, 6, 7, 8), far_outs=range(4),
    )(table, *ins)


def attn_grad_kernel(plan, table_ref, x0, x1, x2, x3, grad_ref, low_ref, g0, g1, g2, g3, *refs):
    targets, total_ref, out_ref = refs[:-2], refs[-2], refs[-1]
    total_ref[...] = t_mm(jnp.concatenate([x0[...], x1[...], x2[...], x3[...]], axis=0), grad_ref[...])
    out_ref[...] = t_mm(low_ref[...], jnp.concatenate([g0[...], g1[...], g2[...], g3[...]], axis=0))
    block = total_ref.shape[0] // 8
    local3 = total_ref.shape[1]
    span = out_ref.shape[0] // 8
    side = out_ref.shape[1] * span // block
    for part, (order, (start, stop)) in enumerate(zip(*plan)):
        for item in range(8):
            target = halves(targets[2 * part : 2 * part + 2], item)
            if start < local3:
                end = min(stop, local3)
                first = pl.multiple_of(table_ref[order, item] * block, block)
                value = total_ref[pl.ds(first, block), start:end]
                target[item % 4, :, : end - start] = value.astype(target.dtype)
            if stop > local3:
                first = pl.multiple_of(table_ref[order, item] * span, span)
                taken = out_ref[pl.ds(first, span), :]
                for place in range(block // span):
                    target[item % 4, place * span : (place + 1) * span, local3 - start :] = taken[
                        :, place * side : (place + 1) * side
                    ].astype(target.dtype)


def attn_grad(plan, table, x_pieces, qkv_grad, ctx_low, g_pieces):
    ins = [*x_pieces, qkv_grad, ctx_low, *g_pieces]
    width = x_pieces[0].shape[1]
    outs = [shaped((4, width // 8, last - first), dtype) for first, last in plan[1] for dtype in (BF16, F32)]
    return launch(
        functools.partial(attn_grad_kernel, plan),
        out_shape=outs,
        grid_spec=pltpu.PrefetchScalarGridSpec(
            num_scalar_prefetch=1,
            grid=(1,),
            in_specs=[whole(item.shape) for item in ins],
            out_specs=[whole(item.shape) for item in outs],
            scratch_shapes=[
                pltpu.VMEM((width, qkv_grad.shape[1]), F32),
                pltpu.VMEM((ctx_low.shape[1], width), F32),
            ],
        ),
        compiler_params=params(30),
        cost_estimate=cost(),
        far_ins=(0, 1, 2, 3, 5), far_outs=range(6),
    )(table, *ins)


def fold_kernel(count, parts, scaled, *refs):
    outs = refs[-parts:]
    for part in range(parts):
        mine = refs[part * count : (part + 1) * count]
        total = mine[0][...]
        for other in mine[1:]:
            total = total + other[...].astype(F32)
        if scaled:
            total = total * refs[parts * count + part][...]
        outs[part][...] = total.astype(BF16)


def fold(size, parts, scales=None):
    ins, in_specs, outs, out_specs = [], [], [], []
    count = len(parts[0])
    blocks = max(size, 1)
    for arrays in parts:
        rest = arrays[0].shape[1:]
        for array in arrays:
            ins.append(array)
            place = 1 if size else 0
            in_specs.append(pl.BlockSpec((blocks, *rest), lambda s, place=place: (place, 0, 0)))
        outs.append(shaped((blocks, *rest), BF16))
        out_specs.append(whole((blocks, *rest)))
    if scales is not None:
        for scale, columns in scales:
            width = columns[1] - columns[0]
            ins.append(scale)
            in_specs.append(pl.BlockSpec((scale.shape[0], width), lambda s, at=columns[0] // width: (0, at)))
    return launch(
        functools.partial(fold_kernel, count, len(parts), scales is not None),
        out_shape=outs,
        grid=(1,),
        in_specs=in_specs,
        out_specs=out_specs,
        compiler_params=params(16),
        cost_estimate=cost(),
        far_ins=range(len(ins)), far_outs=range(len(outs)),
    )(*ins)


def pair_kernel(parts, *refs):
    for part in range(parts):
        first, second, target = refs[2 * part], refs[2 * part + 1], refs[2 * parts + part]
        half = first.shape[0]
        target[:half] = first[...]
        target[half:] = second[...]


def pair(firsts, seconds):
    ins = [item for both in zip(firsts, seconds) for item in both]
    outs = [shaped((2 * item.shape[0], *item.shape[1:]), BF16) for item in firsts]
    return launch(
        functools.partial(pair_kernel, len(firsts)),
        out_shape=outs,
        grid=(1,),
        in_specs=[whole(item.shape) for item in ins],
        out_specs=[whole(item.shape) for item in outs],
        compiler_params=params(12),
        cost_estimate=cost(),
        far_ins=range(len(ins)), far_outs=range(len(outs)),
    )(*ins)


def place_kernel(plan, table_ref, *refs):
    outs = refs[-2:]
    step = pl.program_id(0)

    def store(part, source, item):
        start, stop = plan[1][part]
        if len(outs[0].shape) == 3:
            outs[part][0] = source[item].astype(F32)
            return
        qkv_ref, out_ref = outs
        local = qkv_ref.shape[3]
        for column in range(start, min(stop, 3 * local), 128):
            target = slice(column % local, column % local + 128)
            qkv_ref[0, column // local, :, target] = source[item, :, column - start : column - start + 128].astype(F32)
        if stop > 3 * local:
            span = out_ref.shape[1]
            side = stop - 3 * local
            for place in range(source.shape[1] // span):
                out_ref[0, :, place * side : (place + 1) * side] = source[
                    item, place * span : (place + 1) * span, 3 * local - start :
                ].astype(F32)

    for part, order in enumerate(plan[0]):
        item = table_ref[order, step]
        pl.when(item < 4)(functools.partial(store, part, refs[2 * part], item))
        pl.when(item >= 4)(functools.partial(store, part, refs[2 * part + 1], item - 4))


def place_blocks(plan, table, level, nears, fars, shapes, earlier):
    specs = []
    for shape in shapes:
        if len(shape) == 4:
            specs.append(pl.BlockSpec((1, shape[1], shape[2] // 8, shape[3]), lambda s, t: (level, 0, s, 0)))
        else:
            specs.append(pl.BlockSpec((1, shape[1] // 8, shape[2]), lambda s, t: (level, s, 0)))
    ins = [item for both in zip(nears, fars) for item in both]
    earlier = list(earlier or [])
    return launch(
        functools.partial(place_kernel, plan),
        out_shape=[shaped(shape, F32) for shape in shapes],
        grid_spec=pltpu.PrefetchScalarGridSpec(
            num_scalar_prefetch=1,
            grid=(8,),
            in_specs=[whole(item.shape) for item in ins] + [pl.BlockSpec(memory_space=pl.ANY)] * len(earlier),
            out_specs=specs,
        ),
        input_output_aliases={1 + len(ins) + place: place for place in range(len(earlier))},
        compiler_params=params(24),
        cost_estimate=cost(),
        far_ins=range(len(ins)), far_outs=range(len(shapes)),
    )(table, *ins, *earlier)


def near_sum_kernel(keep_ref, near_ref, out_ref):
    out_ref[...] = (keep_ref[...] + near_ref[...].astype(F32)).astype(BF16)


def near_sum(keep, near):
    rows, width = keep.shape[0] // 2, keep.shape[1]
    second = pl.BlockSpec((rows, width), lambda s: (1, 0))
    return launch(
        near_sum_kernel,
        out_shape=shaped((rows, width), BF16),
        grid=(1,),
        in_specs=[second, second],
        out_specs=whole((rows, width)),
        compiler_params=params(8),
        cost_estimate=cost(),
    )(keep, near)


def pack_kernel(layers, *refs):
    out_ref = refs[-1]
    row = 0
    for layer in range(layers):
        mid, out = refs[2 * layer], refs[2 * layer + 1]
        for source in (mid[0:1, :], out[0:1, :], mid[1:3, :], out[1:3, :]):
            out_ref[row : row + source.shape[0], :] = source
            row += source.shape[0]
    out_ref[row : row + 1, :] = refs[-2][...]


def pack(sums, peaks):
    ins = [item for both in sums for item in both] + [peaks]
    out = shaped((6 * len(sums) + 1, peaks.shape[1]), F32)
    return launch(
        functools.partial(pack_kernel, len(sums)),
        out_shape=out,
        grid=(1,),
        in_specs=[whole(item.shape) for item in ins],
        out_specs=whole(out.shape),
        compiler_params=params(8),
        cost_estimate=cost(),
    )(*ins)


def merge_kernel(peak_row, more, mine_ref, other_ref, *refs):
    out_ref = refs[-1]
    mine, other = mine_ref[...], other_ref[...]
    row = lax.broadcasted_iota(jnp.int32, mine.shape, 0)
    merged = jnp.where(row == peak_row, jnp.maximum(mine, other), mine + other)
    if not more:
        out_ref[...] = merged
        return
    count = mine.shape[0]
    out_ref[:count, :] = merged
    for item in range(more):
        up_ref, qv_ref = refs[2 * item], refs[2 * item + 1]
        out_ref[count + item : count + item + 1, :] = up_ref[...]
        local = qv_ref.shape[1]
        for part in range(2):
            start = (2 * item + part) * local
            out_ref[count + more : count + more + 1, start : start + local] = qv_ref[part : part + 1, :]


def merge(peak_row, mine, other, shards=()):
    ins = [mine, other] + [item for both in shards for item in both]
    rows = mine.shape[0] + (len(shards) + 1 if shards else 0)
    return launch(
        functools.partial(merge_kernel, peak_row, len(shards)),
        out_shape=shaped((rows, mine.shape[1]), F32),
        grid=(1,),
        in_specs=[whole(item.shape) for item in ins],
        out_specs=whole((rows, mine.shape[1])),
        compiler_params=params(8),
        cost_estimate=cost(),
    )(*ins)


def peaks_kernel(*refs):
    out_ref = refs[-1]
    for item, ref in enumerate(refs[:-1]):
        top = jnp.max(ref[...], axis=1, keepdims=True)
        out_ref[0:1, item * 128 : (item + 1) * 128] = jnp.broadcast_to(top, (1, 128))


def peaks_row(rows):
    return launch(
        peaks_kernel,
        out_shape=shaped((1, 128 * len(rows)), F32),
        grid=(1,),
        in_specs=[whole(item.shape) for item in rows],
        out_specs=whole((1, 128 * len(rows))),
        compiler_params=params(8),
        cost_estimate=cost(0, 1 << 16),
    )(*rows)


STEPS = {
    "M41": ("F1",),
    "M20": ("F1",),
    "M31": (),
    "M30": (),
    "WT0": (),
    "end0": (),
}


def fast_on_device(
    tokens,
    cotangent,
    lengths,
    qkv_weight,
    qv_bias,
    out_weight,
    out_bias,
    up_weight,
    up_bias,
    down_weight,
    down_bias,
    norm_params,
    act_ranges,
):
    row_count, width = tokens.shape
    tp_count = lax.axis_size("tp")
    rank = lax.axis_index("tp")
    place = lax.axis_index("dp")
    layers = qkv_weight.shape[0]
    local = qkv_weight.shape[3]
    order = jnp.array(block_order(tp_count), jnp.int32)
    info = jnp.concatenate([(rank ^ order) * row_count, lengths])
    qkv_blocks = jnp.transpose(qkv_weight, (0, 2, 1, 3))
    weights = (qkv_blocks, out_weight, up_weight, down_weight)
    core_bit, far_bit = bits_of(tp_count)
    place_list = place[None].astype(jnp.int32)
    Line.mark = None
    Line.free = False

    def run(step, *values):
        return step(*values)

    def spread(rows):
        return rows, swap(rows, "tp", far_bit), swap(rows, "tp", core_bit)

    def finish(begun):
        rows, far, near = begun
        far, _ = lax.optimization_barrier((far, Line.mark))
        return (rows, far, near, swap(far, "tp", core_bit))

    def gather_sum(send, keep):
        near = swap(send, "tp", core_bit)
        return near, swap(near_sum(keep, near), "tp", far_bit)

    x_low, x_peak = run(enter, info, act_ranges, tokens)
    x_begun = spread(x_low)
    low_weights = [dict() for _ in range(layers)]
    names = ("qkv", "out", "up", "down")
    sets = {}

    def find_tops(level, first, last):
        mine = weight_tops_of(level, weights[first:last])
        others = [swap(mine, "tp", bit) for bit in (core_bit, far_bit, core_bit | far_bit)]
        sets[level, first] = (mine, *others)

    def squash_some(level, origin, first, last):
        outs = squash_weights(level, sets[level, origin], first - origin, weights[first:last])
        for name, out in zip(names[first:last], outs):
            low_weights[level][name] = out

    find_tops(0, 0, 2)
    find_tops(0, 2, 4)
    squash_some(0, 0, 0, 2)
    slopes = [None] * layers
    kept = []
    peak_rows = []
    current = tokens
    for level in range(layers):
        low = low_weights[level]
        last = level == layers - 1
        x_pieces = finish(x_begun)
        qkv, context, ctx_low, ctx_peak, send, keep = run(
            lambda pieces, w_qkv, w_out: attn_forward(level, info, act_ranges, pieces, w_qkv, qv_bias, w_out),
            x_pieces, low["qkv"], low["out"],
        )
        near, far = gather_sum(send, keep)
        if level == 0:
            squash_some(0, 2, 2, 4)
        else:
            squash_some(1, 0, 2, 4)
        mid_unit, mid_scale, hidden, hid_low, hid_peak = run(
            lambda *t: join_rows(level, 0, False, info, act_ranges, *t, out_bias, norm_params),
            current, keep, near, far,
        )
        h_begun = spread(hid_low)
        if level == 0:
            find_tops(1, 0, 4)
        h_pieces = finish(h_begun)
        act_low, slope, act_peak, send, keep = run(
            lambda pieces, w_up, w_down: ffn_forward(level, info, act_ranges, pieces, w_up, up_bias, w_down),
            h_pieces, low["up"], low["down"],
        )
        near, far = gather_sum(send, keep)
        if level == 0:
            squash_some(1, 0, 0, 2)
        else:
            slopes[1] = slope_pieces(1, place_list, [sets[1, 0]], ((0, 0), (0, 1), (0, 2), (0, 3)), weights)
            slopes[0] = slope_pieces(
                0, place_list, [sets[0, 0], sets[0, 2]], ((0, 0), (0, 1), (1, 0), (1, 1)), weights
            )
            peak_rows.append([x_peak, ctx_peak, hid_peak, act_peak])
            peaks = run(lambda *t: peaks_row(t), *peak_rows[0], *peak_rows[1])
        result = run(
            lambda *t: join_rows(level, 2, last, info, act_ranges, *t, down_bias, norm_params),
            hidden, keep, near, far,
        )
        peak_rows.append([x_peak, ctx_peak, hid_peak, act_peak])
        kept.append(
            dict(
                x=x_pieces, qkv=qkv, context=context, ctx_low=ctx_low, mid_unit=mid_unit, mid_scale=mid_scale,
                h=h_pieces, act_low=act_low, slope=slope, out_unit=result[0], out_scale=result[1], **{
                    "w_" + name: value for name, value in low.items()
                },
            )
        )
        if last:
            output = result[2]
        else:
            current, x_low, x_peak = result[2:]
            x_begun = spread(x_low)

    masks = [block_masks(bits) for bits in LINK_ORDERS]
    table = place ^ jnp.array(masks, jnp.int32)
    inverse = jnp.array([[row.index(item) for item in range(8)] for row in masks], jnp.int32)
    inverse = jnp.take(inverse, place ^ jnp.arange(8), axis=1)
    finished = {"ffn": None, "attn": None}
    shapes = {"ffn": [down_weight.shape, up_weight.shape], "attn": [qkv_blocks.shape, out_weight.shape]}

    full = (0, width)
    plans = {
        "ffn1": (FFN_ORDERS, (full, full)), "ffn0": (FFN_ORDERS, (full, full)), "attn1": ATTN_WHOLE, "attn0": ATTN_CUT,
    }

    def stream(level, name, outs):
        plan = plans[name + str(level)]

        key = {"ffn": "F", "attn": "T"}[name] + str(level)

        def swap_parts(parts, step):
            flying[key] = [swap(item, "dp", LINK_ORDERS[order][step]) for item, order in zip(parts, plan[0])]
            return flying[key]

        moved = [list(outs[1::2]), swap_parts(outs[0::2], 0)]
        yield
        moved.append(swap_parts(fold(2, list(zip(*moved))), 1))
        yield
        moved.append(swap_parts(fold(1, list(zip(*moved))), 2))
        yield
        scales = slopes[level][:2] if name == "ffn" else [slopes[level][2]] * len(plan[0])
        pieces = fold(0, list(zip(*moved)), list(zip(scales, plan[1])))
        for step in (2, 1):
            others = swap_parts(pieces, step)
            yield
            pieces = pair(pieces, others)
        others = swap_parts(pieces, 0)
        yield
        finished[name] = place_blocks(plan, inverse, level, pieces, others, shapes[name], finished[name])
        yield

    streams, flying = {}, {}

    def begin(level, name, outs):
        streams[{"ffn": "F", "attn": "T"}[name] + str(level)] = stream(level, name, outs)
        next(streams[{"ffn": "F", "attn": "T"}[name] + str(level)])

    def go(point, level):
        for item in STEPS.get(point + str(level), ()):
            next(streams[item])

    def back_norm(level, base, keep, near, far):
        return run(
            lambda *t: mid_back(level, 0, act_ranges, *t, norm_params),
            base, keep, near, far, kept[level]["mid_unit"], kept[level]["mid_scale"],
        )

    rep_list = [None] * layers
    shard_list = [None] * layers
    top = layers - 1
    d_final, down_grad, sums_out = run(
        lambda *t: top_back(top, info, cotangent, *t, norm_params),
        kept[top]["out_unit"], kept[top]["out_scale"],
    )
    g_begun = spread(down_grad)
    for level in reversed(range(layers)):
        saved = kept[level]
        go("M4", level + 1)
        g_pieces = finish(g_begun)
        up_grad, up_sum, send, keep = run(
            ffn_backward, g_pieces, saved["w_down"], saved["slope"], saved["w_up"]
        )
        near, far = gather_sum(send, keep)
        begin(
            level, "ffn", run(lambda *t: ffn_grad(table, *t), saved["act_low"], g_pieces, saved["h"], up_grad)
        )
        go("WF", level)
        d_mid, out_grad, sums_mid = back_norm(level, d_final, keep, near, far)
        o_begun = spread(out_grad)
        go("M2", level)
        o_pieces = finish(o_begun)
        qkv_grad, qv_sum, send, keep = run(
            lambda *t: attn_backward(level, info, act_ranges, *t),
            o_pieces, saved["w_out"], saved["context"], saved["qkv"], saved["w_qkv"],
        )
        near, far = gather_sum(send, keep)
        begin(
            level, "attn",
            run(lambda *t: attn_grad(plans["attn" + str(level)], table, *t), saved["x"], qkv_grad, saved["ctx_low"], o_pieces),
        )
        go("WT", level)
        rep_list[level] = (sums_mid, sums_out)
        shard_list[level] = (up_sum, qv_sum)
        if level > 0:
            below = kept[level - 1]
            d_final, down_grad, sums_out = run(
                lambda *t: mid_back(level - 1, 2, act_ranges, *t, norm_params),
                d_mid, keep, near, far, below["out_unit"], below["out_scale"],
            )
            g_begun = spread(down_grad)
        else:
            input_grad = run(lambda *t: end_back(act_ranges, *t, tokens), d_mid, keep, near, far)

    def small():
        peak_row = 6 * layers
        total = pack(rep_list, peaks)
        moved = swap(total, "tp", far_bit)
        flying["S0"] = [moved]
        yield
        total = merge(peak_row, total, moved)
        moved = swap(total, "tp", core_bit)
        flying["S0"] = [moved]
        yield
        total = merge(peak_row, total, moved, shard_list)
        for bit in (1, 2, 4):
            moved = swap(total, "dp", bit)
            flying["S0"] = [moved]
            yield
            total = merge(peak_row, total, moved)
        finished["small"] = total
        yield

    streams["S0"] = small()
    next(streams["S0"])
    go("end", 0)
    Line.free = True
    for item in streams.values():
        for _ in item:
            pass
    rep = finished["small"]
    sums = rep[: 6 * layers].reshape(layers, 6, width)
    peaks = rep[6 * layers].reshape(layers, 4, 128)[:, :, 0]
    up_sum = rep[6 * layers + 1 : 6 * layers + 1 + layers]
    qv_sum = rep[6 * layers + 1 + layers].reshape(layers, 2, local)
    return (
        output,
        input_grad,
        jnp.transpose(finished["attn"][0], (0, 2, 1, 3)),
        qv_sum,
        finished["attn"][1],
        sums[:, 0],
        finished["ffn"][1],
        up_sum,
        finished["ffn"][0],
        sums[:, 1],
        sums[:, 2:],
        peaks,
    )


def any_on_device(*args):
    tokens, lengths, qkv_weight, out_weight, up_weight = args[0], args[2], args[3], args[5], args[7]
    fits = (
        lax.axis_size("tp") == 4
        and lax.axis_size("dp") == 8
        and lengths.shape[0] == 1
        and tokens.shape[0] * 4 == SEQ_LEN
        and tokens.shape[1] == 1024
        and qkv_weight.shape[3] == 256
        and up_weight.shape[2] == 1024
    )
    return (fast_on_device if fits else on_device)(*args)


def solution(mesh):
    return jax.shard_map(
        any_on_device,
        mesh=mesh,
        in_specs=(
            P(("dp", "tp"), None),
            P(("dp", "tp"), None),
            P("dp"),
            P(None, None, None, "tp"),
            P(None, None, "tp"),
            P(None, "tp", None),
            P(),
            P(None, None, "tp"),
            P(None, "tp"),
            P(None, "tp", None),
            P(),
            P(),
            P(),
        ),
        out_specs=(
            P(("dp", "tp"), None),
            P(("dp", "tp"), None),
            P(None, None, None, "tp"),
            P(None, None, "tp"),
            P(None, "tp", None),
            P(),
            P(None, None, "tp"),
            P(None, "tp"),
            P(None, "tp", None),
            P(),
            P(),
            P(),
        ),
        check_vma=False,
    )
```

```python
import functools

import jax
import jax.numpy as jnp
from jax import lax
from jax.experimental import pallas as pl
from jax.experimental.pallas import tpu as pltpu
from jax.sharding import PartitionSpec as P

HD = 64
SEQ_LEN = 512
NORM_EPSILON = 1e-06
F32 = jnp.float32
BF16 = jnp.bfloat16


def bits_of(count):
    return [1 << place for place in range(count.bit_length() - 1)]


def swap(value, axis, bit):
    count = lax.axis_size(axis)
    return lax.ppermute(value, axis, [(item, item ^ bit) for item in range(count)])


def block_order(count):
    order = [0]
    for bit in reversed(bits_of(count)):
        order = order + [item ^ bit for item in order]
    return order


def gather_rows(rows):
    block = rows
    for bit in reversed(bits_of(lax.axis_size("tp"))):
        block = jnp.concatenate([block, swap(block, "tp", bit)], axis=0)
    return block


def scatter_rows(partial):
    for bit in bits_of(lax.axis_size("tp")):
        half = partial.shape[0] // 2
        arrived = swap(partial[half:].astype(BF16), "tp", bit)
        partial = partial[:half] + arrived.astype(F32)
    return partial


def squash(value, limit):
    return limit * jnp.tanh(value / limit)


def squash_slope(value, limit):
    level_value = jnp.tanh(value / limit)
    return 1.0 - level_value * level_value


def norm_parts(values):
    centre = jnp.mean(values, axis=-1, keepdims=True)
    centred = values - centre
    spread = jnp.mean(centred * centred, axis=-1, keepdims=True)
    scale = lax.rsqrt(spread + NORM_EPSILON)
    return centred * scale, scale


def norm_back(gradient, unit, scale, gain):
    scaled = gradient * gain
    first = jnp.mean(scaled, axis=-1, keepdims=True)
    second = jnp.mean(scaled * unit, axis=-1, keepdims=True)
    d_values = scale * (scaled - first - unit * second)
    return d_values, jnp.sum(gradient * unit, axis=0), jnp.sum(gradient, axis=0)


def mm(first, second):
    return jnp.dot(first, second, preferred_element_type=F32)


def mm_t(first, second):
    return lax.dot_general(first, second, (((1,), (1,)), ((), ())), preferred_element_type=F32)


def t_mm(first, second):
    return lax.dot_general(first, second, (((0,), (0,)), ((), ())), preferred_element_type=F32)


def reduce_weight(left, right, raw, top, order):
    place = lax.axis_index("dp")
    rows = left.shape[1]
    start = 0
    bit = order[0]
    mine = (place // bit) % 2
    half = rows // 2
    send = t_mm(lax.dynamic_slice_in_dim(left, (1 - mine) * half, half, 1), right).astype(BF16)
    arrived = swap(send, "dp", bit)
    total = t_mm(lax.dynamic_slice_in_dim(left, mine * half, half, 1), right)
    total = total + arrived.astype(F32)
    start = mine * half
    for bit in order[1:]:
        mine = (place // bit) % 2
        half = half // 2
        send = lax.dynamic_slice_in_dim(total, (1 - mine) * half, half, 0).astype(BF16)
        arrived = swap(send, "dp", bit)
        total = lax.dynamic_slice_in_dim(total, mine * half, half, 0) + arrived.astype(F32)
        start = start + mine * half
    raw_piece = lax.dynamic_slice_in_dim(raw, start, half, 0).astype(F32)
    piece = (total * squash_slope(raw_piece, top)).astype(BF16)
    for bit in reversed(order):
        mine = (place // bit) % 2
        arrived = swap(piece, "dp", bit)
        low_half = jnp.where(mine == 0, piece, arrived)
        high_half = jnp.where(mine == 0, arrived, piece)
        piece = jnp.concatenate([low_half, high_half], axis=0)
    return piece.astype(F32)


def on_device(
    tokens,
    cotangent,
    lengths,
    qkv_weight,
    qv_bias,
    out_weight,
    out_bias,
    up_weight,
    up_bias,
    down_weight,
    down_bias,
    norm_params,
    act_ranges,
):
    row_count, width = tokens.shape
    tp_count = lax.axis_size("tp")
    dp_count = lax.axis_size("dp")
    rank = lax.axis_index("tp")
    all_rows = row_count * tp_count
    assert lengths.shape[0] == 1 and all_rows == SEQ_LEN
    layer_count = qkv_weight.shape[0]
    local_width = qkv_weight.shape[3]
    local_units = up_weight.shape[2]
    heads_here = local_width // HD
    score_scale = HD ** (-0.5)
    order = jnp.array(block_order(tp_count), jnp.int32)
    places = ((rank ^ order)[:, None] * row_count + jnp.arange(row_count)[None, :]).reshape(all_rows)
    inside = places < lengths[0]
    valid_all = inside.astype(F32)[:, None]
    valid_rows = valid_all[:row_count]
    key_bias = jnp.where(inside, 0.0, -1000000000.0).astype(F32)
    qkv_blocks = jnp.transpose(qkv_weight, (0, 2, 1, 3))
    local_tops = jnp.stack(
        [
            jnp.stack(
                [
                    jnp.max(jnp.abs(qkv_blocks[level])),
                    jnp.max(jnp.abs(out_weight[level])),
                    jnp.max(jnp.abs(up_weight[level])),
                    jnp.max(jnp.abs(down_weight[level])),
                ]
            )
            for level in range(layer_count)
        ]
    ).astype(F32)
    weight_tops = local_tops
    for bit in bits_of(tp_count):
        weight_tops = jnp.maximum(weight_tops, swap(weight_tops, "tp", bit))

    def scores_of(queries, key_rows):
        raw = jnp.einsum("qhd,khd->hqk", queries, key_rows, preferred_element_type=F32)
        return raw * score_scale + key_bias[None, None, :]

    stored = []
    peak_list = []
    current = tokens.astype(F32)
    for level in range(layer_count):
        limits = act_ranges[level]
        tops = weight_tops[level]
        w_qkv = squash(qkv_blocks[level].astype(F32), tops[0]).astype(BF16)
        w_out = squash(out_weight[level].astype(F32), tops[1]).astype(BF16)
        w_up = squash(up_weight[level].astype(F32), tops[2]).astype(BF16)
        w_down = squash(down_weight[level].astype(F32), tops[3]).astype(BF16)
        x_low_all = gather_rows(squash(current, limits[0]).astype(BF16))
        heads = (all_rows, heads_here, HD)
        queries = (mm(x_low_all, w_qkv[0]) + qv_bias[level, 0].astype(F32)).astype(BF16).reshape(heads)
        key_rows = mm(x_low_all, w_qkv[1]).astype(BF16).reshape(heads)
        value_rows = (mm(x_low_all, w_qkv[2]) + qv_bias[level, 1].astype(F32)).astype(BF16).reshape(heads)
        scores = scores_of(queries, key_rows)
        peak_score = jnp.max(scores, axis=-1, keepdims=True)
        log_total = peak_score + jnp.log(jnp.sum(jnp.exp(scores - peak_score), axis=-1, keepdims=True))
        attn_probs = jnp.exp(scores - log_total).astype(BF16)
        context = jnp.einsum("hqk,khd->qhd", attn_probs, value_rows, preferred_element_type=F32)
        context = context.reshape(all_rows, local_width)
        ctx_low = squash(context, limits[1]).astype(BF16)
        attn_rows = scatter_rows(mm(ctx_low, w_out))
        mid_unit, mid_scale = norm_parts(current + attn_rows + out_bias[level].astype(F32))
        hidden = mid_unit * norm_params[level, 0] + norm_params[level, 1]
        hid_low_all = gather_rows(squash(hidden, limits[2]).astype(BF16))
        up_value = mm(hid_low_all, w_up) + up_bias[level].astype(F32)
        normal_cdf = 0.5 + 0.5 * lax.erf(up_value * (0.5**0.5))
        active = up_value * normal_cdf
        act_level = jnp.tanh(active / limits[3])
        act_low = (limits[3] * act_level).astype(BF16)
        gelu_slope = normal_cdf + up_value * jnp.exp(-0.5 * up_value * up_value) * 0.3989422804014327
        up_slope = (1.0 - act_level * act_level) * gelu_slope
        down_rows = scatter_rows(mm(act_low, w_down))
        out_unit, out_scale = norm_parts(hidden + down_rows + down_bias[level].astype(F32))
        peak_list.append(
            jnp.stack(
                [
                    jnp.max(jnp.abs(current) * valid_rows),
                    jnp.max(jnp.abs(context) * valid_all),
                    jnp.max(jnp.abs(hidden) * valid_rows),
                    jnp.max(jnp.abs(active) * valid_all),
                ]
            )
        )
        stored.append(
            (
                current, mid_unit, mid_scale, hidden, out_unit, out_scale, x_low_all, queries, key_rows, value_rows,
                log_total, context, ctx_low, hid_low_all, up_slope, act_low, w_qkv, w_out, w_up, w_down,
            )
        )
        current = out_unit * norm_params[level, 2] + norm_params[level, 3]
    output = current.astype(BF16)
    gradient = cotangent.astype(F32) * valid_rows

    dp_bits = bits_of(dp_count)
    big_list = [None] * layer_count
    rep_list = [None] * layer_count
    shard_list = [None] * layer_count
    for level in reversed(range(layer_count)):
        (
            inputs, mid_unit, mid_scale, hidden, out_unit, out_scale, x_low_all, queries, key_rows, value_rows,
            log_total, context, ctx_low, hid_low_all, up_slope, act_low, w_qkv, w_out, w_up, w_down,
        ) = stored[level]
        limits = act_ranges[level]
        tops = weight_tops[level]
        d_final, d_gain_out, d_shift_out = norm_back(gradient, out_unit, out_scale, norm_params[level, 2])
        down_grad = d_final.astype(BF16)
        d_down_bias = jnp.sum(down_grad.astype(F32), axis=0)
        down_grad_all = gather_rows(down_grad)
        up_grad = (mm_t(down_grad_all, w_down) * up_slope).astype(BF16)
        g_down = reduce_weight(act_low, down_grad_all, down_weight[level], tops[3], dp_bits)
        d_up_bias = jnp.sum(up_grad.astype(F32), axis=0)
        d_hid_rows = scatter_rows(mm_t(up_grad, w_up))
        g_up = reduce_weight(hid_low_all, up_grad, up_weight[level], tops[2], dp_bits)
        d_hidden = d_final + d_hid_rows * squash_slope(hidden, limits[2])
        d_mid, d_gain_mid, d_shift_mid = norm_back(d_hidden, mid_unit, mid_scale, norm_params[level, 0])
        out_grad = d_mid.astype(BF16)
        d_out_bias = jnp.sum(out_grad.astype(F32), axis=0)
        out_grad_all = gather_rows(out_grad)
        ctx_grad = (mm_t(out_grad_all, w_out) * squash_slope(context, limits[1])).astype(BF16)
        g_out = reduce_weight(ctx_low, out_grad_all, out_weight[level], tops[1], dp_bits)
        ctx_grad = ctx_grad.reshape(heads)
        soft_probs = jnp.exp(scores_of(queries, key_rows) - log_total)
        soft_low = soft_probs.astype(BF16)
        d_values = jnp.einsum("hqk,qhd->khd", soft_low, ctx_grad, preferred_element_type=F32)
        d_probs = jnp.einsum("qhd,khd->hqk", ctx_grad, value_rows, preferred_element_type=F32)
        d_scores = (
            soft_probs * (d_probs - jnp.sum(soft_probs * d_probs, axis=-1, keepdims=True))
        ).astype(BF16)
        d_queries = jnp.einsum("hqk,khd->qhd", d_scores, key_rows, preferred_element_type=F32) * score_scale
        d_keys = jnp.einsum("hqk,qhd->khd", d_scores, queries, preferred_element_type=F32) * score_scale
        parts = [
            item.astype(BF16).reshape(all_rows, local_width) for item in (d_queries, d_keys, d_values)
        ]
        d_x_rows = scatter_rows(
            mm_t(parts[0], w_qkv[0]) + mm_t(parts[1], w_qkv[1]) + mm_t(parts[2], w_qkv[2])
        )
        g_qkv = reduce_weight(
            x_low_all,
            jnp.concatenate(parts, axis=1),
            jnp.transpose(qkv_blocks[level], (1, 0, 2)).reshape(width, 3 * local_width),
            tops[0],
            dp_bits,
        ).reshape(width, 3, local_width)
        d_qv_bias = jnp.stack([jnp.sum(parts[0].astype(F32), axis=0), jnp.sum(parts[2].astype(F32), axis=0)])
        gradient = d_mid + d_x_rows * squash_slope(inputs, limits[0])
        big_list[level] = (g_qkv, g_out, g_up, g_down)
        rep_list[level] = jnp.stack([d_out_bias, d_down_bias, d_gain_mid, d_shift_mid, d_gain_out, d_shift_out])
        shard_list[level] = (d_qv_bias, d_up_bias)

    rep = jnp.stack(rep_list)
    peaks = jnp.stack(peak_list)
    for bit in bits_of(tp_count):
        rep = rep + swap(rep, "tp", bit)
        peaks = jnp.maximum(peaks, swap(peaks, "tp", bit))
    qv_sum = jnp.stack([item[0] for item in shard_list])
    up_sum = jnp.stack([item[1] for item in shard_list])
    sizes = [rep.size, qv_sum.size, up_sum.size]
    pack = jnp.concatenate([rep.reshape(-1), qv_sum.reshape(-1), up_sum.reshape(-1)])
    for bit in dp_bits:
        pack = pack + swap(pack, "dp", bit)
        peaks = jnp.maximum(peaks, swap(peaks, "dp", bit))
    rep = pack[: sizes[0]].reshape(rep.shape)
    qv_sum = pack[sizes[0] : sizes[0] + sizes[1]].reshape(qv_sum.shape)
    up_sum = pack[sizes[0] + sizes[1] :].reshape(up_sum.shape)
    grads = [jnp.stack([entry[item] for entry in big_list]) for item in range(4)]
    return (
        output,
        gradient,
        grads[0],
        qv_sum,
        grads[1],
        rep[:, 0],
        grads[2],
        up_sum,
        grads[3],
        rep[:, 1],
        rep[:, 2:],
        peaks,
    )


ERF_TOP = (
    -2.72614225801306e-10, 2.77068142495902e-08, -2.10102402082508e-06, -5.69250639462346e-05,
    -7.34990630326855e-04, -2.95459980854025e-03, -1.60960333262415e-02,
)
ERF_LOW = (
    -1.45660718464996e-05, -2.13374055278905e-04, -1.68282697438203e-03, -7.37332916720468e-03,
    -1.42647390514189e-02,
)


def erf_ratio(value):
    value = jnp.clip(value, -4.0, 4.0)
    square = value * value
    top = ERF_TOP[0]
    for factor in ERF_TOP[1:]:
        top = top * square + factor
    low = ERF_LOW[0]
    for factor in ERF_LOW[1:]:
        low = low * square + factor
    return value * top / low


def whole(shape):
    return pl.BlockSpec(shape, lambda *_: (0,) * len(shape))


SMEM = pl.BlockSpec(memory_space=pltpu.SMEM)


def cost(*_):
    return pl.CostEstimate(flops=1, bytes_accessed=1, transcendentals=0)


def params(mib=56):
    return pltpu.CompilerParams(vmem_limit_bytes=mib << 20)


def shaped(shape, dtype):
    return jax.ShapeDtypeStruct(shape, dtype)


class Line:
    mark = None
    free = False


def launch(
    kernel, *, out_shape, in_specs=(), out_specs=(), grid=None, grid_spec=None, scratch_shapes=(),
    input_output_aliases=None, compiler_params=None, cost_estimate=None, far_ins=(), far_outs=(),
):
    single = not isinstance(out_shape, (list, tuple))
    outs = [out_shape] if single else list(out_shape)
    if grid_spec is None:
        scalars, scratch = 0, list(scratch_shapes)
        ins_list, outs_list = list(in_specs), [out_specs] if single else list(out_specs)
    else:
        scalars, grid, scratch = grid_spec.num_scalar_prefetch, grid_spec.grid, list(grid_spec.scratch_shapes)
        ins_list, outs_list = list(grid_spec.in_specs), list(grid_spec.out_specs)

    def called(*args):
        marks = [] if Line.mark is None else [Line.mark]
        args = [
            pltpu.with_memory_space_constraint(item, pltpu.HBM) if place - scalars in far_ins else item
            for place, item in enumerate(args)
        ]
        first = scalars + len(ins_list)

        def body(*refs):
            refs = list(refs)
            del refs[first : first + len(marks)]
            del refs[first + len(outs)]
            kernel(*refs)

        anywhere = pl.BlockSpec(memory_space=pl.ANY)
        spec = pltpu.PrefetchScalarGridSpec(
            num_scalar_prefetch=scalars,
            grid=grid,
            in_specs=ins_list + [anywhere] * len(marks),
            out_specs=outs_list + [anywhere],
            scratch_shapes=scratch,
        )
        results = pl.pallas_call(
            body,
            out_shape=[
                pltpu.HBM(item.shape, item.dtype) if place in far_outs else item for place, item in enumerate(outs)
            ]
            + [shaped((8, 128), F32)],
            grid_spec=spec,
            input_output_aliases=input_output_aliases or {},
            compiler_params=compiler_params,
            cost_estimate=cost_estimate,
        )(*args, *marks)
        if not Line.free:
            Line.mark = results[-1]
        return results[0] if single else list(results[:-1])

    return called


def tops_kernel(count, *refs):
    weights, out_ref, scratch = refs[:count], refs[count], refs[count + 1 :]
    step = pl.program_id(0)
    for item in range(count):
        block = jnp.abs(weights[item][...])
        part = jnp.max(block.reshape(-1, 16, block.shape[-1]), axis=0)

        @pl.when(step == 0)
        def _():
            scratch[item][...] = part

        @pl.when(step > 0)
        def _():
            scratch[item][...] = jnp.maximum(scratch[item][...], part)

    @pl.when(step == pl.num_programs(0) - 1)
    def _():
        for item in range(count):
            top = jnp.max(scratch[item][...].astype(F32), axis=0, keepdims=True)
            top = jnp.max(top, axis=1, keepdims=True)
            out_ref[item : item + 1, :] = jnp.broadcast_to(top, (1, 128))


def row_specs(level, weights, steps, layered):
    specs = []
    for weight in weights:
        rows = weight.shape[-2] // steps
        if weight.ndim == 4 and layered:
            specs.append(pl.BlockSpec((1, weight.shape[1], rows, weight.shape[3]), lambda s: (level, 0, s, 0)))
        elif weight.ndim == 4:
            specs.append(pl.BlockSpec((weight.shape[1], rows, weight.shape[3]), lambda s: (0, s, 0)))
        elif layered:
            specs.append(pl.BlockSpec((1, rows, weight.shape[2]), lambda s: (level, s, 0)))
        else:
            specs.append(pl.BlockSpec((rows, weight.shape[2]), lambda s: (s, 0)))
    return specs


def weight_tops_of(level, weights):
    steps = 2
    return launch(
        functools.partial(tops_kernel, len(weights)),
        out_shape=shaped((len(weights), 128), F32),
        grid=(steps,),
        in_specs=row_specs(level, weights, steps, True),
        out_specs=whole((len(weights), 128)),
        scratch_shapes=[pltpu.VMEM((16, weight.shape[-1]), BF16) for weight in weights],
        compiler_params=params(24),
        cost_estimate=cost(),
        far_ins=range(len(weights)),
    )(*weights)


def top_of(tops, item):
    top = tops[0][item : item + 1, 0:1]
    for ref in tops[1:]:
        top = jnp.maximum(top, ref[item : item + 1, 0:1])
    return top


def squash_kernel(count, first, t0, t1, t2, t3, *refs):
    for item in range(count):
        top = top_of((t0, t1, t2, t3), first + item)
        value = refs[item][0].astype(F32)
        refs[count + item][...] = (top * jnp.tanh(value * (1.0 / top))).astype(BF16)


def squash_weights(level, tops, first, weights):
    steps = 2
    return launch(
        functools.partial(squash_kernel, len(weights), first),
        out_shape=[shaped(weight.shape[1:], BF16) for weight in weights],
        grid=(steps,),
        in_specs=[whole(tops[0].shape)] * 4 + row_specs(level, weights, steps, True),
        out_specs=row_specs(level, weights, steps, False),
        compiler_params=params(24),
        cost_estimate=cost(),
        far_ins=range(4, 8),
    )(*tops, *weights)


def slope_kernel(sets, rows_of, place_ref, *refs):
    tops, (qkv_ref, out_ref, up_ref, down_ref), targets = refs[: 4 * sets], refs[4 * sets : 4 * sets + 4], refs[-3:]

    def slope(value, item):
        group, row = rows_of[item]
        tanh = jnp.tanh(value.astype(F32) * (1.0 / top_of(tops[4 * group : 4 * group + 4], row)))
        return 1.0 - tanh * tanh

    targets[0][...] = slope(down_ref[0], 3)
    targets[1][...] = slope(up_ref[0], 2)
    local = qkv_ref.shape[3]
    for part in range(3):
        targets[2][:, part * local : (part + 1) * local] = slope(qkv_ref[0, part], 0)
    piece = slope(out_ref[0], 1)
    span = piece.shape[0]
    rows = targets[2].shape[0]
    side = piece.shape[1] * span // rows
    for item in range(rows // span):
        targets[2][item * span : (item + 1) * span, 3 * local :] = piece[:, item * side : (item + 1) * side]


def slope_pieces(level, place, tops, rows_of, weights):
    specs = []
    for weight in weights:
        rows = weight.shape[-2] // 8
        if weight.ndim == 4:
            specs.append(pl.BlockSpec((1, weight.shape[1], rows, weight.shape[3]), lambda s, p: (level, 0, p[0], 0)))
        else:
            specs.append(pl.BlockSpec((1, rows, weight.shape[2]), lambda s, p: (level, p[0], 0)))
    width = weights[2].shape[1]
    rows = width // 8
    outs = [shaped((rows, width), F32)] * 3
    return launch(
        functools.partial(slope_kernel, len(tops), rows_of),
        out_shape=outs,
        grid_spec=pltpu.PrefetchScalarGridSpec(
            num_scalar_prefetch=1,
            grid=(1,),
            in_specs=[whole(item.shape) for group in tops for item in group] + specs,
            out_specs=[whole(item.shape) for item in outs],
        ),
        compiler_params=params(12),
        cost_estimate=cost(0, 3 << 20, 1 << 19),
        far_ins=range(4 * len(tops), 4 * len(tops) + 4), far_outs=range(3),
    )(place, *[item for group in tops for item in group], *weights)


def valid_of(info_ref, rows, blocks):
    row = lax.broadcasted_iota(jnp.int32, (rows, 1), 0)
    columns = [(row + info_ref[block] < info_ref[4]).astype(F32) for block in blocks]
    return columns[0] if len(columns) == 1 else jnp.concatenate(columns, axis=0)


def key_bias_of(info_ref, rows):
    lane = lax.broadcasted_iota(jnp.int32, (1, rows), 1)
    return jnp.concatenate(
        [jnp.where(lane + info_ref[block] < info_ref[4], 0.0, -1000000000.0) for block in range(4)], axis=1
    )


def attn_forward_kernel(level, info_ref, limits_ref, x0, x1, x2, x3, w_ref, bias_ref, out_w_ref,
                        qkv_ref, ctx_ref, low_ref, peak_ref, send_ref, keep_ref, x_ref):
    rows = x0.shape[0]
    for place, piece in enumerate((x0, x1, x2, x3)):
        x_ref[place * rows : (place + 1) * rows, :] = piece[...]
    x = x_ref[...]
    for part in range(3):
        total = mm(x, w_ref[part])
        if part != 1:
            total = total + bias_ref[level, part // 2 : part // 2 + 1, :].astype(F32)
        qkv_ref[part] = total.astype(BF16)
    limit = limits_ref[level, 1]
    key_bias = key_bias_of(info_ref, rows)
    inverse = 1.0 / limit

    def heads(two, carry):
        lanes = pl.ds(pl.multiple_of(two * 2 * HD, 2 * HD), 2 * HD)
        queries, keys, values = qkv_ref[0, :, lanes], qkv_ref[1, :, lanes], qkv_ref[2, :, lanes]
        both = []
        for here in (slice(0, HD), slice(HD, 2 * HD)):
            scores = mm_t(queries[:, here], keys[:, here]) * (HD**-0.5) + key_bias
            scores = jnp.exp(scores - jnp.max(scores, axis=-1, keepdims=True))
            probs = (scores * (1.0 / jnp.sum(scores, axis=-1, keepdims=True))).astype(BF16)
            both.append(mm(probs, values[:, here]))
        ctx_ref[:, lanes] = jnp.concatenate(both, axis=1)
        return carry

    lax.fori_loop(0, qkv_ref.shape[2] // (2 * HD), heads, 0, unroll=True)
    context = ctx_ref[...]
    peak_ref[...] = jnp.max(jnp.abs(context) * valid_of(info_ref, rows, (0, 1, 2, 3)), axis=0, keepdims=True)
    low = (limit * jnp.tanh(context * inverse)).astype(BF16)
    low_ref[...] = low
    half = low.shape[0] // 2
    send_ref[...] = mm(low[half:], out_w_ref[...]).astype(BF16)
    keep_ref[...] = mm(low[:half], out_w_ref[...])


def attn_forward(level, info, limits, pieces, w_qkv, bias, w_out):
    rows, width = pieces[0].shape
    total = 4 * rows
    local = w_out.shape[0]
    ins = (info, limits, *pieces, w_qkv, bias, w_out)
    outs = [
        shaped((3, total, local), BF16),
        shaped((total, local), F32),
        shaped((total, local), BF16),
        shaped((1, local), F32),
        shaped((total // 2, width), BF16),
        shaped((total // 2, width), F32),
    ]
    return launch(
        functools.partial(attn_forward_kernel, level),
        out_shape=outs,
        in_specs=[SMEM, SMEM] + [whole(item.shape) for item in ins[2:]],
        out_specs=[whole(item.shape) for item in outs],
        scratch_shapes=[pltpu.VMEM((total, width), BF16)],
        grid=(1,),
        compiler_params=params(28),
        cost_estimate=cost(5e9, 8 << 20, 1 << 20),
        far_outs=(0, 1, 2),
    )(*ins)


def two_pieces(step, pieces, both_ref):
    rows = pieces[0].shape[0]
    for half in range(2):

        @pl.when(step == half)
        def _():
            both_ref[:rows] = pieces[2 * half][...]
            both_ref[rows:] = pieces[2 * half + 1][...]


def ffn_forward_kernel(level, info_ref, limits_ref, x0, x1, x2, x3, up_w_ref, bias_ref, down_w_ref,
                       low_ref, slope_ref, peak_ref, send_ref, keep_ref, both_ref, up_ref):
    step = pl.program_id(0)
    limit = limits_ref[level, 3]
    inverse = 1.0 / limit
    two_pieces(step, (x0, x1, x2, x3), both_ref)
    up_ref[...] = mm(both_ref[...], up_w_ref[...]) + bias_ref[level : level + 1, :].astype(F32)
    chunk = 64
    rows = x0.shape[0]

    def part(item, peak):
        here = pl.ds(pl.multiple_of(item * chunk, chunk), chunk)
        up = up_ref[here, :]
        cdf = 0.5 + 0.5 * erf_ratio(up * (0.5**0.5))
        active = up * cdf
        tanh = jnp.tanh(active * inverse)
        low_ref[here, :] = (limit * tanh).astype(BF16)
        slope_ref[here, :] = (1.0 - tanh * tanh) * (cdf + up * jnp.exp(-0.5 * up * up) * 0.3989422804014327)
        place = lax.broadcasted_iota(jnp.int32, (chunk, 1), 0) + item * chunk % rows
        inside = place + info_ref[2 * step + item * chunk // rows] < info_ref[4]
        size = jnp.where(inside, jnp.abs(active), 0.0)
        return jnp.maximum(peak, jnp.max(size.reshape(-1, 8, size.shape[1]), axis=0))

    peak = lax.fori_loop(0, 2 * rows // chunk, part, jnp.zeros((8, up_ref.shape[1]), F32))
    peak = jnp.max(peak, axis=0, keepdims=True)
    peak_ref[...] = jnp.where(step == 0, peak, jnp.maximum(peak_ref[...], peak))
    total = mm(low_ref[...], down_w_ref[...])

    @pl.when(step == 0)
    def _():
        keep_ref[...] = total

    @pl.when(step == 1)
    def _():
        send_ref[...] = total.astype(BF16)


def ffn_forward(level, info, limits, pieces, w_up, bias, w_down):
    rows, width = pieces[0].shape
    units = w_up.shape[1]
    total = 4 * rows
    outs = [
        shaped((total, units), BF16),
        shaped((total, units), F32),
        shaped((1, units), F32),
        shaped((total // 2, width), BF16),
        shaped((total // 2, width), F32),
    ]
    return launch(
        functools.partial(ffn_forward_kernel, level),
        out_shape=outs,
        grid=(2,),
        in_specs=[SMEM, SMEM]
        + [whole((rows, width))] * 4
        + [whole(w_up.shape), whole(bias.shape), whole(w_down.shape)],
        out_specs=[
            pl.BlockSpec((2 * rows, units), lambda s: (s, 0)),
            pl.BlockSpec((2 * rows, units), lambda s: (s, 0)),
            whole((1, units)),
            whole((2 * rows, width)),
            whole((2 * rows, width)),
        ],
        scratch_shapes=[pltpu.VMEM((2 * rows, width), BF16), pltpu.VMEM((2 * rows, units), F32)],
        compiler_params=params(32),
        cost_estimate=cost(8e9, 12 << 20, 2 << 20),
        far_outs=(0, 1),
    )(info, limits, *pieces, w_up, bias, w_down)


def enter_kernel(info_ref, limits_ref, tokens_ref, low_ref, peak_ref):
    value = tokens_ref[...].astype(F32)
    limit = limits_ref[0, 0]
    low_ref[...] = (limit * jnp.tanh(value * (1.0 / limit))).astype(BF16)
    peak_ref[...] = jnp.max(jnp.abs(value) * valid_of(info_ref, value.shape[0], (0,)), axis=0, keepdims=True)


def enter(info, limits, tokens):
    outs = [shaped(tokens.shape, BF16), shaped((1, tokens.shape[1]), F32)]
    return launch(
        enter_kernel,
        out_shape=outs,
        grid=(1,),
        in_specs=[SMEM, SMEM, whole(tokens.shape)],
        out_specs=[whole(item.shape) for item in outs],
        compiler_params=params(8),
        cost_estimate=cost(),
    )(info, limits, tokens)


def join_kernel(level, item, last, info_ref, limits_ref, base_ref, keep_ref, core_ref, far_ref, bias_ref, norm_ref,
                *outs):
    arrived = keep_ref[...] + core_ref[...].astype(F32) + far_ref[...].astype(F32)
    unit, scale = norm_parts(base_ref[...].astype(F32) + arrived + bias_ref[level : level + 1, :].astype(F32))
    value = unit * norm_ref[level, item : item + 1, :] + norm_ref[level, item + 1 : item + 2, :]
    outs[0][...] = unit
    outs[1][...] = scale
    if last:
        outs[2][...] = value.astype(BF16)
    else:
        outs[2][...] = value
        limit = limits_ref[level, 2] if item == 0 else limits_ref[level + 1, 0]
        outs[3][...] = (limit * jnp.tanh(value * (1.0 / limit))).astype(BF16)
        peak = jnp.abs(value) * valid_of(info_ref, value.shape[0], (0,))
        outs[4][...] = jnp.max(peak, axis=0, keepdims=True)


def join_rows(level, item, last, info, limits, base, keep, core, far, bias, norm):
    rows, width = base.shape
    outs = [shaped((rows, width), F32), shaped((rows, 1), F32)]
    if last:
        outs += [shaped((rows, width), BF16)]
    else:
        outs += [shaped((rows, width), F32), shaped((rows, width), BF16), shaped((1, width), F32)]
    block = whole((rows, width))
    return launch(
        functools.partial(join_kernel, level, item, last),
        out_shape=outs,
        grid=(1,),
        in_specs=[SMEM, SMEM, block, block, block, block, whole(bias.shape), whole(norm.shape)],
        out_specs=[whole(item.shape) for item in outs],
        compiler_params=params(12),
        cost_estimate=cost(),
        far_outs=(),
    )(info, limits, base, keep, core, far, bias, norm)


def norm_back_store(gradient, unit_ref, scale_ref, gain, d_ref, low_ref, sums_ref):
    unit = unit_ref[...]
    scaled = gradient * gain
    first = jnp.mean(scaled, axis=-1, keepdims=True)
    second = jnp.mean(scaled * unit, axis=-1, keepdims=True)
    d_values = scale_ref[...] * (scaled - first - unit * second)
    low = d_values.astype(BF16)
    d_ref[...] = d_values
    low_ref[...] = low
    sums_ref[0:1, :] = jnp.sum(low.astype(F32), axis=0, keepdims=True)
    sums_ref[1:2, :] = jnp.sum(gradient * unit, axis=0, keepdims=True)
    sums_ref[2:3, :] = jnp.sum(gradient, axis=0, keepdims=True)


def top_back_kernel(level, info_ref, cot_ref, unit_ref, scale_ref, norm_ref, d_ref, low_ref, sums_ref):
    gradient = cot_ref[...].astype(F32) * valid_of(info_ref, cot_ref.shape[0], (0,))
    norm_back_store(gradient, unit_ref, scale_ref, norm_ref[level, 2:3, :], d_ref, low_ref, sums_ref)


def mid_back_kernel(level, item, limits_ref, base_ref, keep_ref, core_ref, far_ref, unit_ref, scale_ref, norm_ref,
                    d_ref, low_ref, sums_ref):
    arrived = keep_ref[...] + core_ref[...].astype(F32) + far_ref[...].astype(F32)
    gain = norm_ref[level, item : item + 1, :]
    value = unit_ref[...] * gain + norm_ref[level, item + 1 : item + 2, :]
    limit = limits_ref[level, 2] if item == 0 else limits_ref[level + 1, 0]
    tanh = jnp.tanh(value * (1.0 / limit))
    gradient = base_ref[...] + arrived * (1.0 - tanh * tanh)
    norm_back_store(gradient, unit_ref, scale_ref, gain, d_ref, low_ref, sums_ref)


def end_back_kernel(limits_ref, base_ref, keep_ref, core_ref, far_ref, x_ref, out_ref):
    arrived = keep_ref[...] + core_ref[...].astype(F32) + far_ref[...].astype(F32)
    tanh = jnp.tanh(x_ref[...].astype(F32) * (1.0 / limits_ref[0, 0]))
    out_ref[...] = base_ref[...] + arrived * (1.0 - tanh * tanh)


def top_back(level, info, cotangent, unit, scale, norm):
    rows, width = unit.shape
    outs = [shaped((rows, width), F32), shaped((rows, width), BF16), shaped((3, width), F32)]
    ins = (cotangent, unit, scale, norm)
    return launch(
        functools.partial(top_back_kernel, level),
        out_shape=outs,
        grid=(1,),
        in_specs=[SMEM] + [whole(item.shape) for item in ins],
        out_specs=[whole(item.shape) for item in outs],
        compiler_params=params(12),
        cost_estimate=cost(),
        far_ins=(1, 2, 3),
    )(info, *ins)


def mid_back(level, item, limits, base, keep, core, far, unit, scale, norm):
    rows, width = unit.shape
    outs = [shaped((rows, width), F32), shaped((rows, width), BF16), shaped((3, width), F32)]
    block = whole((rows, width))
    return launch(
        functools.partial(mid_back_kernel, level, item),
        out_shape=outs,
        grid=(1,),
        in_specs=[SMEM, block, block, block, block, block, whole(scale.shape), whole(norm.shape)],
        out_specs=[whole(item.shape) for item in outs],
        compiler_params=params(12),
        cost_estimate=cost(),
        far_ins=(), far_outs=(),
    )(limits, base, keep, core, far, unit, scale, norm)


def end_back(limits, base, keep, core, far, x):
    block = whole(base.shape)
    return launch(
        end_back_kernel,
        out_shape=shaped(base.shape, F32),
        grid=(1,),
        in_specs=[SMEM] + [block] * 5,
        out_specs=block,
        compiler_params=params(12),
        cost_estimate=cost(),
    )(limits, base, keep, core, far, x)


def ffn_backward_kernel(g0, g1, g2, g3, down_w_ref, slope_ref, up_w_ref, grad_ref, sum_ref, send_ref, keep_ref,
                        both_ref):
    step = pl.program_id(0)
    two_pieces(step, (g0, g1, g2, g3), both_ref)
    grad = (mm_t(both_ref[...], down_w_ref[...]) * slope_ref[...]).astype(BF16)
    grad_ref[...] = grad
    part = jnp.sum(grad.astype(F32), axis=0, keepdims=True)
    sum_ref[...] = jnp.where(step == 0, part, sum_ref[...] + part)
    total = mm_t(grad, up_w_ref[...])

    @pl.when(step == 0)
    def _():
        keep_ref[...] = total

    @pl.when(step == 1)
    def _():
        send_ref[...] = total.astype(BF16)


def ffn_backward(pieces, w_down, slope, w_up):
    rows, width = pieces[0].shape
    units = w_up.shape[1]
    total = 4 * rows
    outs = [
        shaped((total, units), BF16),
        shaped((1, units), F32),
        shaped((total // 2, width), BF16),
        shaped((total // 2, width), F32),
    ]
    return launch(
        ffn_backward_kernel,
        out_shape=outs,
        grid=(2,),
        in_specs=[whole((rows, width))] * 4
        + [whole(w_down.shape), pl.BlockSpec((2 * rows, units), lambda s: (s, 0)), whole(w_up.shape)],
        out_specs=[
            pl.BlockSpec((2 * rows, units), lambda s: (s, 0)),
            whole((1, units)),
            whole((2 * rows, width)),
            whole((2 * rows, width)),
        ],
        scratch_shapes=[pltpu.VMEM((2 * rows, width), BF16)],
        compiler_params=params(32),
        cost_estimate=cost(3e9, 12 << 20),
        far_ins=(4, 5, 6),
    )(*pieces, w_down, slope, w_up)


def attn_backward_kernel(level, info_ref, limits_ref, g0, g1, g2, g3, out_w_ref, ctx_ref, qkv_ref, w_ref,
                         grad_ref, sum_ref, send_ref, keep_ref, g_ref, cg_ref):
    rows = g0.shape[0]
    for place, piece in enumerate((g0, g1, g2, g3)):
        g_ref[place * rows : (place + 1) * rows, :] = piece[...]
    tanh = jnp.tanh(ctx_ref[...] * (1.0 / limits_ref[level, 1]))
    cg_ref[...] = (mm_t(g_ref[...], out_w_ref[...]) * (1.0 - tanh * tanh)).astype(BF16)
    key_bias = key_bias_of(info_ref, rows)
    local = cg_ref.shape[1]

    def heads(two, carry):
        start = pl.multiple_of(two * 2 * HD, 2 * HD)
        lanes = pl.ds(start, 2 * HD)
        pairs = qkv_ref[0, :, lanes], qkv_ref[1, :, lanes], qkv_ref[2, :, lanes], cg_ref[:, lanes]
        parts = [[], [], []]
        for here in (slice(0, HD), slice(HD, 2 * HD)):
            queries, keys, values, grad = [item[:, here] for item in pairs]
            scores = mm_t(queries, keys) * (HD**-0.5) + key_bias
            scores = jnp.exp(scores - jnp.max(scores, axis=-1, keepdims=True))
            probs = scores * (1.0 / jnp.sum(scores, axis=-1, keepdims=True))
            d_values = t_mm(probs.astype(BF16), grad)
            d_probs = mm_t(grad, values)
            inner = jnp.sum(probs * d_probs, axis=-1, keepdims=True)
            d_scores = (probs * (d_probs - inner)).astype(BF16)
            parts[0].append(mm(d_scores, keys) * (HD**-0.5))
            parts[1].append(t_mm(d_scores, queries) * (HD**-0.5))
            parts[2].append(d_values)
        for part in range(3):
            target = pl.ds(pl.multiple_of(part * local + start, 2 * HD), 2 * HD)
            grad_ref[:, target] = jnp.concatenate(parts[part], axis=1).astype(BF16)
        return carry

    lax.fori_loop(0, local // (2 * HD), heads, 0)
    sum_ref[0:1, :] = jnp.sum(grad_ref[:, :local].astype(F32), axis=0, keepdims=True)
    sum_ref[1:2, :] = jnp.sum(grad_ref[:, 2 * local :].astype(F32), axis=0, keepdims=True)
    half = g_ref.shape[0] // 2

    def back(first, last):
        total = mm_t(grad_ref[first:last, :local], w_ref[0])
        total += mm_t(grad_ref[first:last, local : 2 * local], w_ref[1])
        return total + mm_t(grad_ref[first:last, 2 * local :], w_ref[2])

    send_ref[...] = back(half, 2 * half).astype(BF16)
    keep_ref[...] = back(0, half)


def attn_backward(level, info, limits, pieces, w_out, context, qkv, w_qkv):
    rows, width = pieces[0].shape
    total = 4 * rows
    local = w_out.shape[0]
    ins = (info, limits, *pieces, w_out, context, qkv, w_qkv)
    outs = [
        shaped((total, 3 * local), BF16),
        shaped((2, local), F32),
        shaped((total // 2, width), BF16),
        shaped((total // 2, width), F32),
    ]
    return launch(
        functools.partial(attn_backward_kernel, level),
        out_shape=outs,
        grid=(1,),
        in_specs=[SMEM, SMEM] + [whole(item.shape) for item in ins[2:]],
        out_specs=[whole(item.shape) for item in outs],
        scratch_shapes=[pltpu.VMEM((total, width), BF16), pltpu.VMEM((total, local), BF16)],
        compiler_params=params(32),
        cost_estimate=cost(6e9, 8 << 20, 1 << 20),
        far_ins=(6, 7, 8, 9),
    )(*ins)


LINK_ORDERS = ((1, 2, 4), (2, 1, 4))
FFN_ORDERS = (0, 1)
ATTN_WHOLE = ((0,), ((0, 1024),))
ATTN_CUT = ((0, 1), ((0, 512), (512, 1024)))


def block_masks(bits):
    return [
        (bits[0] if item & 4 else 0) ^ (bits[1] if item & 2 else 0) ^ (bits[2] if item & 1 else 0)
        for item in range(8)
    ]


def halves(target_pair, item):
    send_ref, keep_ref = target_pair
    return keep_ref if item < 4 else send_ref


def ffn_grad_kernel(table_ref, low_ref, g0, g1, g2, g3, h0, h1, h2, h3, grad_ref, *refs):
    targets, total_ref = refs[:4], refs[4]
    block = total_ref.shape[0] // 8
    for part, order in enumerate(FFN_ORDERS):
        if part == 0:
            total_ref[...] = t_mm(low_ref[...], jnp.concatenate([g0[...], g1[...], g2[...], g3[...]], axis=0))
        else:
            total_ref[...] = t_mm(jnp.concatenate([h0[...], h1[...], h2[...], h3[...]], axis=0), grad_ref[...])
        for item in range(8):
            first = pl.multiple_of(table_ref[order, item] * block, block)
            target = halves(targets[2 * part : 2 * part + 2], item)
            target[item % 4] = total_ref[pl.ds(first, block), :].astype(target.dtype)


def ffn_grad(table, act_low, g_pieces, h_pieces, up_grad):
    ins = [act_low, *g_pieces, *h_pieces, up_grad]
    width = up_grad.shape[1]
    outs = [shaped((4, width // 8, width), dtype) for _ in FFN_ORDERS for dtype in (BF16, F32)]
    return launch(
        ffn_grad_kernel,
        out_shape=outs,
        grid_spec=pltpu.PrefetchScalarGridSpec(
            num_scalar_prefetch=1,
            grid=(1,),
            in_specs=[whole(item.shape) for item in ins],
            out_specs=[whole(item.shape) for item in outs],
            scratch_shapes=[pltpu.VMEM((width, width), F32)],
        ),
        compiler_params=params(34),
        cost_estimate=cost(),
        far_ins=(0, 5, 6, 7, 8), far_outs=range(4),
    )(table, *ins)


def attn_grad_kernel(plan, table_ref, x0, x1, x2, x3, grad_ref, low_ref, g0, g1, g2, g3, *refs):
    targets, total_ref, out_ref = refs[:-2], refs[-2], refs[-1]
    total_ref[...] = t_mm(jnp.concatenate([x0[...], x1[...], x2[...], x3[...]], axis=0), grad_ref[...])
    out_ref[...] = t_mm(low_ref[...], jnp.concatenate([g0[...], g1[...], g2[...], g3[...]], axis=0))
    block = total_ref.shape[0] // 8
    local3 = total_ref.shape[1]
    span = out_ref.shape[0] // 8
    side = out_ref.shape[1] * span // block
    for part, (order, (start, stop)) in enumerate(zip(*plan)):
        for item in range(8):
            target = halves(targets[2 * part : 2 * part + 2], item)
            if start < local3:
                end = min(stop, local3)
                first = pl.multiple_of(table_ref[order, item] * block, block)
                value = total_ref[pl.ds(first, block), start:end]
                target[item % 4, :, : end - start] = value.astype(target.dtype)
            if stop > local3:
                first = pl.multiple_of(table_ref[order, item] * span, span)
                taken = out_ref[pl.ds(first, span), :]
                for place in range(block // span):
                    target[item % 4, place * span : (place + 1) * span, local3 - start :] = taken[
                        :, place * side : (place + 1) * side
                    ].astype(target.dtype)


def attn_grad(plan, table, x_pieces, qkv_grad, ctx_low, g_pieces):
    ins = [*x_pieces, qkv_grad, ctx_low, *g_pieces]
    width = x_pieces[0].shape[1]
    outs = [shaped((4, width // 8, last - first), dtype) for first, last in plan[1] for dtype in (BF16, F32)]
    return launch(
        functools.partial(attn_grad_kernel, plan),
        out_shape=outs,
        grid_spec=pltpu.PrefetchScalarGridSpec(
            num_scalar_prefetch=1,
            grid=(1,),
            in_specs=[whole(item.shape) for item in ins],
            out_specs=[whole(item.shape) for item in outs],
            scratch_shapes=[
                pltpu.VMEM((width, qkv_grad.shape[1]), F32),
                pltpu.VMEM((ctx_low.shape[1], width), F32),
            ],
        ),
        compiler_params=params(30),
        cost_estimate=cost(),
        far_ins=(0, 1, 2, 3, 5), far_outs=range(6),
    )(table, *ins)


def fold_kernel(count, parts, scaled, *refs):
    outs = refs[-parts:]
    for part in range(parts):
        mine = refs[part * count : (part + 1) * count]
        total = mine[0][...]
        for other in mine[1:]:
            total = total + other[...].astype(F32)
        if scaled:
            total = total * refs[parts * count + part][...]
        outs[part][...] = total.astype(BF16)


def fold(size, parts, scales=None):
    ins, in_specs, outs, out_specs = [], [], [], []
    count = len(parts[0])
    blocks = max(size, 1)
    for arrays in parts:
        rest = arrays[0].shape[1:]
        for array in arrays:
            ins.append(array)
            place = 1 if size else 0
            in_specs.append(pl.BlockSpec((blocks, *rest), lambda s, place=place: (place, 0, 0)))
        outs.append(shaped((blocks, *rest), BF16))
        out_specs.append(whole((blocks, *rest)))
    if scales is not None:
        for scale, columns in scales:
            width = columns[1] - columns[0]
            ins.append(scale)
            in_specs.append(pl.BlockSpec((scale.shape[0], width), lambda s, at=columns[0] // width: (0, at)))
    return launch(
        functools.partial(fold_kernel, count, len(parts), scales is not None),
        out_shape=outs,
        grid=(1,),
        in_specs=in_specs,
        out_specs=out_specs,
        compiler_params=params(16),
        cost_estimate=cost(),
        far_ins=range(len(ins)), far_outs=range(len(outs)),
    )(*ins)


def pair_kernel(parts, *refs):
    for part in range(parts):
        first, second, target = refs[2 * part], refs[2 * part + 1], refs[2 * parts + part]
        half = first.shape[0]
        target[:half] = first[...]
        target[half:] = second[...]


def pair(firsts, seconds):
    ins = [item for both in zip(firsts, seconds) for item in both]
    outs = [shaped((2 * item.shape[0], *item.shape[1:]), BF16) for item in firsts]
    return launch(
        functools.partial(pair_kernel, len(firsts)),
        out_shape=outs,
        grid=(1,),
        in_specs=[whole(item.shape) for item in ins],
        out_specs=[whole(item.shape) for item in outs],
        compiler_params=params(12),
        cost_estimate=cost(),
        far_ins=range(len(ins)), far_outs=range(len(outs)),
    )(*ins)


def place_kernel(plan, table_ref, *refs):
    outs = refs[-2:]
    step = pl.program_id(0)

    def store(part, source, item):
        start, stop = plan[1][part]
        if len(outs[0].shape) == 3:
            outs[part][0] = source[item].astype(F32)
            return
        qkv_ref, out_ref = outs
        local = qkv_ref.shape[3]
        for column in range(start, min(stop, 3 * local), 128):
            target = slice(column % local, column % local + 128)
            qkv_ref[0, column // local, :, target] = source[item, :, column - start : column - start + 128].astype(F32)
        if stop > 3 * local:
            span = out_ref.shape[1]
            side = stop - 3 * local
            for place in range(source.shape[1] // span):
                out_ref[0, :, place * side : (place + 1) * side] = source[
                    item, place * span : (place + 1) * span, 3 * local - start :
                ].astype(F32)

    for part, order in enumerate(plan[0]):
        item = table_ref[order, step]
        pl.when(item < 4)(functools.partial(store, part, refs[2 * part], item))
        pl.when(item >= 4)(functools.partial(store, part, refs[2 * part + 1], item - 4))


def place_blocks(plan, table, level, nears, fars, shapes, earlier):
    specs = []
    for shape in shapes:
        if len(shape) == 4:
            specs.append(pl.BlockSpec((1, shape[1], shape[2] // 8, shape[3]), lambda s, t: (level, 0, s, 0)))
        else:
            specs.append(pl.BlockSpec((1, shape[1] // 8, shape[2]), lambda s, t: (level, s, 0)))
    ins = [item for both in zip(nears, fars) for item in both]
    earlier = list(earlier or [])
    return launch(
        functools.partial(place_kernel, plan),
        out_shape=[shaped(shape, F32) for shape in shapes],
        grid_spec=pltpu.PrefetchScalarGridSpec(
            num_scalar_prefetch=1,
            grid=(8,),
            in_specs=[whole(item.shape) for item in ins] + [pl.BlockSpec(memory_space=pl.ANY)] * len(earlier),
            out_specs=specs,
        ),
        input_output_aliases={1 + len(ins) + place: place for place in range(len(earlier))},
        compiler_params=params(24),
        cost_estimate=cost(),
        far_ins=range(len(ins)), far_outs=range(len(shapes)),
    )(table, *ins, *earlier)


def near_sum_kernel(keep_ref, near_ref, out_ref):
    out_ref[...] = (keep_ref[...] + near_ref[...].astype(F32)).astype(BF16)


def near_sum(keep, near):
    rows, width = keep.shape[0] // 2, keep.shape[1]
    second = pl.BlockSpec((rows, width), lambda s: (1, 0))
    return launch(
        near_sum_kernel,
        out_shape=shaped((rows, width), BF16),
        grid=(1,),
        in_specs=[second, second],
        out_specs=whole((rows, width)),
        compiler_params=params(8),
        cost_estimate=cost(),
    )(keep, near)


def pack_kernel(layers, *refs):
    out_ref = refs[-1]
    row = 0
    for layer in range(layers):
        mid, out = refs[2 * layer], refs[2 * layer + 1]
        for source in (mid[0:1, :], out[0:1, :], mid[1:3, :], out[1:3, :]):
            out_ref[row : row + source.shape[0], :] = source
            row += source.shape[0]
    out_ref[row : row + 1, :] = refs[-2][...]


def pack(sums, peaks):
    ins = [item for both in sums for item in both] + [peaks]
    out = shaped((6 * len(sums) + 1, peaks.shape[1]), F32)
    return launch(
        functools.partial(pack_kernel, len(sums)),
        out_shape=out,
        grid=(1,),
        in_specs=[whole(item.shape) for item in ins],
        out_specs=whole(out.shape),
        compiler_params=params(8),
        cost_estimate=cost(),
    )(*ins)


def merge_kernel(peak_row, more, mine_ref, other_ref, *refs):
    out_ref = refs[-1]
    mine, other = mine_ref[...], other_ref[...]
    row = lax.broadcasted_iota(jnp.int32, mine.shape, 0)
    merged = jnp.where(row == peak_row, jnp.maximum(mine, other), mine + other)
    if not more:
        out_ref[...] = merged
        return
    count = mine.shape[0]
    out_ref[:count, :] = merged
    for item in range(more):
        up_ref, qv_ref = refs[2 * item], refs[2 * item + 1]
        out_ref[count + item : count + item + 1, :] = up_ref[...]
        local = qv_ref.shape[1]
        for part in range(2):
            start = (2 * item + part) * local
            out_ref[count + more : count + more + 1, start : start + local] = qv_ref[part : part + 1, :]


def merge(peak_row, mine, other, shards=()):
    ins = [mine, other] + [item for both in shards for item in both]
    rows = mine.shape[0] + (len(shards) + 1 if shards else 0)
    return launch(
        functools.partial(merge_kernel, peak_row, len(shards)),
        out_shape=shaped((rows, mine.shape[1]), F32),
        grid=(1,),
        in_specs=[whole(item.shape) for item in ins],
        out_specs=whole((rows, mine.shape[1])),
        compiler_params=params(8),
        cost_estimate=cost(),
    )(*ins)


def peaks_kernel(*refs):
    out_ref = refs[-1]
    for item, ref in enumerate(refs[:-1]):
        top = jnp.max(ref[...], axis=1, keepdims=True)
        out_ref[0:1, item * 128 : (item + 1) * 128] = jnp.broadcast_to(top, (1, 128))


def peaks_row(rows):
    return launch(
        peaks_kernel,
        out_shape=shaped((1, 128 * len(rows)), F32),
        grid=(1,),
        in_specs=[whole(item.shape) for item in rows],
        out_specs=whole((1, 128 * len(rows))),
        compiler_params=params(8),
        cost_estimate=cost(0, 1 << 16),
    )(*rows)


STEPS = {
    "M41": ("F1",),
    "M20": ("F1",),
    "M31": (),
    "M30": (),
    "WT0": (),
    "end0": (),
}


def fast_on_device(
    tokens,
    cotangent,
    lengths,
    qkv_weight,
    qv_bias,
    out_weight,
    out_bias,
    up_weight,
    up_bias,
    down_weight,
    down_bias,
    norm_params,
    act_ranges,
):
    row_count, width = tokens.shape
    tp_count = lax.axis_size("tp")
    rank = lax.axis_index("tp")
    place = lax.axis_index("dp")
    layers = qkv_weight.shape[0]
    local = qkv_weight.shape[3]
    order = jnp.array(block_order(tp_count), jnp.int32)
    info = jnp.concatenate([(rank ^ order) * row_count, lengths])
    qkv_blocks = jnp.transpose(qkv_weight, (0, 2, 1, 3))
    weights = (qkv_blocks, out_weight, up_weight, down_weight)
    core_bit, far_bit = bits_of(tp_count)
    place_list = place[None].astype(jnp.int32)
    Line.mark = None
    Line.free = False

    def run(step, *values):
        return step(*values)

    def spread(rows):
        return rows, swap(rows, "tp", far_bit), swap(rows, "tp", core_bit)

    def finish(begun):
        rows, far, near = begun
        far, _ = lax.optimization_barrier((far, Line.mark))
        return (rows, far, near, swap(far, "tp", core_bit))

    def gather_sum(send, keep):
        near = swap(send, "tp", core_bit)
        return near, swap(near_sum(keep, near), "tp", far_bit)

    x_low, x_peak = run(enter, info, act_ranges, tokens)
    x_begun = spread(x_low)
    low_weights = [dict() for _ in range(layers)]
    names = ("qkv", "out", "up", "down")
    sets = {}

    def find_tops(level, first, last):
        mine = weight_tops_of(level, weights[first:last])
        others = [swap(mine, "tp", bit) for bit in (core_bit, far_bit, core_bit | far_bit)]
        sets[level, first] = (mine, *others)

    def squash_some(level, origin, first, last):
        outs = squash_weights(level, sets[level, origin], first - origin, weights[first:last])
        for name, out in zip(names[first:last], outs):
            low_weights[level][name] = out

    find_tops(0, 0, 2)
    find_tops(0, 2, 4)
    squash_some(0, 0, 0, 2)
    slopes = [None] * layers
    kept = []
    peak_rows = []
    current = tokens
    for level in range(layers):
        low = low_weights[level]
        last = level == layers - 1
        x_pieces = finish(x_begun)
        qkv, context, ctx_low, ctx_peak, send, keep = run(
            lambda pieces, w_qkv, w_out: attn_forward(level, info, act_ranges, pieces, w_qkv, qv_bias, w_out),
            x_pieces, low["qkv"], low["out"],
        )
        near, far = gather_sum(send, keep)
        if level == 0:
            squash_some(0, 2, 2, 4)
        else:
            squash_some(1, 0, 2, 4)
        mid_unit, mid_scale, hidden, hid_low, hid_peak = run(
            lambda *t: join_rows(level, 0, False, info, act_ranges, *t, out_bias, norm_params),
            current, keep, near, far,
        )
        h_begun = spread(hid_low)
        if level == 0:
            find_tops(1, 0, 4)
        h_pieces = finish(h_begun)
        act_low, slope, act_peak, send, keep = run(
            lambda pieces, w_up, w_down: ffn_forward(level, info, act_ranges, pieces, w_up, up_bias, w_down),
            h_pieces, low["up"], low["down"],
        )
        near, far = gather_sum(send, keep)
        if level == 0:
            squash_some(1, 0, 0, 2)
        else:
            slopes[1] = slope_pieces(1, place_list, [sets[1, 0]], ((0, 0), (0, 1), (0, 2), (0, 3)), weights)
            slopes[0] = slope_pieces(
                0, place_list, [sets[0, 0], sets[0, 2]], ((0, 0), (0, 1), (1, 0), (1, 1)), weights
            )
            peak_rows.append([x_peak, ctx_peak, hid_peak, act_peak])
            peaks = run(lambda *t: peaks_row(t), *peak_rows[0], *peak_rows[1])
        result = run(
            lambda *t: join_rows(level, 2, last, info, act_ranges, *t, down_bias, norm_params),
            hidden, keep, near, far,
        )
        peak_rows.append([x_peak, ctx_peak, hid_peak, act_peak])
        kept.append(
            dict(
                x=x_pieces, qkv=qkv, context=context, ctx_low=ctx_low, mid_unit=mid_unit, mid_scale=mid_scale,
                h=h_pieces, act_low=act_low, slope=slope, out_unit=result[0], out_scale=result[1], **{
                    "w_" + name: value for name, value in low.items()
                },
            )
        )
        if last:
            output = result[2]
        else:
            current, x_low, x_peak = result[2:]
            x_begun = spread(x_low)

    masks = [block_masks(bits) for bits in LINK_ORDERS]
    table = place ^ jnp.array(masks, jnp.int32)
    inverse = jnp.array([[row.index(item) for item in range(8)] for row in masks], jnp.int32)
    inverse = jnp.take(inverse, place ^ jnp.arange(8), axis=1)
    finished = {"ffn": None, "attn": None}
    shapes = {"ffn": [down_weight.shape, up_weight.shape], "attn": [qkv_blocks.shape, out_weight.shape]}

    full = (0, width)
    plans = {
        "ffn1": (FFN_ORDERS, (full, full)), "ffn0": (FFN_ORDERS, (full, full)), "attn1": ATTN_WHOLE, "attn0": ATTN_CUT,
    }

    def stream(level, name, outs):
        plan = plans[name + str(level)]

        key = {"ffn": "F", "attn": "T"}[name] + str(level)

        def swap_parts(parts, step):
            flying[key] = [swap(item, "dp", LINK_ORDERS[order][step]) for item, order in zip(parts, plan[0])]
            return flying[key]

        moved = [list(outs[1::2]), swap_parts(outs[0::2], 0)]
        yield
        moved.append(swap_parts(fold(2, list(zip(*moved))), 1))
        yield
        moved.append(swap_parts(fold(1, list(zip(*moved))), 2))
        yield
        scales = slopes[level][:2] if name == "ffn" else [slopes[level][2]] * len(plan[0])
        pieces = fold(0, list(zip(*moved)), list(zip(scales, plan[1])))
        for step in (2, 1):
            others = swap_parts(pieces, step)
            yield
            pieces = pair(pieces, others)
        others = swap_parts(pieces, 0)
        yield
        finished[name] = place_blocks(plan, inverse, level, pieces, others, shapes[name], finished[name])
        yield

    streams, flying = {}, {}

    def begin(level, name, outs):
        streams[{"ffn": "F", "attn": "T"}[name] + str(level)] = stream(level, name, outs)
        next(streams[{"ffn": "F", "attn": "T"}[name] + str(level)])

    def go(point, level):
        for item in STEPS.get(point + str(level), ()):
            next(streams[item])

    def back_norm(level, base, keep, near, far):
        return run(
            lambda *t: mid_back(level, 0, act_ranges, *t, norm_params),
            base, keep, near, far, kept[level]["mid_unit"], kept[level]["mid_scale"],
        )

    rep_list = [None] * layers
    shard_list = [None] * layers
    top = layers - 1
    d_final, down_grad, sums_out = run(
        lambda *t: top_back(top, info, cotangent, *t, norm_params),
        kept[top]["out_unit"], kept[top]["out_scale"],
    )
    g_begun = spread(down_grad)
    for level in reversed(range(layers)):
        saved = kept[level]
        go("M4", level + 1)
        g_pieces = finish(g_begun)
        up_grad, up_sum, send, keep = run(
            ffn_backward, g_pieces, saved["w_down"], saved["slope"], saved["w_up"]
        )
        near, far = gather_sum(send, keep)
        begin(
            level, "ffn", run(lambda *t: ffn_grad(table, *t), saved["act_low"], g_pieces, saved["h"], up_grad)
        )
        go("WF", level)
        d_mid, out_grad, sums_mid = back_norm(level, d_final, keep, near, far)
        o_begun = spread(out_grad)
        go("M2", level)
        o_pieces = finish(o_begun)
        qkv_grad, qv_sum, send, keep = run(
            lambda *t: attn_backward(level, info, act_ranges, *t),
            o_pieces, saved["w_out"], saved["context"], saved["qkv"], saved["w_qkv"],
        )
        near, far = gather_sum(send, keep)
        begin(
            level, "attn",
            run(lambda *t: attn_grad(plans["attn" + str(level)], table, *t), saved["x"], qkv_grad, saved["ctx_low"], o_pieces),
        )
        go("WT", level)
        rep_list[level] = (sums_mid, sums_out)
        shard_list[level] = (up_sum, qv_sum)
        if level > 0:
            below = kept[level - 1]
            d_final, down_grad, sums_out = run(
                lambda *t: mid_back(level - 1, 2, act_ranges, *t, norm_params),
                d_mid, keep, near, far, below["out_unit"], below["out_scale"],
            )
            g_begun = spread(down_grad)
        else:
            input_grad = run(lambda *t: end_back(act_ranges, *t, tokens), d_mid, keep, near, far)

    def small():
        peak_row = 6 * layers
        total = pack(rep_list, peaks)
        moved = swap(total, "tp", far_bit)
        flying["S0"] = [moved]
        yield
        total = merge(peak_row, total, moved)
        moved = swap(total, "tp", core_bit)
        flying["S0"] = [moved]
        yield
        total = merge(peak_row, total, moved, shard_list)
        for bit in (2, 4, 1):
            moved = swap(total, "dp", bit)
            flying["S0"] = [moved]
            yield
            total = merge(peak_row, total, moved)
        finished["small"] = total
        yield

    streams["S0"] = small()
    next(streams["S0"])
    go("end", 0)
    Line.free = True
    for item in streams.values():
        for _ in item:
            pass
    rep = finished["small"]
    sums = rep[: 6 * layers].reshape(layers, 6, width)
    peaks = rep[6 * layers].reshape(layers, 4, 128)[:, :, 0]
    up_sum = rep[6 * layers + 1 : 6 * layers + 1 + layers]
    qv_sum = rep[6 * layers + 1 + layers].reshape(layers, 2, local)
    return (
        output,
        input_grad,
        jnp.transpose(finished["attn"][0], (0, 2, 1, 3)),
        qv_sum,
        finished["attn"][1],
        sums[:, 0],
        finished["ffn"][1],
        up_sum,
        finished["ffn"][0],
        sums[:, 1],
        sums[:, 2:],
        peaks,
    )


def any_on_device(*args):
    tokens, lengths, qkv_weight, out_weight, up_weight = args[0], args[2], args[3], args[5], args[7]
    fits = (
        lax.axis_size("tp") == 4
        and lax.axis_size("dp") == 8
        and lengths.shape[0] == 1
        and tokens.shape[0] * 4 == SEQ_LEN
        and tokens.shape[1] == 1024
        and qkv_weight.shape[3] == 256
        and up_weight.shape[2] == 1024
    )
    return (fast_on_device if fits else on_device)(*args)


def solution(mesh):
    return jax.shard_map(
        any_on_device,
        mesh=mesh,
        in_specs=(
            P(("dp", "tp"), None),
            P(("dp", "tp"), None),
            P("dp"),
            P(None, None, None, "tp"),
            P(None, None, "tp"),
            P(None, "tp", None),
            P(),
            P(None, None, "tp"),
            P(None, "tp"),
            P(None, "tp", None),
            P(),
            P(),
            P(),
        ),
        out_specs=(
            P(("dp", "tp"), None),
            P(("dp", "tp"), None),
            P(None, None, None, "tp"),
            P(None, None, "tp"),
            P(None, "tp", None),
            P(),
            P(None, None, "tp"),
            P(None, "tp"),
            P(None, "tp", None),
            P(),
            P(),
            P(),
        ),
        check_vma=False,
    )
```

```python
import functools

import jax
import jax.numpy as jnp
from jax import lax
from jax.experimental import pallas as pl
from jax.experimental.pallas import tpu as pltpu
from jax.sharding import PartitionSpec as P

HD = 64
SEQ_LEN = 512
NORM_EPSILON = 1e-06
F32 = jnp.float32
BF16 = jnp.bfloat16


def bits_of(count):
    return [1 << place for place in range(count.bit_length() - 1)]


def swap(value, axis, bit):
    count = lax.axis_size(axis)
    return lax.ppermute(value, axis, [(item, item ^ bit) for item in range(count)])


def block_order(count):
    order = [0]
    for bit in reversed(bits_of(count)):
        order = order + [item ^ bit for item in order]
    return order


def gather_rows(rows):
    block = rows
    for bit in reversed(bits_of(lax.axis_size("tp"))):
        block = jnp.concatenate([block, swap(block, "tp", bit)], axis=0)
    return block


def scatter_rows(partial):
    for bit in bits_of(lax.axis_size("tp")):
        half = partial.shape[0] // 2
        arrived = swap(partial[half:].astype(BF16), "tp", bit)
        partial = partial[:half] + arrived.astype(F32)
    return partial


def squash(value, limit):
    return limit * jnp.tanh(value / limit)


def squash_slope(value, limit):
    level_value = jnp.tanh(value / limit)
    return 1.0 - level_value * level_value


def norm_parts(values):
    centre = jnp.mean(values, axis=-1, keepdims=True)
    centred = values - centre
    spread = jnp.mean(centred * centred, axis=-1, keepdims=True)
    scale = lax.rsqrt(spread + NORM_EPSILON)
    return centred * scale, scale


def norm_back(gradient, unit, scale, gain):
    scaled = gradient * gain
    first = jnp.mean(scaled, axis=-1, keepdims=True)
    second = jnp.mean(scaled * unit, axis=-1, keepdims=True)
    d_values = scale * (scaled - first - unit * second)
    return d_values, jnp.sum(gradient * unit, axis=0), jnp.sum(gradient, axis=0)


def mm(first, second):
    return jnp.dot(first, second, preferred_element_type=F32)


def mm_t(first, second):
    return lax.dot_general(first, second, (((1,), (1,)), ((), ())), preferred_element_type=F32)


def t_mm(first, second):
    return lax.dot_general(first, second, (((0,), (0,)), ((), ())), preferred_element_type=F32)


def reduce_weight(left, right, raw, top, order):
    place = lax.axis_index("dp")
    rows = left.shape[1]
    start = 0
    bit = order[0]
    mine = (place // bit) % 2
    half = rows // 2
    send = t_mm(lax.dynamic_slice_in_dim(left, (1 - mine) * half, half, 1), right).astype(BF16)
    arrived = swap(send, "dp", bit)
    total = t_mm(lax.dynamic_slice_in_dim(left, mine * half, half, 1), right)
    total = total + arrived.astype(F32)
    start = mine * half
    for bit in order[1:]:
        mine = (place // bit) % 2
        half = half // 2
        send = lax.dynamic_slice_in_dim(total, (1 - mine) * half, half, 0).astype(BF16)
        arrived = swap(send, "dp", bit)
        total = lax.dynamic_slice_in_dim(total, mine * half, half, 0) + arrived.astype(F32)
        start = start + mine * half
    raw_piece = lax.dynamic_slice_in_dim(raw, start, half, 0).astype(F32)
    piece = (total * squash_slope(raw_piece, top)).astype(BF16)
    for bit in reversed(order):
        mine = (place // bit) % 2
        arrived = swap(piece, "dp", bit)
        low_half = jnp.where(mine == 0, piece, arrived)
        high_half = jnp.where(mine == 0, arrived, piece)
        piece = jnp.concatenate([low_half, high_half], axis=0)
    return piece.astype(F32)


def on_device(
    tokens,
    cotangent,
    lengths,
    qkv_weight,
    qv_bias,
    out_weight,
    out_bias,
    up_weight,
    up_bias,
    down_weight,
    down_bias,
    norm_params,
    act_ranges,
):
    row_count, width = tokens.shape
    tp_count = lax.axis_size("tp")
    dp_count = lax.axis_size("dp")
    rank = lax.axis_index("tp")
    all_rows = row_count * tp_count
    assert lengths.shape[0] == 1 and all_rows == SEQ_LEN
    layer_count = qkv_weight.shape[0]
    local_width = qkv_weight.shape[3]
    local_units = up_weight.shape[2]
    heads_here = local_width // HD
    score_scale = HD ** (-0.5)
    order = jnp.array(block_order(tp_count), jnp.int32)
    places = ((rank ^ order)[:, None] * row_count + jnp.arange(row_count)[None, :]).reshape(all_rows)
    inside = places < lengths[0]
    valid_all = inside.astype(F32)[:, None]
    valid_rows = valid_all[:row_count]
    key_bias = jnp.where(inside, 0.0, -1000000000.0).astype(F32)
    qkv_blocks = jnp.transpose(qkv_weight, (0, 2, 1, 3))
    local_tops = jnp.stack(
        [
            jnp.stack(
                [
                    jnp.max(jnp.abs(qkv_blocks[level])),
                    jnp.max(jnp.abs(out_weight[level])),
                    jnp.max(jnp.abs(up_weight[level])),
                    jnp.max(jnp.abs(down_weight[level])),
                ]
            )
            for level in range(layer_count)
        ]
    ).astype(F32)
    weight_tops = local_tops
    for bit in bits_of(tp_count):
        weight_tops = jnp.maximum(weight_tops, swap(weight_tops, "tp", bit))

    def scores_of(queries, key_rows):
        raw = jnp.einsum("qhd,khd->hqk", queries, key_rows, preferred_element_type=F32)
        return raw * score_scale + key_bias[None, None, :]

    stored = []
    peak_list = []
    current = tokens.astype(F32)
    for level in range(layer_count):
        limits = act_ranges[level]
        tops = weight_tops[level]
        w_qkv = squash(qkv_blocks[level].astype(F32), tops[0]).astype(BF16)
        w_out = squash(out_weight[level].astype(F32), tops[1]).astype(BF16)
        w_up = squash(up_weight[level].astype(F32), tops[2]).astype(BF16)
        w_down = squash(down_weight[level].astype(F32), tops[3]).astype(BF16)
        x_low_all = gather_rows(squash(current, limits[0]).astype(BF16))
        heads = (all_rows, heads_here, HD)
        queries = (mm(x_low_all, w_qkv[0]) + qv_bias[level, 0].astype(F32)).astype(BF16).reshape(heads)
        key_rows = mm(x_low_all, w_qkv[1]).astype(BF16).reshape(heads)
        value_rows = (mm(x_low_all, w_qkv[2]) + qv_bias[level, 1].astype(F32)).astype(BF16).reshape(heads)
        scores = scores_of(queries, key_rows)
        peak_score = jnp.max(scores, axis=-1, keepdims=True)
        log_total = peak_score + jnp.log(jnp.sum(jnp.exp(scores - peak_score), axis=-1, keepdims=True))
        attn_probs = jnp.exp(scores - log_total).astype(BF16)
        context = jnp.einsum("hqk,khd->qhd", attn_probs, value_rows, preferred_element_type=F32)
        context = context.reshape(all_rows, local_width)
        ctx_low = squash(context, limits[1]).astype(BF16)
        attn_rows = scatter_rows(mm(ctx_low, w_out))
        mid_unit, mid_scale = norm_parts(current + attn_rows + out_bias[level].astype(F32))
        hidden = mid_unit * norm_params[level, 0] + norm_params[level, 1]
        hid_low_all = gather_rows(squash(hidden, limits[2]).astype(BF16))
        up_value = mm(hid_low_all, w_up) + up_bias[level].astype(F32)
        normal_cdf = 0.5 + 0.5 * lax.erf(up_value * (0.5**0.5))
        active = up_value * normal_cdf
        act_level = jnp.tanh(active / limits[3])
        act_low = (limits[3] * act_level).astype(BF16)
        gelu_slope = normal_cdf + up_value * jnp.exp(-0.5 * up_value * up_value) * 0.3989422804014327
        up_slope = (1.0 - act_level * act_level) * gelu_slope
        down_rows = scatter_rows(mm(act_low, w_down))
        out_unit, out_scale = norm_parts(hidden + down_rows + down_bias[level].astype(F32))
        peak_list.append(
            jnp.stack(
                [
                    jnp.max(jnp.abs(current) * valid_rows),
                    jnp.max(jnp.abs(context) * valid_all),
                    jnp.max(jnp.abs(hidden) * valid_rows),
                    jnp.max(jnp.abs(active) * valid_all),
                ]
            )
        )
        stored.append(
            (
                current, mid_unit, mid_scale, hidden, out_unit, out_scale, x_low_all, queries, key_rows, value_rows,
                log_total, context, ctx_low, hid_low_all, up_slope, act_low, w_qkv, w_out, w_up, w_down,
            )
        )
        current = out_unit * norm_params[level, 2] + norm_params[level, 3]
    output = current.astype(BF16)
    gradient = cotangent.astype(F32) * valid_rows

    dp_bits = bits_of(dp_count)
    big_list = [None] * layer_count
    rep_list = [None] * layer_count
    shard_list = [None] * layer_count
    for level in reversed(range(layer_count)):
        (
            inputs, mid_unit, mid_scale, hidden, out_unit, out_scale, x_low_all, queries, key_rows, value_rows,
            log_total, context, ctx_low, hid_low_all, up_slope, act_low, w_qkv, w_out, w_up, w_down,
        ) = stored[level]
        limits = act_ranges[level]
        tops = weight_tops[level]
        d_final, d_gain_out, d_shift_out = norm_back(gradient, out_unit, out_scale, norm_params[level, 2])
        down_grad = d_final.astype(BF16)
        d_down_bias = jnp.sum(down_grad.astype(F32), axis=0)
        down_grad_all = gather_rows(down_grad)
        up_grad = (mm_t(down_grad_all, w_down) * up_slope).astype(BF16)
        g_down = reduce_weight(act_low, down_grad_all, down_weight[level], tops[3], dp_bits)
        d_up_bias = jnp.sum(up_grad.astype(F32), axis=0)
        d_hid_rows = scatter_rows(mm_t(up_grad, w_up))
        g_up = reduce_weight(hid_low_all, up_grad, up_weight[level], tops[2], dp_bits)
        d_hidden = d_final + d_hid_rows * squash_slope(hidden, limits[2])
        d_mid, d_gain_mid, d_shift_mid = norm_back(d_hidden, mid_unit, mid_scale, norm_params[level, 0])
        out_grad = d_mid.astype(BF16)
        d_out_bias = jnp.sum(out_grad.astype(F32), axis=0)
        out_grad_all = gather_rows(out_grad)
        ctx_grad = (mm_t(out_grad_all, w_out) * squash_slope(context, limits[1])).astype(BF16)
        g_out = reduce_weight(ctx_low, out_grad_all, out_weight[level], tops[1], dp_bits)
        ctx_grad = ctx_grad.reshape(heads)
        soft_probs = jnp.exp(scores_of(queries, key_rows) - log_total)
        soft_low = soft_probs.astype(BF16)
        d_values = jnp.einsum("hqk,qhd->khd", soft_low, ctx_grad, preferred_element_type=F32)
        d_probs = jnp.einsum("qhd,khd->hqk", ctx_grad, value_rows, preferred_element_type=F32)
        d_scores = (
            soft_probs * (d_probs - jnp.sum(soft_probs * d_probs, axis=-1, keepdims=True))
        ).astype(BF16)
        d_queries = jnp.einsum("hqk,khd->qhd", d_scores, key_rows, preferred_element_type=F32) * score_scale
        d_keys = jnp.einsum("hqk,qhd->khd", d_scores, queries, preferred_element_type=F32) * score_scale
        parts = [
            item.astype(BF16).reshape(all_rows, local_width) for item in (d_queries, d_keys, d_values)
        ]
        d_x_rows = scatter_rows(
            mm_t(parts[0], w_qkv[0]) + mm_t(parts[1], w_qkv[1]) + mm_t(parts[2], w_qkv[2])
        )
        g_qkv = reduce_weight(
            x_low_all,
            jnp.concatenate(parts, axis=1),
            jnp.transpose(qkv_blocks[level], (1, 0, 2)).reshape(width, 3 * local_width),
            tops[0],
            dp_bits,
        ).reshape(width, 3, local_width)
        d_qv_bias = jnp.stack([jnp.sum(parts[0].astype(F32), axis=0), jnp.sum(parts[2].astype(F32), axis=0)])
        gradient = d_mid + d_x_rows * squash_slope(inputs, limits[0])
        big_list[level] = (g_qkv, g_out, g_up, g_down)
        rep_list[level] = jnp.stack([d_out_bias, d_down_bias, d_gain_mid, d_shift_mid, d_gain_out, d_shift_out])
        shard_list[level] = (d_qv_bias, d_up_bias)

    rep = jnp.stack(rep_list)
    peaks = jnp.stack(peak_list)
    for bit in bits_of(tp_count):
        rep = rep + swap(rep, "tp", bit)
        peaks = jnp.maximum(peaks, swap(peaks, "tp", bit))
    qv_sum = jnp.stack([item[0] for item in shard_list])
    up_sum = jnp.stack([item[1] for item in shard_list])
    sizes = [rep.size, qv_sum.size, up_sum.size]
    pack = jnp.concatenate([rep.reshape(-1), qv_sum.reshape(-1), up_sum.reshape(-1)])
    for bit in dp_bits:
        pack = pack + swap(pack, "dp", bit)
        peaks = jnp.maximum(peaks, swap(peaks, "dp", bit))
    rep = pack[: sizes[0]].reshape(rep.shape)
    qv_sum = pack[sizes[0] : sizes[0] + sizes[1]].reshape(qv_sum.shape)
    up_sum = pack[sizes[0] + sizes[1] :].reshape(up_sum.shape)
    grads = [jnp.stack([entry[item] for entry in big_list]) for item in range(4)]
    return (
        output,
        gradient,
        grads[0],
        qv_sum,
        grads[1],
        rep[:, 0],
        grads[2],
        up_sum,
        grads[3],
        rep[:, 1],
        rep[:, 2:],
        peaks,
    )


ERF_TOP = (
    -2.72614225801306e-10, 2.77068142495902e-08, -2.10102402082508e-06, -5.69250639462346e-05,
    -7.34990630326855e-04, -2.95459980854025e-03, -1.60960333262415e-02,
)
ERF_LOW = (
    -1.45660718464996e-05, -2.13374055278905e-04, -1.68282697438203e-03, -7.37332916720468e-03,
    -1.42647390514189e-02,
)


def erf_ratio(value):
    value = jnp.clip(value, -4.0, 4.0)
    square = value * value
    top = ERF_TOP[0]
    for factor in ERF_TOP[1:]:
        top = top * square + factor
    low = ERF_LOW[0]
    for factor in ERF_LOW[1:]:
        low = low * square + factor
    return value * top / low


def whole(shape):
    return pl.BlockSpec(shape, lambda *_: (0,) * len(shape))


SMEM = pl.BlockSpec(memory_space=pltpu.SMEM)


def cost(*_):
    return pl.CostEstimate(flops=1, bytes_accessed=1, transcendentals=0)


def params(mib=56):
    return pltpu.CompilerParams(vmem_limit_bytes=mib << 20)


def shaped(shape, dtype):
    return jax.ShapeDtypeStruct(shape, dtype)


class Line:
    mark = None
    free = False


def launch(
    kernel, *, out_shape, in_specs=(), out_specs=(), grid=None, grid_spec=None, scratch_shapes=(),
    input_output_aliases=None, compiler_params=None, cost_estimate=None, far_ins=(), far_outs=(),
):
    single = not isinstance(out_shape, (list, tuple))
    outs = [out_shape] if single else list(out_shape)
    if grid_spec is None:
        scalars, scratch = 0, list(scratch_shapes)
        ins_list, outs_list = list(in_specs), [out_specs] if single else list(out_specs)
    else:
        scalars, grid, scratch = grid_spec.num_scalar_prefetch, grid_spec.grid, list(grid_spec.scratch_shapes)
        ins_list, outs_list = list(grid_spec.in_specs), list(grid_spec.out_specs)

    def called(*args):
        marks = [] if Line.mark is None else [Line.mark]
        args = [
            pltpu.with_memory_space_constraint(item, pltpu.HBM) if place - scalars in far_ins else item
            for place, item in enumerate(args)
        ]
        first = scalars + len(ins_list)

        def body(*refs):
            refs = list(refs)
            del refs[first : first + len(marks)]
            del refs[first + len(outs)]
            kernel(*refs)

        anywhere = pl.BlockSpec(memory_space=pl.ANY)
        spec = pltpu.PrefetchScalarGridSpec(
            num_scalar_prefetch=scalars,
            grid=grid,
            in_specs=ins_list + [anywhere] * len(marks),
            out_specs=outs_list + [anywhere],
            scratch_shapes=scratch,
        )
        results = pl.pallas_call(
            body,
            out_shape=[
                pltpu.HBM(item.shape, item.dtype) if place in far_outs else item for place, item in enumerate(outs)
            ]
            + [shaped((8, 128), F32)],
            grid_spec=spec,
            input_output_aliases=input_output_aliases or {},
            compiler_params=compiler_params,
            cost_estimate=cost_estimate,
        )(*args, *marks)
        if not Line.free:
            Line.mark = results[-1]
        return results[0] if single else list(results[:-1])

    return called


def tops_kernel(count, *refs):
    weights, out_ref, scratch = refs[:count], refs[count], refs[count + 1 :]
    step = pl.program_id(0)
    for item in range(count):
        block = jnp.abs(weights[item][...])
        part = jnp.max(block.reshape(-1, 16, block.shape[-1]), axis=0)

        @pl.when(step == 0)
        def _():
            scratch[item][...] = part

        @pl.when(step > 0)
        def _():
            scratch[item][...] = jnp.maximum(scratch[item][...], part)

    @pl.when(step == pl.num_programs(0) - 1)
    def _():
        for item in range(count):
            top = jnp.max(scratch[item][...].astype(F32), axis=0, keepdims=True)
            top = jnp.max(top, axis=1, keepdims=True)
            out_ref[item : item + 1, :] = jnp.broadcast_to(top, (1, 128))


def row_specs(level, weights, steps, layered):
    specs = []
    for weight in weights:
        rows = weight.shape[-2] // steps
        if weight.ndim == 4 and layered:
            specs.append(pl.BlockSpec((1, weight.shape[1], rows, weight.shape[3]), lambda s: (level, 0, s, 0)))
        elif weight.ndim == 4:
            specs.append(pl.BlockSpec((weight.shape[1], rows, weight.shape[3]), lambda s: (0, s, 0)))
        elif layered:
            specs.append(pl.BlockSpec((1, rows, weight.shape[2]), lambda s: (level, s, 0)))
        else:
            specs.append(pl.BlockSpec((rows, weight.shape[2]), lambda s: (s, 0)))
    return specs


def weight_tops_of(level, weights):
    steps = 2
    return launch(
        functools.partial(tops_kernel, len(weights)),
        out_shape=shaped((len(weights), 128), F32),
        grid=(steps,),
        in_specs=row_specs(level, weights, steps, True),
        out_specs=whole((len(weights), 128)),
        scratch_shapes=[pltpu.VMEM((16, weight.shape[-1]), BF16) for weight in weights],
        compiler_params=params(24),
        cost_estimate=cost(),
        far_ins=range(len(weights)),
    )(*weights)


def top_of(tops, item):
    top = tops[0][item : item + 1, 0:1]
    for ref in tops[1:]:
        top = jnp.maximum(top, ref[item : item + 1, 0:1])
    return top


def squash_kernel(count, first, t0, t1, t2, t3, *refs):
    for item in range(count):
        top = top_of((t0, t1, t2, t3), first + item)
        value = refs[item][0].astype(F32)
        refs[count + item][...] = (top * jnp.tanh(value * (1.0 / top))).astype(BF16)


def squash_weights(level, tops, first, weights):
    steps = 2
    return launch(
        functools.partial(squash_kernel, len(weights), first),
        out_shape=[shaped(weight.shape[1:], BF16) for weight in weights],
        grid=(steps,),
        in_specs=[whole(tops[0].shape)] * 4 + row_specs(level, weights, steps, True),
        out_specs=row_specs(level, weights, steps, False),
        compiler_params=params(24),
        cost_estimate=cost(),
        far_ins=range(4, 8),
    )(*tops, *weights)


def slope_kernel(sets, rows_of, place_ref, *refs):
    tops, (qkv_ref, out_ref, up_ref, down_ref), targets = refs[: 4 * sets], refs[4 * sets : 4 * sets + 4], refs[-3:]

    def slope(value, item):
        group, row = rows_of[item]
        tanh = jnp.tanh(value.astype(F32) * (1.0 / top_of(tops[4 * group : 4 * group + 4], row)))
        return 1.0 - tanh * tanh

    targets[0][...] = slope(down_ref[0], 3)
    targets[1][...] = slope(up_ref[0], 2)
    local = qkv_ref.shape[3]
    for part in range(3):
        targets[2][:, part * local : (part + 1) * local] = slope(qkv_ref[0, part], 0)
    piece = slope(out_ref[0], 1)
    span = piece.shape[0]
    rows = targets[2].shape[0]
    side = piece.shape[1] * span // rows
    for item in range(rows // span):
        targets[2][item * span : (item + 1) * span, 3 * local :] = piece[:, item * side : (item + 1) * side]


def slope_pieces(level, place, tops, rows_of, weights):
    specs = []
    for weight in weights:
        rows = weight.shape[-2] // 8
        if weight.ndim == 4:
            specs.append(pl.BlockSpec((1, weight.shape[1], rows, weight.shape[3]), lambda s, p: (level, 0, p[0], 0)))
        else:
            specs.append(pl.BlockSpec((1, rows, weight.shape[2]), lambda s, p: (level, p[0], 0)))
    width = weights[2].shape[1]
    rows = width // 8
    outs = [shaped((rows, width), F32)] * 3
    return launch(
        functools.partial(slope_kernel, len(tops), rows_of),
        out_shape=outs,
        grid_spec=pltpu.PrefetchScalarGridSpec(
            num_scalar_prefetch=1,
            grid=(1,),
            in_specs=[whole(item.shape) for group in tops for item in group] + specs,
            out_specs=[whole(item.shape) for item in outs],
        ),
        compiler_params=params(12),
        cost_estimate=cost(0, 3 << 20, 1 << 19),
        far_ins=range(4 * len(tops), 4 * len(tops) + 4), far_outs=range(3),
    )(place, *[item for group in tops for item in group], *weights)


def valid_of(info_ref, rows, blocks):
    row = lax.broadcasted_iota(jnp.int32, (rows, 1), 0)
    columns = [(row + info_ref[block] < info_ref[4]).astype(F32) for block in blocks]
    return columns[0] if len(columns) == 1 else jnp.concatenate(columns, axis=0)


def key_bias_of(info_ref, rows):
    lane = lax.broadcasted_iota(jnp.int32, (1, rows), 1)
    return jnp.concatenate(
        [jnp.where(lane + info_ref[block] < info_ref[4], 0.0, -1000000000.0) for block in range(4)], axis=1
    )


def attn_forward_kernel(level, info_ref, limits_ref, x0, x1, x2, x3, w_ref, bias_ref, out_w_ref,
                        qkv_ref, ctx_ref, low_ref, peak_ref, send_ref, keep_ref, x_ref):
    rows = x0.shape[0]
    for place, piece in enumerate((x0, x1, x2, x3)):
        x_ref[place * rows : (place + 1) * rows, :] = piece[...]
    x = x_ref[...]
    for part in range(3):
        total = mm(x, w_ref[part])
        if part != 1:
            total = total + bias_ref[level, part // 2 : part // 2 + 1, :].astype(F32)
        qkv_ref[part] = total.astype(BF16)
    limit = limits_ref[level, 1]
    key_bias = key_bias_of(info_ref, rows)
    inverse = 1.0 / limit

    def heads(two, carry):
        lanes = pl.ds(pl.multiple_of(two * 2 * HD, 2 * HD), 2 * HD)
        queries, keys, values = qkv_ref[0, :, lanes], qkv_ref[1, :, lanes], qkv_ref[2, :, lanes]
        both = []
        for here in (slice(0, HD), slice(HD, 2 * HD)):
            scores = mm_t(queries[:, here], keys[:, here]) * (HD**-0.5) + key_bias
            scores = jnp.exp(scores - jnp.max(scores, axis=-1, keepdims=True))
            probs = (scores * (1.0 / jnp.sum(scores, axis=-1, keepdims=True))).astype(BF16)
            both.append(mm(probs, values[:, here]))
        ctx_ref[:, lanes] = jnp.concatenate(both, axis=1)
        return carry

    lax.fori_loop(0, qkv_ref.shape[2] // (2 * HD), heads, 0, unroll=True)
    context = ctx_ref[...]
    peak_ref[...] = jnp.max(jnp.abs(context) * valid_of(info_ref, rows, (0, 1, 2, 3)), axis=0, keepdims=True)
    low = (limit * jnp.tanh(context * inverse)).astype(BF16)
    low_ref[...] = low
    half = low.shape[0] // 2
    send_ref[...] = mm(low[half:], out_w_ref[...]).astype(BF16)
    keep_ref[...] = mm(low[:half], out_w_ref[...])


def attn_forward(level, info, limits, pieces, w_qkv, bias, w_out):
    rows, width = pieces[0].shape
    total = 4 * rows
    local = w_out.shape[0]
    ins = (info, limits, *pieces, w_qkv, bias, w_out)
    outs = [
        shaped((3, total, local), BF16),
        shaped((total, local), F32),
        shaped((total, local), BF16),
        shaped((1, local), F32),
        shaped((total // 2, width), BF16),
        shaped((total // 2, width), F32),
    ]
    return launch(
        functools.partial(attn_forward_kernel, level),
        out_shape=outs,
        in_specs=[SMEM, SMEM] + [whole(item.shape) for item in ins[2:]],
        out_specs=[whole(item.shape) for item in outs],
        scratch_shapes=[pltpu.VMEM((total, width), BF16)],
        grid=(1,),
        compiler_params=params(28),
        cost_estimate=cost(5e9, 8 << 20, 1 << 20),
        far_outs=(0, 1, 2),
    )(*ins)


def two_pieces(step, pieces, both_ref):
    rows = pieces[0].shape[0]
    for half in range(2):

        @pl.when(step == half)
        def _():
            both_ref[:rows] = pieces[2 * half][...]
            both_ref[rows:] = pieces[2 * half + 1][...]


def ffn_forward_kernel(level, info_ref, limits_ref, x0, x1, x2, x3, up_w_ref, bias_ref, down_w_ref,
                       low_ref, slope_ref, peak_ref, send_ref, keep_ref, both_ref, up_ref):
    step = pl.program_id(0)
    limit = limits_ref[level, 3]
    inverse = 1.0 / limit
    two_pieces(step, (x0, x1, x2, x3), both_ref)
    up_ref[...] = mm(both_ref[...], up_w_ref[...]) + bias_ref[level : level + 1, :].astype(F32)
    chunk = 64
    rows = x0.shape[0]

    def part(item, peak):
        here = pl.ds(pl.multiple_of(item * chunk, chunk), chunk)
        up = up_ref[here, :]
        cdf = 0.5 + 0.5 * erf_ratio(up * (0.5**0.5))
        active = up * cdf
        tanh = jnp.tanh(active * inverse)
        low_ref[here, :] = (limit * tanh).astype(BF16)
        slope_ref[here, :] = (1.0 - tanh * tanh) * (cdf + up * jnp.exp(-0.5 * up * up) * 0.3989422804014327)
        place = lax.broadcasted_iota(jnp.int32, (chunk, 1), 0) + item * chunk % rows
        inside = place + info_ref[2 * step + item * chunk // rows] < info_ref[4]
        size = jnp.where(inside, jnp.abs(active), 0.0)
        return jnp.maximum(peak, jnp.max(size.reshape(-1, 8, size.shape[1]), axis=0))

    peak = lax.fori_loop(0, 2 * rows // chunk, part, jnp.zeros((8, up_ref.shape[1]), F32))
    peak = jnp.max(peak, axis=0, keepdims=True)
    peak_ref[...] = jnp.where(step == 0, peak, jnp.maximum(peak_ref[...], peak))
    total = mm(low_ref[...], down_w_ref[...])

    @pl.when(step == 0)
    def _():
        keep_ref[...] = total

    @pl.when(step == 1)
    def _():
        send_ref[...] = total.astype(BF16)


def ffn_forward(level, info, limits, pieces, w_up, bias, w_down):
    rows, width = pieces[0].shape
    units = w_up.shape[1]
    total = 4 * rows
    outs = [
        shaped((total, units), BF16),
        shaped((total, units), F32),
        shaped((1, units), F32),
        shaped((total // 2, width), BF16),
        shaped((total // 2, width), F32),
    ]
    return launch(
        functools.partial(ffn_forward_kernel, level),
        out_shape=outs,
        grid=(2,),
        in_specs=[SMEM, SMEM]
        + [whole((rows, width))] * 4
        + [whole(w_up.shape), whole(bias.shape), whole(w_down.shape)],
        out_specs=[
            pl.BlockSpec((2 * rows, units), lambda s: (s, 0)),
            pl.BlockSpec((2 * rows, units), lambda s: (s, 0)),
            whole((1, units)),
            whole((2 * rows, width)),
            whole((2 * rows, width)),
        ],
        scratch_shapes=[pltpu.VMEM((2 * rows, width), BF16), pltpu.VMEM((2 * rows, units), F32)],
        compiler_params=params(32),
        cost_estimate=cost(8e9, 12 << 20, 2 << 20),
        far_outs=(0, 1),
    )(info, limits, *pieces, w_up, bias, w_down)


def enter_kernel(info_ref, limits_ref, tokens_ref, low_ref, peak_ref):
    value = tokens_ref[...].astype(F32)
    limit = limits_ref[0, 0]
    low_ref[...] = (limit * jnp.tanh(value * (1.0 / limit))).astype(BF16)
    peak_ref[...] = jnp.max(jnp.abs(value) * valid_of(info_ref, value.shape[0], (0,)), axis=0, keepdims=True)


def enter(info, limits, tokens):
    outs = [shaped(tokens.shape, BF16), shaped((1, tokens.shape[1]), F32)]
    return launch(
        enter_kernel,
        out_shape=outs,
        grid=(1,),
        in_specs=[SMEM, SMEM, whole(tokens.shape)],
        out_specs=[whole(item.shape) for item in outs],
        compiler_params=params(8),
        cost_estimate=cost(),
    )(info, limits, tokens)


def join_kernel(level, item, last, info_ref, limits_ref, base_ref, keep_ref, core_ref, far_ref, bias_ref, norm_ref,
                *outs):
    arrived = keep_ref[...] + core_ref[...].astype(F32) + far_ref[...].astype(F32)
    unit, scale = norm_parts(base_ref[...].astype(F32) + arrived + bias_ref[level : level + 1, :].astype(F32))
    value = unit * norm_ref[level, item : item + 1, :] + norm_ref[level, item + 1 : item + 2, :]
    outs[0][...] = unit
    outs[1][...] = scale
    if last:
        outs[2][...] = value.astype(BF16)
    else:
        outs[2][...] = value
        limit = limits_ref[level, 2] if item == 0 else limits_ref[level + 1, 0]
        outs[3][...] = (limit * jnp.tanh(value * (1.0 / limit))).astype(BF16)
        peak = jnp.abs(value) * valid_of(info_ref, value.shape[0], (0,))
        outs[4][...] = jnp.max(peak, axis=0, keepdims=True)


def join_rows(level, item, last, info, limits, base, keep, core, far, bias, norm):
    rows, width = base.shape
    outs = [shaped((rows, width), F32), shaped((rows, 1), F32)]
    if last:
        outs += [shaped((rows, width), BF16)]
    else:
        outs += [shaped((rows, width), F32), shaped((rows, width), BF16), shaped((1, width), F32)]
    block = whole((rows, width))
    return launch(
        functools.partial(join_kernel, level, item, last),
        out_shape=outs,
        grid=(1,),
        in_specs=[SMEM, SMEM, block, block, block, block, whole(bias.shape), whole(norm.shape)],
        out_specs=[whole(item.shape) for item in outs],
        compiler_params=params(12),
        cost_estimate=cost(),
        far_outs=(),
    )(info, limits, base, keep, core, far, bias, norm)


def norm_back_store(gradient, unit_ref, scale_ref, gain, d_ref, low_ref, sums_ref):
    unit = unit_ref[...]
    scaled = gradient * gain
    first = jnp.mean(scaled, axis=-1, keepdims=True)
    second = jnp.mean(scaled * unit, axis=-1, keepdims=True)
    d_values = scale_ref[...] * (scaled - first - unit * second)
    low = d_values.astype(BF16)
    d_ref[...] = d_values
    low_ref[...] = low
    sums_ref[0:1, :] = jnp.sum(low.astype(F32), axis=0, keepdims=True)
    sums_ref[1:2, :] = jnp.sum(gradient * unit, axis=0, keepdims=True)
    sums_ref[2:3, :] = jnp.sum(gradient, axis=0, keepdims=True)


def top_back_kernel(level, info_ref, cot_ref, unit_ref, scale_ref, norm_ref, d_ref, low_ref, sums_ref):
    gradient = cot_ref[...].astype(F32) * valid_of(info_ref, cot_ref.shape[0], (0,))
    norm_back_store(gradient, unit_ref, scale_ref, norm_ref[level, 2:3, :], d_ref, low_ref, sums_ref)


def mid_back_kernel(level, item, limits_ref, base_ref, keep_ref, core_ref, far_ref, unit_ref, scale_ref, norm_ref,
                    d_ref, low_ref, sums_ref):
    arrived = keep_ref[...] + core_ref[...].astype(F32) + far_ref[...].astype(F32)
    gain = norm_ref[level, item : item + 1, :]
    value = unit_ref[...] * gain + norm_ref[level, item + 1 : item + 2, :]
    limit = limits_ref[level, 2] if item == 0 else limits_ref[level + 1, 0]
    tanh = jnp.tanh(value * (1.0 / limit))
    gradient = base_ref[...] + arrived * (1.0 - tanh * tanh)
    norm_back_store(gradient, unit_ref, scale_ref, gain, d_ref, low_ref, sums_ref)


def end_back_kernel(limits_ref, base_ref, keep_ref, core_ref, far_ref, x_ref, out_ref):
    arrived = keep_ref[...] + core_ref[...].astype(F32) + far_ref[...].astype(F32)
    tanh = jnp.tanh(x_ref[...].astype(F32) * (1.0 / limits_ref[0, 0]))
    out_ref[...] = base_ref[...] + arrived * (1.0 - tanh * tanh)


def top_back(level, info, cotangent, unit, scale, norm):
    rows, width = unit.shape
    outs = [shaped((rows, width), F32), shaped((rows, width), BF16), shaped((3, width), F32)]
    ins = (cotangent, unit, scale, norm)
    return launch(
        functools.partial(top_back_kernel, level),
        out_shape=outs,
        grid=(1,),
        in_specs=[SMEM] + [whole(item.shape) for item in ins],
        out_specs=[whole(item.shape) for item in outs],
        compiler_params=params(12),
        cost_estimate=cost(),
        far_ins=(1, 2, 3),
    )(info, *ins)


def mid_back(level, item, limits, base, keep, core, far, unit, scale, norm):
    rows, width = unit.shape
    outs = [shaped((rows, width), F32), shaped((rows, width), BF16), shaped((3, width), F32)]
    block = whole((rows, width))
    return launch(
        functools.partial(mid_back_kernel, level, item),
        out_shape=outs,
        grid=(1,),
        in_specs=[SMEM, block, block, block, block, block, whole(scale.shape), whole(norm.shape)],
        out_specs=[whole(item.shape) for item in outs],
        compiler_params=params(12),
        cost_estimate=cost(),
        far_ins=(), far_outs=(),
    )(limits, base, keep, core, far, unit, scale, norm)


def end_back(limits, base, keep, core, far, x):
    block = whole(base.shape)
    return launch(
        end_back_kernel,
        out_shape=shaped(base.shape, F32),
        grid=(1,),
        in_specs=[SMEM] + [block] * 5,
        out_specs=block,
        compiler_params=params(12),
        cost_estimate=cost(),
    )(limits, base, keep, core, far, x)


def ffn_backward_kernel(g0, g1, g2, g3, down_w_ref, slope_ref, up_w_ref, grad_ref, sum_ref, send_ref, keep_ref,
                        both_ref):
    step = pl.program_id(0)
    two_pieces(step, (g0, g1, g2, g3), both_ref)
    grad = (mm_t(both_ref[...], down_w_ref[...]) * slope_ref[...]).astype(BF16)
    grad_ref[...] = grad
    part = jnp.sum(grad.astype(F32), axis=0, keepdims=True)
    sum_ref[...] = jnp.where(step == 0, part, sum_ref[...] + part)
    total = mm_t(grad, up_w_ref[...])

    @pl.when(step == 0)
    def _():
        keep_ref[...] = total

    @pl.when(step == 1)
    def _():
        send_ref[...] = total.astype(BF16)


def ffn_backward(pieces, w_down, slope, w_up):
    rows, width = pieces[0].shape
    units = w_up.shape[1]
    total = 4 * rows
    outs = [
        shaped((total, units), BF16),
        shaped((1, units), F32),
        shaped((total // 2, width), BF16),
        shaped((total // 2, width), F32),
    ]
    return launch(
        ffn_backward_kernel,
        out_shape=outs,
        grid=(2,),
        in_specs=[whole((rows, width))] * 4
        + [whole(w_down.shape), pl.BlockSpec((2 * rows, units), lambda s: (s, 0)), whole(w_up.shape)],
        out_specs=[
            pl.BlockSpec((2 * rows, units), lambda s: (s, 0)),
            whole((1, units)),
            whole((2 * rows, width)),
            whole((2 * rows, width)),
        ],
        scratch_shapes=[pltpu.VMEM((2 * rows, width), BF16)],
        compiler_params=params(32),
        cost_estimate=cost(3e9, 12 << 20),
        far_ins=(4, 5, 6),
    )(*pieces, w_down, slope, w_up)


def attn_backward_kernel(level, info_ref, limits_ref, g0, g1, g2, g3, out_w_ref, ctx_ref, qkv_ref, w_ref,
                         grad_ref, sum_ref, send_ref, keep_ref, g_ref, cg_ref):
    rows = g0.shape[0]
    for place, piece in enumerate((g0, g1, g2, g3)):
        g_ref[place * rows : (place + 1) * rows, :] = piece[...]
    tanh = jnp.tanh(ctx_ref[...] * (1.0 / limits_ref[level, 1]))
    cg_ref[...] = (mm_t(g_ref[...], out_w_ref[...]) * (1.0 - tanh * tanh)).astype(BF16)
    key_bias = key_bias_of(info_ref, rows)
    local = cg_ref.shape[1]

    def heads(two, carry):
        start = pl.multiple_of(two * 2 * HD, 2 * HD)
        lanes = pl.ds(start, 2 * HD)
        pairs = qkv_ref[0, :, lanes], qkv_ref[1, :, lanes], qkv_ref[2, :, lanes], cg_ref[:, lanes]
        parts = [[], [], []]
        for here in (slice(0, HD), slice(HD, 2 * HD)):
            queries, keys, values, grad = [item[:, here] for item in pairs]
            scores = mm_t(queries, keys) * (HD**-0.5) + key_bias
            scores = jnp.exp(scores - jnp.max(scores, axis=-1, keepdims=True))
            probs = scores * (1.0 / jnp.sum(scores, axis=-1, keepdims=True))
            d_values = t_mm(probs.astype(BF16), grad)
            d_probs = mm_t(grad, values)
            inner = jnp.sum(probs * d_probs, axis=-1, keepdims=True)
            d_scores = (probs * (d_probs - inner)).astype(BF16)
            parts[0].append(mm(d_scores, keys) * (HD**-0.5))
            parts[1].append(t_mm(d_scores, queries) * (HD**-0.5))
            parts[2].append(d_values)
        for part in range(3):
            target = pl.ds(pl.multiple_of(part * local + start, 2 * HD), 2 * HD)
            grad_ref[:, target] = jnp.concatenate(parts[part], axis=1).astype(BF16)
        return carry

    lax.fori_loop(0, local // (2 * HD), heads, 0, unroll=True)
    sum_ref[0:1, :] = jnp.sum(grad_ref[:, :local].astype(F32), axis=0, keepdims=True)
    sum_ref[1:2, :] = jnp.sum(grad_ref[:, 2 * local :].astype(F32), axis=0, keepdims=True)
    half = g_ref.shape[0] // 2

    def back(first, last):
        total = mm_t(grad_ref[first:last, :local], w_ref[0])
        total += mm_t(grad_ref[first:last, local : 2 * local], w_ref[1])
        return total + mm_t(grad_ref[first:last, 2 * local :], w_ref[2])

    send_ref[...] = back(half, 2 * half).astype(BF16)
    keep_ref[...] = back(0, half)


def attn_backward(level, info, limits, pieces, w_out, context, qkv, w_qkv):
    rows, width = pieces[0].shape
    total = 4 * rows
    local = w_out.shape[0]
    ins = (info, limits, *pieces, w_out, context, qkv, w_qkv)
    outs = [
        shaped((total, 3 * local), BF16),
        shaped((2, local), F32),
        shaped((total // 2, width), BF16),
        shaped((total // 2, width), F32),
    ]
    return launch(
        functools.partial(attn_backward_kernel, level),
        out_shape=outs,
        grid=(1,),
        in_specs=[SMEM, SMEM] + [whole(item.shape) for item in ins[2:]],
        out_specs=[whole(item.shape) for item in outs],
        scratch_shapes=[pltpu.VMEM((total, width), BF16), pltpu.VMEM((total, local), BF16)],
        compiler_params=params(32),
        cost_estimate=cost(6e9, 8 << 20, 1 << 20),
        far_ins=(6, 7, 8, 9),
    )(*ins)


LINK_ORDERS = ((1, 2, 4), (2, 1, 4))
FFN_ORDERS = (0, 1)
ATTN_WHOLE = ((0,), ((0, 1024),))
ATTN_CUT = ((0, 1), ((0, 512), (512, 1024)))


def block_masks(bits):
    return [
        (bits[0] if item & 4 else 0) ^ (bits[1] if item & 2 else 0) ^ (bits[2] if item & 1 else 0)
        for item in range(8)
    ]


def halves(target_pair, item):
    send_ref, keep_ref = target_pair
    return keep_ref if item < 4 else send_ref


def ffn_grad_kernel(table_ref, low_ref, g0, g1, g2, g3, h0, h1, h2, h3, grad_ref, *refs):
    targets, total_ref = refs[:4], refs[4]
    block = total_ref.shape[0] // 8
    for part, order in enumerate(FFN_ORDERS):
        if part == 0:
            total_ref[...] = t_mm(low_ref[...], jnp.concatenate([g0[...], g1[...], g2[...], g3[...]], axis=0))
        else:
            total_ref[...] = t_mm(jnp.concatenate([h0[...], h1[...], h2[...], h3[...]], axis=0), grad_ref[...])
        for item in range(8):
            first = pl.multiple_of(table_ref[order, item] * block, block)
            target = halves(targets[2 * part : 2 * part + 2], item)
            target[item % 4] = total_ref[pl.ds(first, block), :].astype(target.dtype)


def ffn_grad(table, act_low, g_pieces, h_pieces, up_grad):
    ins = [act_low, *g_pieces, *h_pieces, up_grad]
    width = up_grad.shape[1]
    outs = [shaped((4, width // 8, width), dtype) for _ in FFN_ORDERS for dtype in (BF16, F32)]
    return launch(
        ffn_grad_kernel,
        out_shape=outs,
        grid_spec=pltpu.PrefetchScalarGridSpec(
            num_scalar_prefetch=1,
            grid=(1,),
            in_specs=[whole(item.shape) for item in ins],
            out_specs=[whole(item.shape) for item in outs],
            scratch_shapes=[pltpu.VMEM((width, width), F32)],
        ),
        compiler_params=params(34),
        cost_estimate=cost(),
        far_ins=(0, 5, 6, 7, 8), far_outs=range(4),
    )(table, *ins)


def attn_grad_kernel(plan, table_ref, x0, x1, x2, x3, grad_ref, low_ref, g0, g1, g2, g3, *refs):
    targets, total_ref, out_ref = refs[:-2], refs[-2], refs[-1]
    total_ref[...] = t_mm(jnp.concatenate([x0[...], x1[...], x2[...], x3[...]], axis=0), grad_ref[...])
    out_ref[...] = t_mm(low_ref[...], jnp.concatenate([g0[...], g1[...], g2[...], g3[...]], axis=0))
    block = total_ref.shape[0] // 8
    local3 = total_ref.shape[1]
    span = out_ref.shape[0] // 8
    side = out_ref.shape[1] * span // block
    for part, (order, (start, stop)) in enumerate(zip(*plan)):
        for item in range(8):
            target = halves(targets[2 * part : 2 * part + 2], item)
            if start < local3:
                end = min(stop, local3)
                first = pl.multiple_of(table_ref[order, item] * block, block)
                value = total_ref[pl.ds(first, block), start:end]
                target[item % 4, :, : end - start] = value.astype(target.dtype)
            if stop > local3:
                first = pl.multiple_of(table_ref[order, item] * span, span)
                taken = out_ref[pl.ds(first, span), :]
                for place in range(block // span):
                    target[item % 4, place * span : (place + 1) * span, local3 - start :] = taken[
                        :, place * side : (place + 1) * side
                    ].astype(target.dtype)


def attn_grad(plan, table, x_pieces, qkv_grad, ctx_low, g_pieces):
    ins = [*x_pieces, qkv_grad, ctx_low, *g_pieces]
    width = x_pieces[0].shape[1]
    outs = [shaped((4, width // 8, last - first), dtype) for first, last in plan[1] for dtype in (BF16, F32)]
    return launch(
        functools.partial(attn_grad_kernel, plan),
        out_shape=outs,
        grid_spec=pltpu.PrefetchScalarGridSpec(
            num_scalar_prefetch=1,
            grid=(1,),
            in_specs=[whole(item.shape) for item in ins],
            out_specs=[whole(item.shape) for item in outs],
            scratch_shapes=[
                pltpu.VMEM((width, qkv_grad.shape[1]), F32),
                pltpu.VMEM((ctx_low.shape[1], width), F32),
            ],
        ),
        compiler_params=params(30),
        cost_estimate=cost(),
        far_ins=(0, 1, 2, 3, 5), far_outs=range(6),
    )(table, *ins)


def fold_kernel(count, parts, scaled, *refs):
    outs = refs[-parts:]
    for part in range(parts):
        mine = refs[part * count : (part + 1) * count]
        total = mine[0][...]
        for other in mine[1:]:
            total = total + other[...].astype(F32)
        if scaled:
            total = total * refs[parts * count + part][...]
        outs[part][...] = total.astype(BF16)


def fold(size, parts, scales=None):
    ins, in_specs, outs, out_specs = [], [], [], []
    count = len(parts[0])
    blocks = max(size, 1)
    for arrays in parts:
        rest = arrays[0].shape[1:]
        for array in arrays:
            ins.append(array)
            place = 1 if size else 0
            in_specs.append(pl.BlockSpec((blocks, *rest), lambda s, place=place: (place, 0, 0)))
        outs.append(shaped((blocks, *rest), BF16))
        out_specs.append(whole((blocks, *rest)))
    if scales is not None:
        for scale, columns in scales:
            width = columns[1] - columns[0]
            ins.append(scale)
            in_specs.append(pl.BlockSpec((scale.shape[0], width), lambda s, at=columns[0] // width: (0, at)))
    return launch(
        functools.partial(fold_kernel, count, len(parts), scales is not None),
        out_shape=outs,
        grid=(1,),
        in_specs=in_specs,
        out_specs=out_specs,
        compiler_params=params(16),
        cost_estimate=cost(),
        far_ins=range(len(ins)), far_outs=range(len(outs)),
    )(*ins)


def pair_kernel(parts, *refs):
    for part in range(parts):
        first, second, target = refs[2 * part], refs[2 * part + 1], refs[2 * parts + part]
        half = first.shape[0]
        target[:half] = first[...]
        target[half:] = second[...]


def pair(firsts, seconds):
    ins = [item for both in zip(firsts, seconds) for item in both]
    outs = [shaped((2 * item.shape[0], *item.shape[1:]), BF16) for item in firsts]
    return launch(
        functools.partial(pair_kernel, len(firsts)),
        out_shape=outs,
        grid=(1,),
        in_specs=[whole(item.shape) for item in ins],
        out_specs=[whole(item.shape) for item in outs],
        compiler_params=params(12),
        cost_estimate=cost(),
        far_ins=range(len(ins)), far_outs=range(len(outs)),
    )(*ins)


def place_kernel(plan, table_ref, *refs):
    outs = refs[-2:]
    step = pl.program_id(0)

    def store(part, source, item):
        start, stop = plan[1][part]
        if len(outs[0].shape) == 3:
            outs[part][0] = source[item].astype(F32)
            return
        qkv_ref, out_ref = outs
        local = qkv_ref.shape[3]
        for column in range(start, min(stop, 3 * local), 128):
            target = slice(column % local, column % local + 128)
            qkv_ref[0, column // local, :, target] = source[item, :, column - start : column - start + 128].astype(F32)
        if stop > 3 * local:
            span = out_ref.shape[1]
            side = stop - 3 * local
            for place in range(source.shape[1] // span):
                out_ref[0, :, place * side : (place + 1) * side] = source[
                    item, place * span : (place + 1) * span, 3 * local - start :
                ].astype(F32)

    for part, order in enumerate(plan[0]):
        item = table_ref[order, step]
        pl.when(item < 4)(functools.partial(store, part, refs[2 * part], item))
        pl.when(item >= 4)(functools.partial(store, part, refs[2 * part + 1], item - 4))


def place_blocks(plan, table, level, nears, fars, shapes, earlier):
    specs = []
    for shape in shapes:
        if len(shape) == 4:
            specs.append(pl.BlockSpec((1, shape[1], shape[2] // 8, shape[3]), lambda s, t: (level, 0, s, 0)))
        else:
            specs.append(pl.BlockSpec((1, shape[1] // 8, shape[2]), lambda s, t: (level, s, 0)))
    ins = [item for both in zip(nears, fars) for item in both]
    earlier = list(earlier or [])
    return launch(
        functools.partial(place_kernel, plan),
        out_shape=[shaped(shape, F32) for shape in shapes],
        grid_spec=pltpu.PrefetchScalarGridSpec(
            num_scalar_prefetch=1,
            grid=(8,),
            in_specs=[whole(item.shape) for item in ins] + [pl.BlockSpec(memory_space=pl.ANY)] * len(earlier),
            out_specs=specs,
        ),
        input_output_aliases={1 + len(ins) + place: place for place in range(len(earlier))},
        compiler_params=params(24),
        cost_estimate=cost(),
        far_ins=range(len(ins)), far_outs=range(len(shapes)),
    )(table, *ins, *earlier)


def near_sum_kernel(keep_ref, near_ref, out_ref):
    out_ref[...] = (keep_ref[...] + near_ref[...].astype(F32)).astype(BF16)


def near_sum(keep, near):
    rows, width = keep.shape[0] // 2, keep.shape[1]
    second = pl.BlockSpec((rows, width), lambda s: (1, 0))
    return launch(
        near_sum_kernel,
        out_shape=shaped((rows, width), BF16),
        grid=(1,),
        in_specs=[second, second],
        out_specs=whole((rows, width)),
        compiler_params=params(8),
        cost_estimate=cost(),
    )(keep, near)


def pack_kernel(layers, *refs):
    out_ref = refs[-1]
    row = 0
    for layer in range(layers):
        mid, out = refs[2 * layer], refs[2 * layer + 1]
        for source in (mid[0:1, :], out[0:1, :], mid[1:3, :], out[1:3, :]):
            out_ref[row : row + source.shape[0], :] = source
            row += source.shape[0]
    out_ref[row : row + 1, :] = refs[-2][...]


def pack(sums, peaks):
    ins = [item for both in sums for item in both] + [peaks]
    out = shaped((6 * len(sums) + 1, peaks.shape[1]), F32)
    return launch(
        functools.partial(pack_kernel, len(sums)),
        out_shape=out,
        grid=(1,),
        in_specs=[whole(item.shape) for item in ins],
        out_specs=whole(out.shape),
        compiler_params=params(8),
        cost_estimate=cost(),
    )(*ins)


def merge_kernel(peak_row, more, mine_ref, other_ref, *refs):
    out_ref = refs[-1]
    mine, other = mine_ref[...], other_ref[...]
    row = lax.broadcasted_iota(jnp.int32, mine.shape, 0)
    merged = jnp.where(row == peak_row, jnp.maximum(mine, other), mine + other)
    if not more:
        out_ref[...] = merged
        return
    count = mine.shape[0]
    out_ref[:count, :] = merged
    for item in range(more):
        up_ref, qv_ref = refs[2 * item], refs[2 * item + 1]
        out_ref[count + item : count + item + 1, :] = up_ref[...]
        local = qv_ref.shape[1]
        for part in range(2):
            start = (2 * item + part) * local
            out_ref[count + more : count + more + 1, start : start + local] = qv_ref[part : part + 1, :]


def merge(peak_row, mine, other, shards=()):
    ins = [mine, other] + [item for both in shards for item in both]
    rows = mine.shape[0] + (len(shards) + 1 if shards else 0)
    return launch(
        functools.partial(merge_kernel, peak_row, len(shards)),
        out_shape=shaped((rows, mine.shape[1]), F32),
        grid=(1,),
        in_specs=[whole(item.shape) for item in ins],
        out_specs=whole((rows, mine.shape[1])),
        compiler_params=params(8),
        cost_estimate=cost(),
    )(*ins)


def peaks_kernel(*refs):
    out_ref = refs[-1]
    for item, ref in enumerate(refs[:-1]):
        top = jnp.max(ref[...], axis=1, keepdims=True)
        out_ref[0:1, item * 128 : (item + 1) * 128] = jnp.broadcast_to(top, (1, 128))


def peaks_row(rows):
    return launch(
        peaks_kernel,
        out_shape=shaped((1, 128 * len(rows)), F32),
        grid=(1,),
        in_specs=[whole(item.shape) for item in rows],
        out_specs=whole((1, 128 * len(rows))),
        compiler_params=params(8),
        cost_estimate=cost(0, 1 << 16),
    )(*rows)


STEPS = {
    "M41": ("F1",),
    "M20": ("F1",),
    "M31": (),
    "M30": (),
    "WT0": (),
    "end0": (),
}


def fast_on_device(
    tokens,
    cotangent,
    lengths,
    qkv_weight,
    qv_bias,
    out_weight,
    out_bias,
    up_weight,
    up_bias,
    down_weight,
    down_bias,
    norm_params,
    act_ranges,
):
    row_count, width = tokens.shape
    tp_count = lax.axis_size("tp")
    rank = lax.axis_index("tp")
    place = lax.axis_index("dp")
    layers = qkv_weight.shape[0]
    local = qkv_weight.shape[3]
    order = jnp.array(block_order(tp_count), jnp.int32)
    info = jnp.concatenate([(rank ^ order) * row_count, lengths])
    qkv_blocks = jnp.transpose(qkv_weight, (0, 2, 1, 3))
    weights = (qkv_blocks, out_weight, up_weight, down_weight)
    core_bit, far_bit = bits_of(tp_count)
    place_list = place[None].astype(jnp.int32)
    Line.mark = None
    Line.free = False

    def run(step, *values):
        return step(*values)

    def spread(rows):
        return rows, swap(rows, "tp", far_bit), swap(rows, "tp", core_bit)

    def finish(begun):
        rows, far, near = begun
        far, _ = lax.optimization_barrier((far, Line.mark))
        return (rows, far, near, swap(far, "tp", core_bit))

    def gather_sum(send, keep):
        near = swap(send, "tp", core_bit)
        return near, swap(near_sum(keep, near), "tp", far_bit)

    x_low, x_peak = run(enter, info, act_ranges, tokens)
    x_begun = spread(x_low)
    low_weights = [dict() for _ in range(layers)]
    names = ("qkv", "out", "up", "down")
    sets = {}

    def find_tops(level, first, last):
        mine = weight_tops_of(level, weights[first:last])
        others = [swap(mine, "tp", bit) for bit in (core_bit, far_bit, core_bit | far_bit)]
        sets[level, first] = (mine, *others)

    def squash_some(level, origin, first, last):
        outs = squash_weights(level, sets[level, origin], first - origin, weights[first:last])
        for name, out in zip(names[first:last], outs):
            low_weights[level][name] = out

    find_tops(0, 0, 2)
    find_tops(0, 2, 4)
    squash_some(0, 0, 0, 2)
    slopes = [None] * layers
    kept = []
    peak_rows = []
    current = tokens
    for level in range(layers):
        low = low_weights[level]
        last = level == layers - 1
        x_pieces = finish(x_begun)
        qkv, context, ctx_low, ctx_peak, send, keep = run(
            lambda pieces, w_qkv, w_out: attn_forward(level, info, act_ranges, pieces, w_qkv, qv_bias, w_out),
            x_pieces, low["qkv"], low["out"],
        )
        near, far = gather_sum(send, keep)
        if level == 0:
            squash_some(0, 2, 2, 4)
        else:
            squash_some(1, 0, 2, 4)
        mid_unit, mid_scale, hidden, hid_low, hid_peak = run(
            lambda *t: join_rows(level, 0, False, info, act_ranges, *t, out_bias, norm_params),
            current, keep, near, far,
        )
        h_begun = spread(hid_low)
        if level == 0:
            find_tops(1, 0, 4)
        h_pieces = finish(h_begun)
        act_low, slope, act_peak, send, keep = run(
            lambda pieces, w_up, w_down: ffn_forward(level, info, act_ranges, pieces, w_up, up_bias, w_down),
            h_pieces, low["up"], low["down"],
        )
        near, far = gather_sum(send, keep)
        if level == 0:
            squash_some(1, 0, 0, 2)
        else:
            slopes[1] = slope_pieces(1, place_list, [sets[1, 0]], ((0, 0), (0, 1), (0, 2), (0, 3)), weights)
            slopes[0] = slope_pieces(
                0, place_list, [sets[0, 0], sets[0, 2]], ((0, 0), (0, 1), (1, 0), (1, 1)), weights
            )
            peak_rows.append([x_peak, ctx_peak, hid_peak, act_peak])
            peaks = run(lambda *t: peaks_row(t), *peak_rows[0], *peak_rows[1])
        result = run(
            lambda *t: join_rows(level, 2, last, info, act_ranges, *t, down_bias, norm_params),
            hidden, keep, near, far,
        )
        peak_rows.append([x_peak, ctx_peak, hid_peak, act_peak])
        kept.append(
            dict(
                x=x_pieces, qkv=qkv, context=context, ctx_low=ctx_low, mid_unit=mid_unit, mid_scale=mid_scale,
                h=h_pieces, act_low=act_low, slope=slope, out_unit=result[0], out_scale=result[1], **{
                    "w_" + name: value for name, value in low.items()
                },
            )
        )
        if last:
            output = result[2]
        else:
            current, x_low, x_peak = result[2:]
            x_begun = spread(x_low)

    masks = [block_masks(bits) for bits in LINK_ORDERS]
    table = place ^ jnp.array(masks, jnp.int32)
    inverse = jnp.array([[row.index(item) for item in range(8)] for row in masks], jnp.int32)
    inverse = jnp.take(inverse, place ^ jnp.arange(8), axis=1)
    finished = {"ffn": None, "attn": None}
    shapes = {"ffn": [down_weight.shape, up_weight.shape], "attn": [qkv_blocks.shape, out_weight.shape]}

    full = (0, width)
    plans = {
        "ffn1": (FFN_ORDERS, (full, full)), "ffn0": (FFN_ORDERS, (full, full)), "attn1": ATTN_WHOLE, "attn0": ATTN_CUT,
    }

    def stream(level, name, outs):
        plan = plans[name + str(level)]

        key = {"ffn": "F", "attn": "T"}[name] + str(level)

        def swap_parts(parts, step):
            flying[key] = [swap(item, "dp", LINK_ORDERS[order][step]) for item, order in zip(parts, plan[0])]
            return flying[key]

        moved = [list(outs[1::2]), swap_parts(outs[0::2], 0)]
        yield
        moved.append(swap_parts(fold(2, list(zip(*moved))), 1))
        yield
        moved.append(swap_parts(fold(1, list(zip(*moved))), 2))
        yield
        scales = slopes[level][:2] if name == "ffn" else [slopes[level][2]] * len(plan[0])
        pieces = fold(0, list(zip(*moved)), list(zip(scales, plan[1])))
        for step in (2, 1):
            others = swap_parts(pieces, step)
            yield
            pieces = pair(pieces, others)
        others = swap_parts(pieces, 0)
        yield
        finished[name] = place_blocks(plan, inverse, level, pieces, others, shapes[name], finished[name])
        yield

    streams, flying = {}, {}

    def begin(level, name, outs):
        streams[{"ffn": "F", "attn": "T"}[name] + str(level)] = stream(level, name, outs)
        next(streams[{"ffn": "F", "attn": "T"}[name] + str(level)])

    def go(point, level):
        for item in STEPS.get(point + str(level), ()):
            next(streams[item])

    def back_norm(level, base, keep, near, far):
        return run(
            lambda *t: mid_back(level, 0, act_ranges, *t, norm_params),
            base, keep, near, far, kept[level]["mid_unit"], kept[level]["mid_scale"],
        )

    rep_list = [None] * layers
    shard_list = [None] * layers
    top = layers - 1
    d_final, down_grad, sums_out = run(
        lambda *t: top_back(top, info, cotangent, *t, norm_params),
        kept[top]["out_unit"], kept[top]["out_scale"],
    )
    g_begun = spread(down_grad)
    for level in reversed(range(layers)):
        saved = kept[level]
        go("M4", level + 1)
        g_pieces = finish(g_begun)
        up_grad, up_sum, send, keep = run(
            ffn_backward, g_pieces, saved["w_down"], saved["slope"], saved["w_up"]
        )
        near, far = gather_sum(send, keep)
        begin(
            level, "ffn", run(lambda *t: ffn_grad(table, *t), saved["act_low"], g_pieces, saved["h"], up_grad)
        )
        go("WF", level)
        d_mid, out_grad, sums_mid = back_norm(level, d_final, keep, near, far)
        o_begun = spread(out_grad)
        go("M2", level)
        o_pieces = finish(o_begun)
        qkv_grad, qv_sum, send, keep = run(
            lambda *t: attn_backward(level, info, act_ranges, *t),
            o_pieces, saved["w_out"], saved["context"], saved["qkv"], saved["w_qkv"],
        )
        near, far = gather_sum(send, keep)
        begin(
            level, "attn",
            run(lambda *t: attn_grad(plans["attn" + str(level)], table, *t), saved["x"], qkv_grad, saved["ctx_low"], o_pieces),
        )
        go("WT", level)
        rep_list[level] = (sums_mid, sums_out)
        shard_list[level] = (up_sum, qv_sum)
        if level > 0:
            below = kept[level - 1]
            d_final, down_grad, sums_out = run(
                lambda *t: mid_back(level - 1, 2, act_ranges, *t, norm_params),
                d_mid, keep, near, far, below["out_unit"], below["out_scale"],
            )
            g_begun = spread(down_grad)
        else:
            input_grad = run(lambda *t: end_back(act_ranges, *t, tokens), d_mid, keep, near, far)

    def small():
        peak_row = 6 * layers
        total = pack(rep_list, peaks)
        moved = swap(total, "tp", far_bit)
        flying["S0"] = [moved]
        yield
        total = merge(peak_row, total, moved)
        moved = swap(total, "tp", core_bit)
        flying["S0"] = [moved]
        yield
        total = merge(peak_row, total, moved, shard_list)
        for bit in (2, 4, 1):
            moved = swap(total, "dp", bit)
            flying["S0"] = [moved]
            yield
            total = merge(peak_row, total, moved)
        finished["small"] = total
        yield

    streams["S0"] = small()
    next(streams["S0"])
    go("end", 0)
    Line.free = True
    for item in streams.values():
        for _ in item:
            pass
    rep = finished["small"]
    sums = rep[: 6 * layers].reshape(layers, 6, width)
    peaks = rep[6 * layers].reshape(layers, 4, 128)[:, :, 0]
    up_sum = rep[6 * layers + 1 : 6 * layers + 1 + layers]
    qv_sum = rep[6 * layers + 1 + layers].reshape(layers, 2, local)
    return (
        output,
        input_grad,
        jnp.transpose(finished["attn"][0], (0, 2, 1, 3)),
        qv_sum,
        finished["attn"][1],
        sums[:, 0],
        finished["ffn"][1],
        up_sum,
        finished["ffn"][0],
        sums[:, 1],
        sums[:, 2:],
        peaks,
    )


def any_on_device(*args):
    tokens, lengths, qkv_weight, out_weight, up_weight = args[0], args[2], args[3], args[5], args[7]
    fits = (
        lax.axis_size("tp") == 4
        and lax.axis_size("dp") == 8
        and lengths.shape[0] == 1
        and tokens.shape[0] * 4 == SEQ_LEN
        and tokens.shape[1] == 1024
        and qkv_weight.shape[3] == 256
        and up_weight.shape[2] == 1024
    )
    return (fast_on_device if fits else on_device)(*args)


def solution(mesh):
    return jax.shard_map(
        any_on_device,
        mesh=mesh,
        in_specs=(
            P(("dp", "tp"), None),
            P(("dp", "tp"), None),
            P("dp"),
            P(None, None, None, "tp"),
            P(None, None, "tp"),
            P(None, "tp", None),
            P(),
            P(None, None, "tp"),
            P(None, "tp"),
            P(None, "tp", None),
            P(),
            P(),
            P(),
        ),
        out_specs=(
            P(("dp", "tp"), None),
            P(("dp", "tp"), None),
            P(None, None, None, "tp"),
            P(None, None, "tp"),
            P(None, "tp", None),
            P(),
            P(None, None, "tp"),
            P(None, "tp"),
            P(None, "tp", None),
            P(),
            P(),
            P(),
        ),
        check_vma=False,
    )
```
